128 devices in a mesh: row: 8 (over x, core), col: 16 (over z, y).
Axes of the slice: x: 4, y: 4, z: 4, core: 2. Of those that a mesh axis runs over, the one named last changes fastest.
Arguments:
- tile_feats: bfloat16 [128, 128, 32, 192], P(('row', 'col')), may hold values from -6 to 6
- tile_cell: int32 [128, 128, 32], P(('row', 'col')), may hold values from 0 to 4095, as said below
- tile_mask: int32 [128, 128, 32], P(('row', 'col')), may hold values 0 or 1
- tile_count: int32 [128, 128], P(('row', 'col')), may hold values from 0 to 32, as said below
- background: bfloat16 [192], replicated, may hold values from -6 to 6
- norm_gain: float32 [192], replicated, may hold values from 0.1 to 1.9
- in_x: bfloat16 [192, 384], replicated, may hold values from -0.4375 to 0.4375
- in_z: bfloat16 [192, 384], replicated, may hold values from -0.4375 to 0.4375
- conv_w: float32 [3, 3, 384], replicated, may hold values from -2 to 2
- conv_bias: float32 [384], replicated, may hold values from -3 to 3
- x_proj: bfloat16 [384, 128], replicated, may hold values from -0.15625 to 0.15625
- skip_gain: float32 [384], replicated, may hold values from 0.5 to 1.5
- decay_rate: float32 [4, 6, 256, 2048], P(None, None, 'row', 'col'), may hold values from 0 to 1
- out_gain: float32 [384], replicated, may hold values from 0.1 to 1.9
- out_w: bfloat16 [384, 192], replicated, may hold values from -0.3125 to 0.3125
- mlp_gain: float32 [192], replicated, may hold values from 0.1 to 1.9
- ff_in: bfloat16 [192, 768], replicated, may hold values from -0.4375 to 0.4375
- ff_out: bfloat16 [768, 192], replicated, may hold values from -0.21875 to 0.21875
Outputs:
- block_out: bfloat16 [256, 2048, 192], P('row', 'col')
The draws below stay inside these ranges and needn't reach their ends.
Inputs may be any that keep to these rules, and one draw needn't show every extreme that they name: `tile_cell`: cells of the owner's block of 32 x 128 cells, numbered row by row; the live slots sent to one owner by all loaders name distinct cells. `tile_count`: the live slots from a loader to an owner are its first ones; some owner receives 32 from every loader.
All inputs are finite; a program needn't handle non-finite values. No bound on the sum of `tile_mask` on one device may be relied on, other than what follows from the above.
Results may differ from the reference program's by a relative error of at most 0.015.
Values may be sent and summed in bfloat16 or wider, within the bound.
No kernel may reach another device: no remote copies, remote signals or barrier semaphores. Data moves between devices by JAX's collectives and lax.ppermute only.
A program may use at most 384 MiB of HBM per device.

```python
import math
import jax
import jax.numpy as jnp
from jax import lax

C = 192
DI = 384
STATE = 16
FF = 768
DIRS = 4
RH = 32
RW = 128
HEADS = 6
GRID_H = 256
GRID_W = 2048
CAP = 32
DEVICES = 128


def routing_parts(key):
    key_ceiling, key_count, key_full, key_order, key_filler = jax.random.split(jax.random.fold_in(key, 7), 5)
    ceiling = jax.random.randint(key_ceiling, (1, DEVICES), CAP // 2, CAP + 1)
    ceiling = jnp.broadcast_to(ceiling, (DEVICES, DEVICES))
    counts = jax.random.randint(key_count, (DEVICES, DEVICES), ceiling // 2, ceiling + 1)
    full_owner = jax.random.randint(key_full, (), 0, DEVICES)
    counts = jnp.where(jnp.arange(DEVICES)[None, :] == full_owner, CAP, counts)
    cells = RH * RW
    orders = jax.vmap(lambda subkey: jax.random.permutation(subkey, cells))(jax.random.split(key_order, DEVICES))
    offsets = jnp.cumsum(counts, axis=0) - counts
    slot_index = jnp.arange(CAP)
    position = jnp.minimum(offsets[:, :, None] + slot_index[None, None, :], cells - 1)
    picked = orders[jnp.arange(DEVICES)[None, :, None], position]
    filler = jax.random.randint(key_filler, (DEVICES, DEVICES, CAP), 0, cells)
    cell_ids = jnp.where(slot_index[None, None, :] < counts[:, :, None], picked, filler)
    return (counts.astype(jnp.int32), cell_ids.astype(jnp.int32))


def draw_tile_cell(key, part):
    return routing_parts(key)[1]


def draw_tile_count(key, part):
    return routing_parts(key)[0]


def draw_decay_rate(key, part):
    keys = jax.random.split(jax.random.fold_in(key, 11), 7)
    fast_share = 0.5
    fast = jax.random.uniform(keys[0], (DIRS, HEADS, 1, 1)) < fast_share
    chain = jnp.array([GRID_W, GRID_W, GRID_H, GRID_H], jnp.float32).reshape(DIRS, 1, 1, 1)
    fast_rate = jnp.exp(jax.random.uniform(keys[1], (DIRS, HEADS, 1, 1), minval=math.log(1.0 / 50.0), maxval=math.log(1.0 / 30.0)))
    slow_rate = jnp.exp(jax.random.uniform(keys[2], (DIRS, HEADS, 1, 1), minval=math.log(0.05), maxval=math.log(0.25))) / chain
    base = jnp.where(fast, fast_rate, slow_rate)
    factor = 2.0 ** jax.random.uniform(keys[3], (DIRS, HEADS, GRID_H // RH, GRID_W // RW), minval=-1.0, maxval=1.0)
    factor = jnp.repeat(jnp.repeat(factor, RH, axis=2), RW, axis=3)
    rough = jnp.clip(1.0 + 0.25 * jax.random.normal(keys[4], (DIRS, HEADS, GRID_H, GRID_W)), 0.5, 1.5)
    hit = jax.random.uniform(keys[5], (DIRS, HEADS, GRID_H, GRID_W)) < 2.0 / chain
    loss = jax.random.uniform(keys[6], (DIRS, HEADS, GRID_H, GRID_W), minval=0.22, maxval=0.69)
    rate = base * factor * rough + jnp.where(hit, loss, 0.0)
    return rate.astype(jnp.float32)


def set_ends(entries, own_key, smallest, high):
    longest = entries.shape.index(max(entries.shape))
    spots = []
    for shift in (0, 1):
        where = [jax.random.randint(jax.random.fold_in(own_key, axis), (), 0, length) for axis, length in enumerate(entries.shape)]
        where[longest] = (where[longest] + shift) % entries.shape[longest]
        spots.append(tuple(where))
    return entries.at[spots[0]].set(smallest).at[spots[1]].set(high)


def block_scale(stream_key, dims, cuts, least, top_value):
    def one(dim, parts):
        draws = jax.random.uniform(jax.random.fold_in(jax.random.fold_in(stream_key, 6), dim), (parts,), jnp.float32, least / len(cuts), top_value / len(cuts))
        return jnp.repeat(jnp.exp(draws), dims[dim] // parts).reshape((-1,) + (1,) * (len(dims) - dim - 1))

    factor_of = one(*cuts[0])
    for cut in cuts[1:]:
        factor_of = factor_of * one(*cut)
    return factor_of


def gaussian(stream_key, shape, scale, most, shards=(), held_as=jnp.bfloat16):
    values = jax.random.normal(stream_key, shape, jnp.float32) * scale
    if len(shards) > 0:
        values = block_scale(stream_key, shape, shards, -0.22, 0.18) * values
    return jnp.clip(values, min=-most, max=most).astype(held_as)


def setup_inputs(seed: int = 0) -> dict:
    key_of = jax.random.split(jax.random.key(seed), 19)
    tile_feats = gaussian(key_of[0], (DEVICES, DEVICES, CAP, C), 1.0, 6.0, ((0, 128),))
    tile_cell = draw_tile_cell(jax.random.fold_in(key_of[18], 71), 0)
    tile_mask = set_ends((jax.random.randint(key_of[2], (DEVICES, DEVICES, CAP), 0, 4) < 3).astype(jnp.int32), jax.random.fold_in(key_of[2], 1), 0, 1)
    tile_count = draw_tile_count(jax.random.fold_in(key_of[18], 71), 0)
    background = gaussian(key_of[4], (C,), 1.0, 6.0)
    norm_gain = jnp.clip(1.0 + 0.18 * jax.random.normal(key_of[5], (C,), jnp.float32), 0.1, 1.9)
    in_x = gaussian(key_of[6], (C, DI), C ** -0.5, 0.4375)
    in_z = gaussian(key_of[7], (C, DI), C ** -0.5, 0.4375)
    conv_w = gaussian(key_of[8], (3, 3, DI), 9 ** -0.5, 2.0, (), jnp.float32)
    conv_bias = gaussian(key_of[9], (DI,), 0.5, 3.0, (), jnp.float32)
    x_proj = gaussian(key_of[10], (DI, 2 * DIRS * STATE), (4 * DI) ** -0.5, 0.15625)
    skip_gain = jnp.clip(jax.random.uniform(key_of[11], (DI,), jnp.float32, 0.5, 1.5), 0.5, 1.5)
    decay_rate = draw_decay_rate(jax.random.fold_in(key_of[18], 71), 0)
    out_gain = jnp.clip(1.0 + 0.18 * jax.random.normal(key_of[13], (DI,), jnp.float32), 0.1, 1.9)
    out_w = gaussian(key_of[14], (DI, C), DI ** -0.5, 0.3125)
    mlp_gain = jnp.clip(1.0 + 0.18 * jax.random.normal(key_of[15], (C,), jnp.float32), 0.1, 1.9)
    ff_in = gaussian(key_of[16], (C, FF), C ** -0.5, 0.4375)
    ff_out = gaussian(key_of[17], (FF, C), FF ** -0.5, 0.21875)
    return dict(tile_feats=tile_feats, tile_cell=tile_cell, tile_mask=tile_mask, tile_count=tile_count, background=background, norm_gain=norm_gain, in_x=in_x, in_z=in_z, conv_w=conv_w, conv_bias=conv_bias, x_proj=x_proj, skip_gain=skip_gain, decay_rate=decay_rate, out_gain=out_gain, out_w=out_w, mlp_gain=mlp_gain, ff_in=ff_in, ff_out=ff_out)


def rms_scale(values, gains):
    return values * lax.rsqrt(lax.optimization_barrier(jnp.mean(values * values, axis=-1, keepdims=True)) + 1e-06) * gains

def block_parts(x_vals, b_coef, c_coef, rates):
    cumulative = jnp.cumsum(rates, axis=2)
    weight = jnp.sqrt(-jnp.expm1(-2.0 * rates))
    scaled = x_vals.astype(jnp.float32) * jnp.swapaxes(weight, 1, 2)[..., None]
    scores = jnp.einsum('stn,sun->stu', c_coef.astype(jnp.float32), b_coef.astype(jnp.float32))
    length = rates.shape[2]
    causal = lax.broadcasted_iota(jnp.int32, (length, length), 0) >= lax.broadcasted_iota(jnp.int32, (length, length), 1)
    log_gap = cumulative[:, :, :, None] - cumulative[:, :, None, :]
    mixing = jnp.where(causal, jnp.exp(-jnp.maximum(log_gap, 0.0)), 0.0) * scores[:, None]
    inner_part = jnp.einsum('shtu,suhp->sthp', mixing, scaled, precision=lax.Precision.HIGHEST)
    to_end = jnp.exp(cumulative - cumulative[:, :, -1:])
    weighted = scaled * jnp.swapaxes(to_end, 1, 2)[..., None]
    final_state = jnp.einsum('suhp,sun->shpn', weighted, b_coef.astype(jnp.float32), precision=lax.Precision.HIGHEST)
    total_decay = jnp.exp(-cumulative[:, :, -1])
    return (inner_part, final_state, total_decay, cumulative)

def carry_part(c_coef, cumulative, entering):
    reached = jnp.einsum('stn,shpn->sthp', c_coef.astype(jnp.float32), entering, precision=lax.Precision.HIGHEST)
    return reached * jnp.swapaxes(jnp.exp(-cumulative), 1, 2)[..., None]

def along_sequences(x_vals, b_coef, c_coef, rates, length):
    sequences, full_len, head_count, head_dim = x_vals.shape
    state_size = b_coef.shape[2]
    spans = full_len // length
    inputs = (jnp.moveaxis(x_vals.reshape(sequences, spans, length, head_count, head_dim), 1, 0), jnp.moveaxis(b_coef.reshape(sequences, spans, length, state_size), 1, 0), jnp.moveaxis(c_coef.reshape(sequences, spans, length, state_size), 1, 0), jnp.moveaxis(rates.reshape(sequences, head_count, spans, length), 2, 0))

    def advance(carried, block_args):
        inner_part, final_state, total_decay, cumulative = block_parts(*block_args)
        result = inner_part + carry_part(block_args[2], cumulative, carried)
        return (total_decay[:, :, None, None] * carried + final_state, result)
    initial = jnp.zeros((sequences, head_count, head_dim, state_size), jnp.float32)
    _, results = lax.scan(advance, initial, inputs)
    return jnp.moveaxis(results, 0, 1).reshape(sequences, full_len, head_count, head_dim)

def orient(direction, scan_in, coeffs, rate_all):
    rows_n, cols_n, width = scan_in.shape
    head_count = rate_all.shape[1]
    state_size = coeffs.shape[2] // 8
    x_vals = scan_in.reshape(rows_n, cols_n, head_count, width // head_count)
    b_coef = coeffs[:, :, 2 * direction * state_size:(2 * direction + 1) * state_size]
    c_coef = coeffs[:, :, (2 * direction + 1) * state_size:(2 * direction + 2) * state_size]
    rates = rate_all[direction]
    if direction >= 2:
        x_vals = jnp.swapaxes(x_vals, 0, 1)
        b_coef = jnp.swapaxes(b_coef, 0, 1)
        c_coef = jnp.swapaxes(c_coef, 0, 1)
        rates = jnp.transpose(rates, (2, 0, 1))
    else:
        rates = jnp.transpose(rates, (1, 0, 2))
    if direction % 2 == 1:
        x_vals = jnp.flip(x_vals, 1)
        b_coef = jnp.flip(b_coef, 1)
        c_coef = jnp.flip(c_coef, 1)
        rates = jnp.flip(rates, 2)
    return (x_vals, b_coef, c_coef, rates)

def restore(direction, result, rows_n, cols_n):
    if direction % 2 == 1:
        result = jnp.flip(result, 1)
    if direction >= 2:
        result = jnp.swapaxes(result, 0, 1)
    return result.reshape(rows_n, cols_n, -1)

def reference(tile_feats, tile_cell, tile_mask, tile_count, background, norm_gain, in_x, in_z, conv_w, conv_bias, x_proj, skip_gain, decay_rate, out_gain, out_w, mlp_gain, ff_in, ff_out):
    cols_dev = GRID_W // RW
    slot_live = jnp.arange(CAP, dtype=jnp.int32)[None, None, :] < tile_count[:, :, None]
    owner_index = jnp.arange(DEVICES, dtype=jnp.int32)[None, :, None]
    row_pos = owner_index // cols_dev * RH + tile_cell // RW
    col_pos = owner_index % cols_dev * RW + tile_cell % RW
    target = jnp.where(slot_live, row_pos * GRID_W + col_pos, GRID_H * GRID_W).astype(jnp.int32)
    values = jnp.where(tile_mask[..., None] == 1, tile_feats, background[None, None, None, :])
    tile_grid = jnp.zeros((GRID_H * GRID_W + 1, C), jnp.bfloat16).at[target.reshape(-1)].set(values.reshape(-1, C))
    tile_grid = tile_grid[:-1].reshape(GRID_H, GRID_W, C)

    def project(window):
        normed = rms_scale(window.astype(jnp.float32), norm_gain).astype(jnp.bfloat16)
        inner_x = jnp.dot(normed, in_x, preferred_element_type=jnp.float32).astype(jnp.bfloat16)
        gate_out = jnp.dot(normed, in_z, preferred_element_type=jnp.float32).astype(jnp.bfloat16)
        return (inner_x, gate_out)
    inner_x, gate_out = lax.map(project, tile_grid.reshape(GRID_H // RH, RH, GRID_W, C))
    inner_x = inner_x.reshape(GRID_H, GRID_W, DI)
    gate_out = gate_out.reshape(GRID_H, GRID_W, DI)
    padded = jnp.pad(inner_x, ((1, 1), (1, 1), (0, 0)))

    def convolve(block_index):
        window = lax.dynamic_slice_in_dim(padded, (block_index * RH).astype(jnp.int32), RH + 2, 0)
        summed_conv = jnp.zeros((RH, GRID_W, DI), jnp.float32) + conv_bias
        for shift_row in range(3):
            for shift_col in range(3):
                summed_conv = summed_conv + window[shift_row:shift_row + RH, shift_col:shift_col + GRID_W].astype(jnp.float32) * conv_w[shift_row, shift_col]
        return jax.nn.silu(summed_conv).astype(jnp.bfloat16)
    scan_in = lax.map(convolve, jnp.arange(GRID_H // RH, dtype=jnp.int32)).reshape(GRID_H, GRID_W, DI)
    coeffs = jnp.dot(scan_in, x_proj, preferred_element_type=jnp.float32).astype(jnp.bfloat16)
    summed = skip_gain * scan_in.astype(jnp.float32)
    for direction in range(DIRS):
        x_vals, b_coef, c_coef, rates = orient(direction, scan_in, coeffs, decay_rate)
        length = RH if direction >= 2 else RW
        result = along_sequences(x_vals, b_coef, c_coef, rates, length)
        summed = summed + restore(direction, result, GRID_H, GRID_W)

    def finish(window):
        summed_part, gate_part, grid_part = window
        gated_out = (rms_scale(summed_part, out_gain) * jax.nn.silu(gate_part.astype(jnp.float32))).astype(jnp.bfloat16)
        middle = (jnp.dot(gated_out, out_w, preferred_element_type=jnp.float32) + grid_part.astype(jnp.float32)).astype(jnp.bfloat16)
        normed_mid = rms_scale(middle.astype(jnp.float32), mlp_gain).astype(jnp.bfloat16)
        hidden = jax.nn.gelu(jnp.dot(normed_mid, ff_in, preferred_element_type=jnp.float32), approximate=False).astype(jnp.bfloat16)
        return (jnp.dot(hidden, ff_out, preferred_element_type=jnp.float32) + middle.astype(jnp.float32)).astype(jnp.bfloat16)
    blocks = GRID_H // RH
    block_out = lax.map(finish, (summed.reshape(blocks, RH, GRID_W, DI), gate_out.reshape(blocks, RH, GRID_W, DI), tile_grid.reshape(blocks, RH, GRID_W, C)))
    return block_out.reshape(GRID_H, GRID_W, C)
```

```python
import functools
import jax
import jax.numpy as jnp
from jax import lax
from jax.experimental import pallas as pl
from jax.experimental.pallas import tpu as pltpu
from jax.sharding import PartitionSpec as P

F32 = jnp.float32
BF16 = jnp.bfloat16
LANES = 128
SUB = 8
VMEM_BYTES = 58 * 1024 * 1024


def whole():
    return pl.BlockSpec(memory_space=pltpu.VMEM)


def call(body, outs, ins, scratch=(), name=None):
    return pl.pallas_call(
        body,
        out_shape=outs,
        in_specs=ins,
        out_specs=jax.tree.map(lambda _: whole(), outs),
        scratch_shapes=list(scratch),
        compiler_params=pltpu.CompilerParams(vmem_limit_bytes=VMEM_BYTES),
        name=name,
    )


def dot(a, b):
    return jnp.dot(a, b, preferred_element_type=F32)


def dot_nt(a, b):
    return lax.dot_general(a, b, (((1,), (1,)), ((), ())), preferred_element_type=F32)


def dot_tn(a, b):
    return lax.dot_general(a, b, (((0,), (0,)), ((), ())), preferred_element_type=F32)


def rms_scale(values, gains):
    return values * lax.rsqrt(jnp.mean(values * values, axis=-1, keepdims=True) + 1e-06) * gains


def two_parts(values):
    high = lax.reduce_precision(values, 8, 7)
    return high.astype(BF16), (values - high).astype(BF16)


def factor_rows(values):
    high, low = two_parts(values)
    heads = values.shape[1]
    both = jnp.concatenate([high, low], axis=1)
    return jnp.pad(both, ((0, 0), (0, 16 - 2 * heads), (0, 0), (0, 0)))


def row_layout(parts):
    return jnp.transpose(parts, (0, 2, 1, 3))


def col_layout(parts):
    k, m, r, c = parts.shape
    parts = parts.reshape(k, m, r, c // SUB, SUB)
    return jnp.transpose(parts, (0, 3, 1, 2, 4)).reshape(k, c // SUB, m, r * SUB)


def decay_factors(decay):
    rows_n, cols_n = decay.shape[2:]
    upto_c = jnp.triu(jnp.ones((cols_n, cols_n), F32))
    upto_r = jnp.triu(jnp.ones((rows_n, rows_n), F32))
    exact = lax.Precision.HIGHEST
    cum = jnp.stack(
        [
            jnp.einsum("hru,ut->hrt", decay[0], upto_c, precision=exact),
            jnp.einsum("hru,ut->hrt", decay[1], upto_c.T, precision=exact),
            jnp.einsum("huc,ut->htc", decay[2], upto_r, precision=exact),
            jnp.einsum("huc,ut->htc", decay[3], upto_r.T, precision=exact),
        ]
    )
    total_row = jnp.sum(decay[:2], axis=3)
    total_col = jnp.sum(decay[2:], axis=2)
    mid = 0.5 * jnp.concatenate(
        [
            jnp.broadcast_to(total_row[..., None], decay[:2].shape),
            jnp.broadcast_to(total_col[:, :, None, :], decay[2:].shape),
        ]
    )
    weight = jnp.sqrt(-jnp.expm1(-2.0 * decay))
    into = factor_rows(weight * jnp.exp(cum - mid))
    out = factor_rows(jnp.exp(mid - cum))
    return (
        row_layout(into[:2]),
        row_layout(out[:2]),
        col_layout(into[2:]),
        col_layout(out[2:]),
        total_row,
        total_col,
    )


def place_body(cells, got, gain, in_x, grid_out, inner_out, left_out, right_out, src, dst):
    slots = got.shape[0]
    channels = grid_out.shape[1]
    cells_n = grid_out.shape[0]
    cols_n = cells_n // left_out.shape[0]

    def fill(i, carry):
        at = pl.ds(pl.multiple_of(i * 256, 256), 256)
        dst[at, :] = jnp.zeros((256, dst.shape[1]), F32)
        return carry

    lax.fori_loop(0, cells_n // 256, fill, 0)

    def widen(i, carry):
        at = pl.ds(pl.multiple_of(i * 256, 256), 256)
        src[at, :] = got[at, :].astype(F32)
        return carry

    lax.fori_loop(0, slots // 256, widen, 0)

    def place(i, carry):
        base = i * 16
        for j in range(16):
            cell = cells[base + j]
            dst[pl.ds(cell, 1), :] = src[pl.ds(base + j, 1), :]
        return carry

    lax.fori_loop(0, slots // 16, place, 0)

    def project(r, carry):
        at = pl.ds(pl.multiple_of(r * cols_n, cols_n), cols_n)
        tiles = dst[at, :channels]
        grid_out[at, :] = tiles.astype(BF16)
        normed = rms_scale(tiles, gain[...]).astype(BF16)
        inner = dot(normed, in_x[...]).astype(BF16)
        inner_out[at, :] = inner
        wide = inner.astype(F32)
        left_out[pl.ds(r, 1), :] = wide[:1]
        right_out[pl.ds(r, 1), :] = wide[cols_n - 1 :]
        return carry

    lax.fori_loop(0, cells_n // cols_n, project, 0)


def place(cells, got, gain, in_x, rows_n, cols_n, channels):
    cells_n = rows_n * cols_n
    width = in_x.shape[1]
    outs = (
        jax.ShapeDtypeStruct((cells_n, channels), BF16),
        jax.ShapeDtypeStruct((cells_n, width), BF16),
        jax.ShapeDtypeStruct((rows_n, width), F32),
        jax.ShapeDtypeStruct((rows_n, width), F32),
    )
    return call(
        place_body,
        outs,
        [pl.BlockSpec(memory_space=pltpu.SMEM), whole(), whole(), whole()],
        [
            pltpu.VMEM(got.shape, F32),
            pltpu.VMEM((cells_n + SUB, got.shape[1]), F32),
        ],
        name="place_norm_project",
    )(cells, got, gain, in_x)


def gate_body(grid, gain, in_z, gate_out, *, block):
    def step(i, carry):
        at = pl.ds(pl.multiple_of(i * block, block), block)
        normed = rms_scale(grid[at, :].astype(F32), gain[...]).astype(BF16)
        gate = dot(normed, in_z[...]).astype(BF16).astype(F32)
        gate_out[at, :] = (gate / (1.0 + jnp.exp(-gate))).astype(BF16)
        return carry

    lax.fori_loop(0, grid.shape[0] // block, step, 0)


def gate(grid, gain, in_z):
    return call(
        functools.partial(gate_body, block=128),
        jax.ShapeDtypeStruct((grid.shape[0], in_z.shape[1]), BF16),
        [whole()] * 3,
        name="gate",
    )(grid, gain, in_z)


def spread(parts, heads_map):
    return dot_tn(parts, heads_map)


def own_column(shape, row_mod, col_mod):
    rows = lax.broadcasted_iota(jnp.int32, shape, 0)
    cols = lax.broadcasted_iota(jnp.int32, shape, 1)
    return (rows & (row_mod - 1)) == (cols & (col_mod - 1))


def conv_body(
    inner, above, below, left, right, conv_w, conv_bias, x_proj, into_row, into_col, heads_map, pick_b,
    x_out, coef_out, state_row, state_col,
    padded, x_wide, coef_wide, left_sum, right_sum,
):
    rows_n, cols_n, width = inner.shape
    state_size = state_row.shape[2]
    padded[0] = above[...]
    padded[rows_n + 1] = below[...]

    def move(r, carry):
        padded[r + 1] = inner[r]
        return carry

    lax.fori_loop(0, rows_n, move, 0)
    for edge, column, sums in ((left, 0, left_sum), (right, 2, right_sum)):
        total = jnp.zeros((rows_n, 1, width), F32)
        for i in range(3):
            total = total + edge[i : i + rows_n] * conv_w[3 * i + column : 3 * i + column + 1, :][None]
        sums[...] = total
    first = lax.broadcasted_iota(jnp.int32, (cols_n, LANES), 0) == 0
    last = lax.broadcasted_iota(jnp.int32, (cols_n, LANES), 0) == cols_n - 1

    def row_step(r, carry):
        for part in range(width // LANES):
            lanes = slice(part * LANES, (part + 1) * LANES)
            rows = [padded[r + i, :, lanes].astype(F32) for i in range(3)]
            sums = []
            for j in range(3):
                total = rows[0] * conv_w[j : j + 1, lanes]
                total = total + rows[1] * conv_w[3 + j : 4 + j, lanes]
                sums.append(total + rows[2] * conv_w[6 + j : 7 + j, lanes])
            from_left = jnp.where(first, left_sum[r, :, lanes], pltpu.roll(sums[0], 1, 0))
            from_right = jnp.where(
                last, right_sum[r, :, lanes], pltpu.roll(sums[2], cols_n - 1, 0)
            )
            value = conv_bias[:, lanes] + from_left + sums[1] + from_right
            scanned = (value / (1.0 + jnp.exp(-value))).astype(BF16)
            x_out[r, :, lanes] = scanned
            x_wide[r, :, lanes] = scanned.astype(F32)
        coef = dot(x_out[r], x_proj[...]).astype(BF16)
        coef_out[r] = coef
        coef_wide[r] = coef.astype(F32)
        flipped = coef.T
        for k in range(2):
            scaled = (x_wide[r] * spread(into_row[k, r], heads_map[...])).astype(BF16)
            b_part = flipped[2 * k * state_size : (2 * k + 1) * state_size, :]
            state_row[r, k] = dot(b_part, scaled).astype(BF16)
        return carry

    lax.fori_loop(0, rows_n, row_step, 0)
    size = rows_n * SUB
    own = own_column((LANES, size), SUB, SUB)

    def col_step(g, carry):
        at = pl.ds(pl.multiple_of(g * SUB, SUB), SUB)
        x_group = x_wide[:, at, :].reshape(size, width)
        coef = coef_wide[:, at, :].reshape(size, LANES).astype(BF16)
        for k in range(2):
            scaled = (x_group * spread(into_col[k, g], heads_map[...])).astype(BF16)
            b_part = jnp.where(own, dot_nt(pick_b[k], coef), 0.0).astype(BF16)
            state_col[g, k] = dot(b_part, scaled).astype(BF16)
        return carry

    lax.fori_loop(0, cols_n // SUB, col_step, 0)


def conv_and_states(inner, above, below, left, right, conv_w, conv_bias, x_proj, into_row, into_col, heads_map, pick_b, state_size):
    rows_n, cols_n, width = inner.shape
    outs = (
        jax.ShapeDtypeStruct((rows_n, cols_n, width), BF16),
        jax.ShapeDtypeStruct((rows_n, cols_n, LANES), BF16),
        jax.ShapeDtypeStruct((rows_n, 2, state_size, width), BF16),
        jax.ShapeDtypeStruct((cols_n // SUB, 2, SUB * state_size, width), BF16),
    )
    return call(
        conv_body,
        outs,
        [whole()] * 12,
        [
            pltpu.VMEM((rows_n + 2, cols_n, width), BF16),
            pltpu.VMEM((rows_n, cols_n, width), F32),
            pltpu.VMEM((rows_n, cols_n, LANES), F32),
            pltpu.VMEM((rows_n, 1, width), F32),
            pltpu.VMEM((rows_n, 1, width), F32),
        ],
        name="conv_states",
    )(inner, above, below, left, right, conv_w, conv_bias, x_proj, into_row, into_col, heads_map, pick_b)


def inner_body(
    x_in, coef_in, into_row, out_row, into_col, out_col, heads_map, skip, total_out, x_wide, coef_wide, acc
):
    rows_n, cols_n, width = x_in.shape
    state_size = LANES // 8
    lane = lax.broadcasted_iota(jnp.int32, (1, LANES), 1)
    t_row = lax.broadcasted_iota(jnp.int32, (cols_n, cols_n), 0)
    u_row = lax.broadcasted_iota(jnp.int32, (cols_n, cols_n), 1)
    row_masks = (t_row >= u_row, t_row <= u_row)

    def c_at_b(wide, k):
        rolled = pltpu.roll(wide, LANES - state_size, 1)
        return jnp.where((lane // state_size) == 2 * k, rolled, 0.0).astype(BF16)

    def row_step(r, carry):
        x_row = x_in[r].astype(F32)
        x_wide[r] = x_row
        coef = coef_in[r]
        wide = coef.astype(F32)
        coef_wide[r] = wide
        total = x_row * skip[...]
        for k in range(2):
            scores = dot_nt(c_at_b(wide, k), coef)
            mixing = jnp.where(row_masks[k], scores, 0.0).astype(BF16)
            scaled = (x_row * spread(into_row[k, r], heads_map[...])).astype(BF16)
            total = total + dot(mixing, scaled) * spread(out_row[k, r], heads_map[...])
        acc[r] = total
        return carry

    lax.fori_loop(0, rows_n, row_step, 0)
    size = rows_n * SUB
    t_col = lax.broadcasted_iota(jnp.int32, (size, size), 0)
    u_col = lax.broadcasted_iota(jnp.int32, (size, size), 1)
    same = (t_col & (SUB - 1)) == (u_col & (SUB - 1))
    col_masks = (same & (t_col >= u_col), same & (t_col <= u_col))

    def col_step(g, carry):
        at = pl.ds(pl.multiple_of(g * SUB, SUB), SUB)
        x_group = x_wide[:, at, :].reshape(size, width)
        wide = coef_wide[:, at, :].reshape(size, LANES)
        coef = wide.astype(BF16)
        total = acc[:, at, :].reshape(size, width)
        for k in range(2):
            scores = dot_nt(c_at_b(wide, k + 2), coef)
            mixing = jnp.where(col_masks[k], scores, 0.0).astype(BF16)
            scaled = (x_group * spread(into_col[k, g], heads_map[...])).astype(BF16)
            total = total + dot(mixing, scaled) * spread(out_col[k, g], heads_map[...])
        acc[:, at, :] = total.reshape(rows_n, SUB, width)
        return carry

    lax.fori_loop(0, cols_n // SUB, col_step, 0)

    def emit(r, carry):
        total_out[r] = acc[r].astype(total_out.dtype)
        return carry

    lax.fori_loop(0, rows_n, emit, 0)


def inner_scans(x_in, coef_in, into_row, out_row, into_col, out_col, heads_map, skip):
    return call(
        inner_body,
        jax.ShapeDtypeStruct(x_in.shape, BF16),
        [whole()] * 8,
        [
            pltpu.VMEM(x_in.shape, F32),
            pltpu.VMEM(coef_in.shape, F32),
            pltpu.VMEM(x_in.shape, F32),
        ],
        name="inner_scans",
    )(x_in, coef_in, into_row, out_row, into_col, out_col, heads_map, skip)


def chain_body(states, half, decay, entering):
    peers, units = states.shape[0], states.shape[1]
    deep = states.shape[3]
    lines = half.shape[3]
    width = states.shape[4]
    for k in range(2):
        order = range(peers) if k == 0 else range(peers - 1, -1, -1)
        for unit in range(units):
            for part in range(width // LANES):
                lanes = slice(part * LANES, (part + 1) * LANES)
                before = jnp.zeros((deep, LANES), F32)
                for at in order:
                    scale = half[at, k, unit, :, lanes]
                    keep = decay[at, k, unit, :, lanes]
                    own = states[at, unit, k, :, lanes].astype(F32)
                    if lines > 1:
                        shape = (deep // lines, lines, LANES)
                        scale, keep = scale[None], keep[None]
                        before, own = before.reshape(shape), own.reshape(shape)
                    entering[at, unit, k, :, lanes] = (scale * before).reshape(deep, LANES).astype(BF16)
                    before = (keep * before + scale * own).reshape(deep, LANES)


def chain(states, half, decay):
    return call(
        chain_body, jax.ShapeDtypeStruct(states.shape, BF16), [whole()] * 3, name="chain"
    )(states, half, decay)


def line_factors(total, axis, width, unit_lines):
    peers, index = lax.axis_size(axis), lax.axis_index(axis)
    k, heads, lines = total.shape
    mine = lines // peers
    everyone = lax.all_gather(total, axis)
    ours = lax.dynamic_slice_in_dim(everyone, index * mine, mine, axis=3)
    ours = jnp.transpose(ours, (0, 1, 3, 2)).reshape(peers, k, mine // unit_lines, unit_lines, heads)
    ours = jnp.repeat(ours, width // heads, axis=-1)
    return jnp.exp(-0.5 * ours), jnp.exp(-ours)


def pass_states(states, factors, axis):
    peers = lax.axis_size(axis)
    got = lax.all_to_all(states, axis, split_axis=0, concat_axis=0, tiled=True)
    split = got.reshape((peers, got.shape[0] // peers) + got.shape[1:])
    entering = chain(split, *factors).reshape(states.shape)
    return lax.all_to_all(entering, axis, split_axis=0, concat_axis=0, tiled=True)


def finish_body(
    total, coef_in, enter_row, enter_col, out_row, out_col, heads_map, pick_c, gate_in, grid, out_gain, out_w,
    mlp_gain, ff_in, ff_out, block_out, coef_wide, acc,
):
    rows_n, cols_n, width = total.shape
    state_size = enter_row.shape[2]

    def row_step(r, carry):
        coef = coef_in[r]
        wide = coef.astype(F32)
        coef_wide[r] = wide
        value = total[r].astype(F32)
        for k in range(2):
            c_part = coef[:, (2 * k + 1) * state_size : (2 * k + 2) * state_size]
            value = value + dot(c_part, enter_row[r, k]) * spread(out_row[k, r], heads_map[...])
        acc[r] = value
        return carry

    lax.fori_loop(0, rows_n, row_step, 0)
    size = rows_n * SUB
    own = own_column((size, LANES), SUB, SUB)

    def col_step(g, carry):
        at = pl.ds(pl.multiple_of(g * SUB, SUB), SUB)
        coef = coef_wide[:, at, :].reshape(size, LANES).astype(BF16)
        value = acc[:, at, :].reshape(size, width)
        for k in range(2):
            c_part = jnp.where(own, dot(coef, pick_c[k]), 0.0).astype(BF16)
            value = value + dot(c_part, enter_col[g, k]) * spread(out_col[k, g], heads_map[...])
        acc[:, at, :] = value.reshape(rows_n, SUB, width)
        return carry

    lax.fori_loop(0, cols_n // SUB, col_step, 0)

    def last(r, carry):
        at = pl.ds(pl.multiple_of(r * cols_n, cols_n), cols_n)
        gated = (rms_scale(acc[r], out_gain[...]) * gate_in[at, :].astype(F32)).astype(BF16)
        middle = (dot(gated, out_w[...]) + grid[at, :].astype(F32)).astype(BF16)
        wide = middle.astype(F32)
        normed = rms_scale(wide, mlp_gain[...]).astype(BF16)
        hidden = dot(normed, ff_in[...])
        hidden = (hidden * (0.5 + 0.5 * lax.erf(hidden * (0.5**0.5)))).astype(BF16)
        block_out[r] = (dot(hidden, ff_out[...]) + wide).astype(BF16)
        return carry

    lax.fori_loop(0, rows_n, last, 0)


def finish(total, coef, *rest, channels):
    rows_n, cols_n, width = total.shape
    return call(
        finish_body,
        jax.ShapeDtypeStruct((rows_n, cols_n, channels), BF16),
        [whole()] * 15,
        [pltpu.VMEM(coef.shape, F32), pltpu.VMEM(total.shape, F32)],
        name="finish",
    )(total, coef, *rest)


def shifted(block, axis, up):
    count = lax.axis_size(axis)
    pairs = [(i, i + 1) if up else (i + 1, i) for i in range(count - 1)]
    return lax.ppermute(block, axis, pairs)


def local(
    tile_feats, tile_cell, tile_mask, tile_count, background, norm_gain, in_x, in_z, conv_w, conv_bias, x_proj,
    skip_gain, decay_rate, out_gain, out_w, mlp_gain, ff_in, ff_out,
):
    heads, rows_n, cols_n = decay_rate.shape[1:]
    owners, slots, channels = tile_feats.shape[1:]
    width = in_x.shape[1]
    state_size = x_proj.shape[1] // 8
    cells_n = rows_n * cols_n

    values = jnp.where(tile_mask[0][..., None] == 1, tile_feats[0], background)
    live = jnp.arange(slots, dtype=jnp.int32)[None, :] < tile_count[0][:, None]
    marked = jnp.where(live, tile_cell[0], cells_n)
    where = jnp.stack([marked // 64, marked % 64], axis=-1).astype(BF16)
    where = jnp.pad(where, ((0, 0), (0, 0), (0, 62)))
    sent = jnp.concatenate([values, where], axis=-1)
    got = lax.all_to_all(sent, ("row", "col"), split_axis=0, concat_axis=0, tiled=True)
    got = got.reshape(owners * slots, sent.shape[2])
    cells = got[:, channels].astype(jnp.int32) * 64 + got[:, channels + 1].astype(jnp.int32)

    into_row, out_row, into_col, out_col, total_row, total_col = decay_factors(decay_rate)
    row_factors = line_factors(total_row, "col", width, 1)
    col_factors = line_factors(total_col, "row", width, SUB)
    head_of = jnp.arange(width, dtype=jnp.int32) // (width // heads)
    part_of = jnp.arange(16, dtype=jnp.int32)
    heads_map = (
        ((part_of % heads)[:, None] == head_of[None, :]) & (part_of < 2 * heads)[:, None]
    ).astype(BF16)
    lane = jnp.arange(LANES, dtype=jnp.int32)
    picks = [
        (lane[:, None] == (m * state_size + lane // SUB)[None, :]).astype(BF16) for m in range(4, 8)
    ]
    pick_b = jnp.stack([picks[0].T, picks[2].T])
    pick_c = jnp.stack([picks[1], picks[3]])

    grid, inner, left_edge, right_edge = place(
        cells, got, norm_gain[None], in_x, rows_n, cols_n, channels
    )
    from_left = shifted(right_edge, "col", True).astype(BF16)
    from_right = shifted(left_edge, "col", False).astype(BF16)
    top = jnp.concatenate([inner[:cols_n], from_left[:1], from_right[:1]])
    bottom = jnp.concatenate([inner[cells_n - cols_n :], from_left[rows_n - 1 :], from_right[rows_n - 1 :]])
    above = shifted(bottom, "row", True)
    below = shifted(top, "row", False)
    gated = gate(grid, norm_gain[None], in_z)
    left = jnp.concatenate([above[cols_n : cols_n + 1], from_left, below[cols_n : cols_n + 1]])[:, None].astype(F32)
    right = jnp.concatenate([above[cols_n + 1 :], from_right, below[cols_n + 1 :]])[:, None].astype(F32)

    x_in, coef, state_row, state_col = conv_and_states(
        inner.reshape(rows_n, cols_n, width), above[:cols_n], below[:cols_n], left, right,
        conv_w.reshape(9, width), conv_bias[None], x_proj, into_row, into_col, heads_map, pick_b, state_size,
    )
    enter_col = pass_states(state_col, col_factors, "row")
    enter_row = pass_states(state_row, row_factors, "col")
    total = inner_scans(x_in, coef, into_row, out_row, into_col, out_col, heads_map, skip_gain[None])
    return finish(
        total, coef, enter_row, enter_col, out_row, out_col, heads_map, pick_c, gated, grid, out_gain[None], out_w,
        mlp_gain[None], ff_in, ff_out, channels=channels,
    )


def solution(mesh):
    spread_all = (
        P(("row", "col"), None, None, None),
        P(("row", "col"), None, None),
        P(("row", "col"), None, None),
        P(("row", "col"), None),
    )
    placed = spread_all + (P(),) * 8 + (P(None, None, "row", "col"),) + (P(),) * 5
    return jax.shard_map(
        local, mesh=mesh, in_specs=placed, out_specs=P("row", "col", None), check_vma=False
    )
```

```python
import functools
import jax
import jax.numpy as jnp
from jax import lax
from jax.experimental import pallas as pl
from jax.experimental.pallas import tpu as pltpu
from jax.sharding import PartitionSpec as P

F32 = jnp.float32
BF16 = jnp.bfloat16
BLOCK = 1024
UNROLL = 4
LANES = 128
SUB = 8
VMEM_BYTES = 58 * 1024 * 1024


def whole():
    return pl.BlockSpec(memory_space=pltpu.VMEM)


def call(body, outs, ins, scratch=(), name=None):
    return pl.pallas_call(
        body,
        out_shape=outs,
        in_specs=ins,
        out_specs=jax.tree.map(lambda _: whole(), outs),
        scratch_shapes=list(scratch),
        compiler_params=pltpu.CompilerParams(vmem_limit_bytes=VMEM_BYTES),
        name=name,
    )


def loop(count, step, unroll=1):
    def body(i, carry):
        for j in range(unroll):
            step(i * unroll + j)
        return carry

    lax.fori_loop(0, count // unroll, body, 0)


def dot(a, b):
    return jnp.dot(a, b, preferred_element_type=F32)


def dot_nt(a, b):
    return lax.dot_general(a, b, (((1,), (1,)), ((), ())), preferred_element_type=F32)


def dot_tn(a, b):
    return lax.dot_general(a, b, (((0,), (0,)), ((), ())), preferred_element_type=F32)


def rms_scale(values, gains):
    return values * lax.rsqrt(jnp.mean(values * values, axis=-1, keepdims=True) + 1e-06) * gains


def two_parts(values):
    high = lax.reduce_precision(values, 8, 7)
    return high.astype(BF16), (values - high).astype(BF16)


def factor_rows(values):
    high, low = two_parts(values)
    heads = values.shape[1]
    both = jnp.concatenate([high, low], axis=1)
    return jnp.pad(both, ((0, 0), (0, 16 - 2 * heads), (0, 0), (0, 0)))


def row_layout(parts):
    return jnp.transpose(parts, (0, 2, 1, 3))


def col_layout(parts):
    k, m, r, c = parts.shape
    parts = parts.reshape(k, m, r, c // SUB, SUB)
    return jnp.transpose(parts, (0, 3, 1, 2, 4)).reshape(k, c // SUB, m, r * SUB)


def decay_factors(decay):
    rows_n, cols_n = decay.shape[2:]
    upto_c = jnp.triu(jnp.ones((cols_n, cols_n), F32))
    upto_r = jnp.triu(jnp.ones((rows_n, rows_n), F32))
    exact = lax.Precision.HIGHEST
    cum = jnp.stack(
        [
            jnp.einsum("hru,ut->hrt", decay[0], upto_c, precision=exact),
            jnp.einsum("hru,ut->hrt", decay[1], upto_c.T, precision=exact),
            jnp.einsum("huc,ut->htc", decay[2], upto_r, precision=exact),
            jnp.einsum("huc,ut->htc", decay[3], upto_r.T, precision=exact),
        ]
    )
    total_row = jnp.sum(decay[:2], axis=3)
    total_col = jnp.sum(decay[2:], axis=2)
    mid = 0.5 * jnp.concatenate(
        [
            jnp.broadcast_to(total_row[..., None], decay[:2].shape),
            jnp.broadcast_to(total_col[:, :, None, :], decay[2:].shape),
        ]
    )
    weight = jnp.sqrt(-jnp.expm1(-2.0 * decay))
    into = factor_rows(weight * jnp.exp(cum - mid))
    out = factor_rows(jnp.exp(mid - cum))
    return (
        row_layout(into[:2]),
        row_layout(out[:2]),
        col_layout(into[2:]),
        col_layout(out[2:]),
        total_row,
        total_col,
    )


def place_body(cells, got, gain, in_x, grid_out, inner_out, left_out, right_out, src, dst):
    slots = got.shape[0]
    channels = grid_out.shape[1]
    cells_n = grid_out.shape[0]
    cols_n = cells_n // left_out.shape[0]

    def fill(i, carry):
        at = pl.ds(pl.multiple_of(i * 256, 256), 256)
        dst[at, :] = jnp.zeros((256, dst.shape[1]), F32)
        return carry

    lax.fori_loop(0, cells_n // 256, fill, 0)

    def widen(i, carry):
        at = pl.ds(pl.multiple_of(i * 256, 256), 256)
        src[at, :] = got[at, :].astype(F32)
        return carry

    lax.fori_loop(0, slots // 256, widen, 0)

    def place(i, carry):
        base = i * 16
        for j in range(16):
            cell = cells[base + j]
            dst[pl.ds(cell, 1), :] = src[pl.ds(base + j, 1), :]
        return carry

    lax.fori_loop(0, slots // 16, place, 0)

    def project(r, carry):
        at = pl.ds(pl.multiple_of(r * cols_n, cols_n), cols_n)
        tiles = dst[at, :channels]
        grid_out[at, :] = tiles.astype(BF16)
        normed = rms_scale(tiles, gain[...]).astype(BF16)
        inner = dot(normed, in_x[...]).astype(BF16)
        inner_out[at, :] = inner
        wide = inner.astype(F32)
        left_out[pl.ds(r, 1), :] = wide[:1]
        right_out[pl.ds(r, 1), :] = wide[cols_n - 1 :]
        return carry

    loop(cells_n // cols_n, lambda r: project(r, 0), UNROLL)


def place(cells, got, gain, in_x, rows_n, cols_n, channels):
    cells_n = rows_n * cols_n
    width = in_x.shape[1]
    outs = (
        jax.ShapeDtypeStruct((cells_n, channels), BF16),
        jax.ShapeDtypeStruct((cells_n, width), BF16),
        jax.ShapeDtypeStruct((rows_n, width), F32),
        jax.ShapeDtypeStruct((rows_n, width), F32),
    )
    return call(
        place_body,
        outs,
        [pl.BlockSpec(memory_space=pltpu.SMEM), whole(), whole(), whole()],
        [
            pltpu.VMEM(got.shape, F32),
            pltpu.VMEM((cells_n + SUB, got.shape[1]), F32),
        ],
        name="place_norm_project",
    )(cells, got, gain, in_x)


def gate_body(grid, gain, in_z, gate_out, *, block):
    def step(i, carry):
        at = pl.ds(pl.multiple_of(i * block, block), block)
        normed = rms_scale(grid[at, :].astype(F32), gain[...]).astype(BF16)
        gate = dot(normed, in_z[...]).astype(BF16).astype(F32)
        gate_out[at, :] = (gate / (1.0 + jnp.exp(-gate))).astype(BF16)
        return carry

    lax.fori_loop(0, grid.shape[0] // block, step, 0)


def gate(grid, gain, in_z):
    return call(
        functools.partial(gate_body, block=BLOCK),
        jax.ShapeDtypeStruct((grid.shape[0], in_z.shape[1]), BF16),
        [whole()] * 3,
        name="gate",
    )(grid, gain, in_z)


def spread(parts, heads_map):
    return dot_tn(parts, heads_map)


def own_column(shape, row_mod, col_mod):
    rows = lax.broadcasted_iota(jnp.int32, shape, 0)
    cols = lax.broadcasted_iota(jnp.int32, shape, 1)
    return (rows & (row_mod - 1)) == (cols & (col_mod - 1))


def conv_body(
    inner, above, below, left, right, conv_w, conv_bias, x_proj, into_row, into_col, heads_map, pick_b,
    x_out, coef_out, state_row, state_col,
    padded, x_wide, coef_wide, left_sum, right_sum,
):
    rows_n, cols_n, width = inner.shape
    state_size = state_row.shape[2]
    padded[0] = above[...]
    padded[rows_n + 1] = below[...]

    def move(r, carry):
        padded[r + 1] = inner[r]
        return carry

    lax.fori_loop(0, rows_n, move, 0)
    for edge, column, sums in ((left, 0, left_sum), (right, 2, right_sum)):
        total = jnp.zeros((rows_n, 1, width), F32)
        for i in range(3):
            total = total + edge[i : i + rows_n] * conv_w[3 * i + column : 3 * i + column + 1, :][None]
        sums[...] = total
    first = lax.broadcasted_iota(jnp.int32, (cols_n, LANES), 0) == 0
    last = lax.broadcasted_iota(jnp.int32, (cols_n, LANES), 0) == cols_n - 1

    def row_step(r, carry):
        for part in range(width // LANES):
            lanes = slice(part * LANES, (part + 1) * LANES)
            rows = [padded[r + i, :, lanes].astype(F32) for i in range(3)]
            sums = []
            for j in range(3):
                total = rows[0] * conv_w[j : j + 1, lanes]
                total = total + rows[1] * conv_w[3 + j : 4 + j, lanes]
                sums.append(total + rows[2] * conv_w[6 + j : 7 + j, lanes])
            from_left = jnp.where(first, left_sum[r, :, lanes], pltpu.roll(sums[0], 1, 0))
            from_right = jnp.where(
                last, right_sum[r, :, lanes], pltpu.roll(sums[2], cols_n - 1, 0)
            )
            value = conv_bias[:, lanes] + from_left + sums[1] + from_right
            scanned = (value / (1.0 + jnp.exp(-value))).astype(BF16)
            x_out[r, :, lanes] = scanned
            x_wide[r, :, lanes] = scanned.astype(F32)
        coef = dot(x_out[r], x_proj[...]).astype(BF16)
        coef_out[r] = coef
        coef_wide[r] = coef.astype(F32)
        flipped = coef.T
        for k in range(2):
            scaled = (x_wide[r] * spread(into_row[k, r], heads_map[...])).astype(BF16)
            b_part = flipped[2 * k * state_size : (2 * k + 1) * state_size, :]
            state_row[r, k] = dot(b_part, scaled).astype(BF16)
        return carry

    loop(rows_n, lambda r: row_step(r, 0), UNROLL)
    size = rows_n * SUB
    own = own_column((LANES, size), SUB, SUB)

    def col_step(g, carry):
        at = pl.ds(pl.multiple_of(g * SUB, SUB), SUB)
        x_group = x_wide[:, at, :].reshape(size, width)
        coef = coef_wide[:, at, :].reshape(size, LANES).astype(BF16)
        for k in range(2):
            scaled = (x_group * spread(into_col[k, g], heads_map[...])).astype(BF16)
            b_part = jnp.where(own, dot_nt(pick_b[k], coef), 0.0).astype(BF16)
            state_col[g, k] = dot(b_part, scaled).astype(BF16)
        return carry

    loop(cols_n // SUB, lambda g: col_step(g, 0), UNROLL)


def conv_and_states(inner, above, below, left, right, conv_w, conv_bias, x_proj, into_row, into_col, heads_map, pick_b, state_size):
    rows_n, cols_n, width = inner.shape
    outs = (
        jax.ShapeDtypeStruct((rows_n, cols_n, width), BF16),
        jax.ShapeDtypeStruct((rows_n, cols_n, LANES), BF16),
        jax.ShapeDtypeStruct((rows_n, 2, state_size, width), BF16),
        jax.ShapeDtypeStruct((cols_n // SUB, 2, SUB * state_size, width), BF16),
    )
    return call(
        conv_body,
        outs,
        [whole()] * 12,
        [
            pltpu.VMEM((rows_n + 2, cols_n, width), BF16),
            pltpu.VMEM((rows_n, cols_n, width), F32),
            pltpu.VMEM((rows_n, cols_n, LANES), F32),
            pltpu.VMEM((rows_n, 1, width), F32),
            pltpu.VMEM((rows_n, 1, width), F32),
        ],
        name="conv_states",
    )(inner, above, below, left, right, conv_w, conv_bias, x_proj, into_row, into_col, heads_map, pick_b)


def c_at_b(wide, k):
    state_size = LANES // 8
    lane = lax.broadcasted_iota(jnp.int32, (1, LANES), 1)
    rolled = pltpu.roll(wide, LANES - state_size, 1)
    return jnp.where((lane // state_size) == 2 * k, rolled, 0.0).astype(BF16)


def inner_row_body(x_in, coef_in, into_row, out_row, heads_map, skip, total_out):
    rows_n, cols_n, width = x_in.shape
    t_row = lax.broadcasted_iota(jnp.int32, (cols_n, cols_n), 0)
    u_row = lax.broadcasted_iota(jnp.int32, (cols_n, cols_n), 1)
    masks = (t_row >= u_row, t_row <= u_row)

    def row_step(r):
        x_row = x_in[r].astype(F32)
        coef = coef_in[r]
        wide = coef.astype(F32)
        total = x_row * skip[...]
        for k in range(2):
            scores = dot_nt(c_at_b(wide, k), coef)
            mixing = jnp.where(masks[k], scores, 0.0).astype(BF16)
            scaled = (x_row * spread(into_row[k, r], heads_map[...])).astype(BF16)
            total = total + dot(mixing, scaled) * spread(out_row[k, r], heads_map[...])
        total_out[r] = total.astype(BF16)

    loop(rows_n, row_step, UNROLL)


def inner_row(x_in, coef_in, into_row, out_row, heads_map, skip):
    return call(
        inner_row_body, jax.ShapeDtypeStruct(x_in.shape, BF16), [whole()] * 6, name="inner_row"
    )(x_in, coef_in, into_row, out_row, heads_map, skip)


def inner_col_body(x_in, coef_in, into_col, out_col, heads_map, total_out, x_wide, coef_wide, acc):
    rows_n, cols_n, width = x_in.shape

    def widen(r):
        x_wide[r] = x_in[r].astype(F32)
        coef_wide[r] = coef_in[r].astype(F32)

    loop(rows_n, widen, UNROLL)
    size = rows_n * SUB
    t_col = lax.broadcasted_iota(jnp.int32, (size, size), 0)
    u_col = lax.broadcasted_iota(jnp.int32, (size, size), 1)
    same = (t_col & (SUB - 1)) == (u_col & (SUB - 1))
    masks = (same & (t_col >= u_col), same & (t_col <= u_col))

    def col_step(g):
        at = pl.ds(pl.multiple_of(g * SUB, SUB), SUB)
        x_group = x_wide[:, at, :].reshape(size, width)
        wide = coef_wide[:, at, :].reshape(size, LANES)
        coef = wide.astype(BF16)
        total = jnp.zeros((size, width), F32)
        for k in range(2):
            scores = dot_nt(c_at_b(wide, k + 2), coef)
            mixing = jnp.where(masks[k], scores, 0.0).astype(BF16)
            scaled = (x_group * spread(into_col[k, g], heads_map[...])).astype(BF16)
            total = total + dot(mixing, scaled) * spread(out_col[k, g], heads_map[...])
        acc[:, at, :] = total.reshape(rows_n, SUB, width)

    loop(cols_n // SUB, col_step, UNROLL)

    def emit(r):
        total_out[r] = acc[r].astype(BF16)

    loop(rows_n, emit, UNROLL)


def inner_col(x_in, coef_in, into_col, out_col, heads_map):
    return call(
        inner_col_body,
        jax.ShapeDtypeStruct(x_in.shape, BF16),
        [whole()] * 5,
        [
            pltpu.VMEM(x_in.shape, F32),
            pltpu.VMEM(coef_in.shape, F32),
            pltpu.VMEM(x_in.shape, F32),
        ],
        name="inner_col",
    )(x_in, coef_in, into_col, out_col, heads_map)


def chain_body(states, half, decay, entering):
    peers, units = states.shape[0], states.shape[1]
    deep = states.shape[3]
    lines = half.shape[3]
    width = states.shape[4]
    for k in range(2):
        order = range(peers) if k == 0 else range(peers - 1, -1, -1)
        for unit in range(units):
            for part in range(width // LANES):
                lanes = slice(part * LANES, (part + 1) * LANES)
                before = jnp.zeros((deep, LANES), F32)
                for at in order:
                    scale = half[at, k, unit, :, lanes]
                    keep = decay[at, k, unit, :, lanes]
                    own = states[at, unit, k, :, lanes].astype(F32)
                    if lines > 1:
                        shape = (deep // lines, lines, LANES)
                        scale, keep = scale[None], keep[None]
                        before, own = before.reshape(shape), own.reshape(shape)
                    entering[at, unit, k, :, lanes] = (scale * before).reshape(deep, LANES).astype(BF16)
                    before = (keep * before + scale * own).reshape(deep, LANES)


def chain(states, half, decay):
    return call(
        chain_body, jax.ShapeDtypeStruct(states.shape, BF16), [whole()] * 3, name="chain"
    )(states, half, decay)


def line_factors(total, axis, width, unit_lines):
    peers, index = lax.axis_size(axis), lax.axis_index(axis)
    k, heads, lines = total.shape
    mine = lines // peers
    everyone = lax.all_gather(total, axis)
    ours = lax.dynamic_slice_in_dim(everyone, index * mine, mine, axis=3)
    ours = jnp.transpose(ours, (0, 1, 3, 2)).reshape(peers, k, mine // unit_lines, unit_lines, heads)
    ours = jnp.repeat(ours, width // heads, axis=-1)
    return jnp.exp(-0.5 * ours), jnp.exp(-ours)


def to_chain(states, axis):
    peers = lax.axis_size(axis)
    got = lax.all_to_all(states, axis, split_axis=0, concat_axis=0, tiled=True)
    return got.reshape((peers, got.shape[0] // peers) + got.shape[1:])


def from_chain(split, factors, axis):
    entering = chain(split, *factors)
    entering = entering.reshape((-1,) + entering.shape[2:])
    return lax.all_to_all(entering, axis, split_axis=0, concat_axis=0, tiled=True)


def finish_body(
    total_row, total_col, coef_in, enter_row, enter_col, out_row, out_col, heads_map, pick_c, gate_in, grid, out_gain, out_w,
    mlp_gain, ff_in, ff_out, block_out, coef_wide, acc,
):
    rows_n, cols_n, width = total_row.shape
    state_size = enter_row.shape[2]

    def row_step(r, carry):
        coef = coef_in[r]
        wide = coef.astype(F32)
        coef_wide[r] = wide
        value = total_row[r].astype(F32) + total_col[r].astype(F32)
        for k in range(2):
            c_part = coef[:, (2 * k + 1) * state_size : (2 * k + 2) * state_size]
            value = value + dot(c_part, enter_row[r, k]) * spread(out_row[k, r], heads_map[...])
        acc[r] = value
        return carry

    loop(rows_n, lambda r: row_step(r, 0), UNROLL)
    size = rows_n * SUB
    own = own_column((size, LANES), SUB, SUB)

    def col_step(g, carry):
        at = pl.ds(pl.multiple_of(g * SUB, SUB), SUB)
        coef = coef_wide[:, at, :].reshape(size, LANES).astype(BF16)
        value = acc[:, at, :].reshape(size, width)
        for k in range(2):
            c_part = jnp.where(own, dot(coef, pick_c[k]), 0.0).astype(BF16)
            value = value + dot(c_part, enter_col[g, k]) * spread(out_col[k, g], heads_map[...])
        acc[:, at, :] = value.reshape(rows_n, SUB, width)
        return carry

    loop(cols_n // SUB, lambda g: col_step(g, 0), UNROLL)

    def last(r, carry):
        at = pl.ds(pl.multiple_of(r * cols_n, cols_n), cols_n)
        gated = (rms_scale(acc[r], out_gain[...]) * gate_in[at, :].astype(F32)).astype(BF16)
        middle = (dot(gated, out_w[...]) + grid[at, :].astype(F32)).astype(BF16)
        wide = middle.astype(F32)
        normed = rms_scale(wide, mlp_gain[...]).astype(BF16)
        hidden = dot(normed, ff_in[...])
        hidden = (hidden * (0.5 + 0.5 * lax.erf(hidden * (0.5**0.5)))).astype(BF16)
        block_out[r] = (dot(hidden, ff_out[...]) + wide).astype(BF16)
        return carry

    loop(rows_n, lambda r: last(r, 0), UNROLL)


def finish(total, total_col, coef, *rest, channels):
    rows_n, cols_n, width = total.shape
    return call(
        finish_body,
        jax.ShapeDtypeStruct((rows_n, cols_n, channels), BF16),
        [whole()] * 16,
        [pltpu.VMEM(coef.shape, F32), pltpu.VMEM(total.shape, F32)],
        name="finish",
    )(total, total_col, coef, *rest)


def shifted(block, axis, up):
    count = lax.axis_size(axis)
    pairs = [(i, i + 1) if up else (i + 1, i) for i in range(count - 1)]
    return lax.ppermute(block, axis, pairs)


def local(
    tile_feats, tile_cell, tile_mask, tile_count, background, norm_gain, in_x, in_z, conv_w, conv_bias, x_proj,
    skip_gain, decay_rate, out_gain, out_w, mlp_gain, ff_in, ff_out,
):
    heads, rows_n, cols_n = decay_rate.shape[1:]
    owners, slots, channels = tile_feats.shape[1:]
    width = in_x.shape[1]
    state_size = x_proj.shape[1] // 8
    cells_n = rows_n * cols_n

    values = jnp.where(tile_mask[0][..., None] == 1, tile_feats[0], background)
    live = jnp.arange(slots, dtype=jnp.int32)[None, :] < tile_count[0][:, None]
    marked = jnp.where(live, tile_cell[0], cells_n)
    where = jnp.stack([marked // 64, marked % 64], axis=-1).astype(BF16)
    where = jnp.pad(where, ((0, 0), (0, 0), (0, 62)))
    sent = jnp.concatenate([values, where], axis=-1)
    got = lax.all_to_all(sent, ("row", "col"), split_axis=0, concat_axis=0, tiled=True)
    into_row, out_row, into_col, out_col, total_row, total_col = decay_factors(decay_rate)
    row_factors = line_factors(total_row, "col", width, 1)
    col_factors = line_factors(total_col, "row", width, SUB)
    head_of = jnp.arange(width, dtype=jnp.int32) // (width // heads)
    part_of = jnp.arange(16, dtype=jnp.int32)
    heads_map = (
        ((part_of % heads)[:, None] == head_of[None, :]) & (part_of < 2 * heads)[:, None]
    ).astype(BF16)
    lane = jnp.arange(LANES, dtype=jnp.int32)
    picks = [
        (lane[:, None] == (m * state_size + lane // SUB)[None, :]).astype(BF16) for m in range(4, 8)
    ]
    pick_b = jnp.stack([picks[0].T, picks[2].T])
    pick_c = jnp.stack([picks[1], picks[3]])

    got = got.reshape(owners * slots, sent.shape[2])
    ready = (into_row, out_row, into_col, out_col, row_factors, col_factors, heads_map, pick_b, pick_c)
    got, ready = lax.optimization_barrier((got, ready))
    into_row, out_row, into_col, out_col, row_factors, col_factors, heads_map, pick_b, pick_c = ready
    cells = got[:, channels].astype(jnp.int32) * 64 + got[:, channels + 1].astype(jnp.int32)

    grid, inner, left_edge, right_edge = place(
        cells, got, norm_gain[None], in_x, rows_n, cols_n, channels
    )
    from_left = shifted(right_edge, "col", True).astype(BF16)
    from_right = shifted(left_edge, "col", False).astype(BF16)
    top = jnp.concatenate([inner[:cols_n], from_left[:1], from_right[:1]])
    bottom = jnp.concatenate([inner[cells_n - cols_n :], from_left[rows_n - 1 :], from_right[rows_n - 1 :]])
    above = shifted(bottom, "row", True)
    below = shifted(top, "row", False)
    left = jnp.concatenate([above[cols_n : cols_n + 1], from_left, below[cols_n : cols_n + 1]])[:, None].astype(F32)
    right = jnp.concatenate([above[cols_n + 1 :], from_right, below[cols_n + 1 :]])[:, None].astype(F32)

    x_in, coef, state_row, state_col = conv_and_states(
        inner.reshape(rows_n, cols_n, width), above[:cols_n], below[:cols_n], left, right,
        conv_w.reshape(9, width), conv_bias[None], x_proj, into_row, into_col, heads_map, pick_b, state_size,
    )
    split_col = to_chain(state_col, "row")
    split_row = to_chain(state_row, "col")
    gated = gate(grid, norm_gain[None], in_z)
    total = inner_row(x_in, coef, into_row, out_row, heads_map, skip_gain[None])
    split_col, split_row, gated, total = lax.optimization_barrier((split_col, split_row, gated, total))
    enter_col = from_chain(split_col, col_factors, "row")
    enter_row = from_chain(split_row, row_factors, "col")
    total_col = inner_col(x_in, coef, into_col, out_col, heads_map)
    return finish(
        total, total_col, coef, enter_row, enter_col, out_row, out_col, heads_map, pick_c, gated, grid, out_gain[None], out_w,
        mlp_gain[None], ff_in, ff_out, channels=channels,
    )


def solution(mesh):
    spread_all = (
        P(("row", "col"), None, None, None),
        P(("row", "col"), None, None),
        P(("row", "col"), None, None),
        P(("row", "col"), None),
    )
    placed = spread_all + (P(),) * 8 + (P(None, None, "row", "col"),) + (P(),) * 5
    return jax.shard_map(
        local, mesh=mesh, in_specs=placed, out_specs=P("row", "col", None), check_vma=False
    )
```

```python
import functools
import jax
import jax.numpy as jnp
from jax import lax
from jax.experimental import pallas as pl
from jax.experimental.pallas import tpu as pltpu
from jax.sharding import PartitionSpec as P

F32 = jnp.float32
BF16 = jnp.bfloat16
BLOCK = 1024
UNROLL = 4
LANES = 128
SUB = 8
VMEM_BYTES = 58 * 1024 * 1024


def whole():
    return pl.BlockSpec(memory_space=pltpu.VMEM)


def call(body, outs, ins, scratch=(), name=None):
    return pl.pallas_call(
        body,
        out_shape=outs,
        in_specs=ins,
        out_specs=jax.tree.map(lambda _: whole(), outs),
        scratch_shapes=list(scratch),
        compiler_params=pltpu.CompilerParams(vmem_limit_bytes=VMEM_BYTES),
        name=name,
    )


def loop(count, step, unroll=1):
    def body(i, carry):
        for j in range(unroll):
            step(i * unroll + j)
        return carry

    lax.fori_loop(0, count // unroll, body, 0)


def dot(a, b):
    return jnp.dot(a, b, preferred_element_type=F32)


def dot_nt(a, b):
    return lax.dot_general(a, b, (((1,), (1,)), ((), ())), preferred_element_type=F32)


def dot_tn(a, b):
    return lax.dot_general(a, b, (((0,), (0,)), ((), ())), preferred_element_type=F32)


def rms_scale(values, gains):
    return values * lax.rsqrt(jnp.mean(values * values, axis=-1, keepdims=True) + 1e-06) * gains


def two_parts(values):
    high = lax.reduce_precision(values, 8, 7)
    return high.astype(BF16), (values - high).astype(BF16)


def factor_rows(values):
    high, low = two_parts(values)
    heads = values.shape[1]
    both = jnp.concatenate([high, low], axis=1)
    return jnp.pad(both, ((0, 0), (0, 16 - 2 * heads), (0, 0), (0, 0)))


def row_layout(parts):
    return jnp.transpose(parts, (0, 2, 1, 3))


def col_layout(parts):
    k, m, r, c = parts.shape
    parts = parts.reshape(k, m, r, c // SUB, SUB)
    return jnp.transpose(parts, (0, 3, 1, 2, 4)).reshape(k, c // SUB, m, r * SUB)


def decay_factors(decay):
    rows_n, cols_n = decay.shape[2:]
    upto_c = jnp.triu(jnp.ones((cols_n, cols_n), F32))
    upto_r = jnp.triu(jnp.ones((rows_n, rows_n), F32))
    exact = lax.Precision.HIGHEST
    cum = jnp.stack(
        [
            jnp.einsum("hru,ut->hrt", decay[0], upto_c, precision=exact),
            jnp.einsum("hru,ut->hrt", decay[1], upto_c.T, precision=exact),
            jnp.einsum("huc,ut->htc", decay[2], upto_r, precision=exact),
            jnp.einsum("huc,ut->htc", decay[3], upto_r.T, precision=exact),
        ]
    )
    total_row = jnp.sum(decay[:2], axis=3)
    total_col = jnp.sum(decay[2:], axis=2)
    mid = 0.5 * jnp.concatenate(
        [
            jnp.broadcast_to(total_row[..., None], decay[:2].shape),
            jnp.broadcast_to(total_col[:, :, None, :], decay[2:].shape),
        ]
    )
    weight = jnp.sqrt(-jnp.expm1(-2.0 * decay))
    into = factor_rows(weight * jnp.exp(cum - mid))
    out = factor_rows(jnp.exp(mid - cum))
    return (
        row_layout(into[:2]),
        row_layout(out[:2]),
        col_layout(into[2:]),
        col_layout(out[2:]),
        total_row,
        total_col,
    )


def place_body(cells, got, gain, in_x, grid_out, inner_out, left_out, right_out, src, dst):
    slots = got.shape[0]
    channels = grid_out.shape[1]
    cells_n = grid_out.shape[0]
    cols_n = cells_n // left_out.shape[0]

    def fill(i, carry):
        at = pl.ds(pl.multiple_of(i * 256, 256), 256)
        dst[at, :] = jnp.zeros((256, dst.shape[1]), F32)
        return carry

    lax.fori_loop(0, cells_n // 256, fill, 0)

    def widen(i, carry):
        at = pl.ds(pl.multiple_of(i * 256, 256), 256)
        src[at, :] = got[at, :].astype(F32)
        return carry

    lax.fori_loop(0, slots // 256, widen, 0)

    def place(i, carry):
        base = i * 16
        for j in range(16):
            cell = cells[base + j]
            dst[pl.ds(cell, 1), :] = src[pl.ds(base + j, 1), :]
        return carry

    lax.fori_loop(0, slots // 16, place, 0)

    def project(r, carry):
        at = pl.ds(pl.multiple_of(r * cols_n, cols_n), cols_n)
        tiles = dst[at, :channels]
        grid_out[at, :] = tiles.astype(BF16)
        normed = rms_scale(tiles, gain[...]).astype(BF16)
        inner = dot(normed, in_x[...]).astype(BF16)
        inner_out[at, :] = inner
        wide = inner.astype(F32)
        left_out[pl.ds(r, 1), :] = wide[:1]
        right_out[pl.ds(r, 1), :] = wide[cols_n - 1 :]
        return carry

    loop(cells_n // cols_n, lambda r: project(r, 0), UNROLL)


def place(cells, got, gain, in_x, rows_n, cols_n, channels):
    cells_n = rows_n * cols_n
    width = in_x.shape[1]
    outs = (
        jax.ShapeDtypeStruct((cells_n, channels), BF16),
        jax.ShapeDtypeStruct((cells_n, width), BF16),
        jax.ShapeDtypeStruct((rows_n, width), F32),
        jax.ShapeDtypeStruct((rows_n, width), F32),
    )
    return call(
        place_body,
        outs,
        [pl.BlockSpec(memory_space=pltpu.SMEM), whole(), whole(), whole()],
        [
            pltpu.VMEM(got.shape, F32),
            pltpu.VMEM((cells_n + SUB, got.shape[1]), F32),
        ],
        name="place_norm_project",
    )(cells, got, gain, in_x)


def gate_body(grid, gain, in_z, gate_out, *, block):
    def step(i, carry):
        at = pl.ds(pl.multiple_of(i * block, block), block)
        normed = rms_scale(grid[at, :].astype(F32), gain[...]).astype(BF16)
        gate = dot(normed, in_z[...]).astype(BF16).astype(F32)
        gate_out[at, :] = (gate / (1.0 + jnp.exp(-gate))).astype(BF16)
        return carry

    lax.fori_loop(0, grid.shape[0] // block, step, 0)


def gate(grid, gain, in_z):
    return call(
        functools.partial(gate_body, block=BLOCK),
        jax.ShapeDtypeStruct((grid.shape[0], in_z.shape[1]), BF16),
        [whole()] * 3,
        name="gate",
    )(grid, gain, in_z)


def spread(parts, heads_map):
    return dot_tn(parts, heads_map)


def own_column(shape, row_mod, col_mod):
    rows = lax.broadcasted_iota(jnp.int32, shape, 0)
    cols = lax.broadcasted_iota(jnp.int32, shape, 1)
    return (rows & (row_mod - 1)) == (cols & (col_mod - 1))


def conv_body(
    spot, inner, above, below, left, right, conv_w, conv_bias, x_proj, into_row, into_col, heads_map, pick_b,
    half_row, half_col, x_out, coef_out, state_row, state_own, state_other,
    padded, x_wide, coef_wide, left_sum, right_sum,
):
    rows_n, cols_n, width = inner.shape
    state_size = LANES // 8
    peers, tile_rows = half_row.shape[:2]
    each = rows_n // peers
    for q in range(peers):
        state_row[q, 2 * each * state_size :] = half_row[q]
    padded[0] = above[...]
    padded[rows_n + 1] = below[...]

    def move(r, carry):
        padded[r + 1] = inner[r]
        return carry

    lax.fori_loop(0, rows_n, move, 0)
    for edge, column, sums in ((left, 0, left_sum), (right, 2, right_sum)):
        total = jnp.zeros((rows_n, 1, width), F32)
        for i in range(3):
            total = total + edge[i : i + rows_n] * conv_w[3 * i + column : 3 * i + column + 1, :][None]
        sums[...] = total
    first = lax.broadcasted_iota(jnp.int32, (cols_n, LANES), 0) == 0
    last = lax.broadcasted_iota(jnp.int32, (cols_n, LANES), 0) == cols_n - 1

    def row_step(r, carry):
        for part in range(width // LANES):
            lanes = slice(part * LANES, (part + 1) * LANES)
            rows = [padded[r + i, :, lanes].astype(F32) for i in range(3)]
            sums = []
            for j in range(3):
                total = rows[0] * conv_w[j : j + 1, lanes]
                total = total + rows[1] * conv_w[3 + j : 4 + j, lanes]
                sums.append(total + rows[2] * conv_w[6 + j : 7 + j, lanes])
            from_left = jnp.where(first, left_sum[r, :, lanes], pltpu.roll(sums[0], 1, 0))
            from_right = jnp.where(
                last, right_sum[r, :, lanes], pltpu.roll(sums[2], cols_n - 1, 0)
            )
            value = conv_bias[:, lanes] + from_left + sums[1] + from_right
            scanned = (value / (1.0 + jnp.exp(-value))).astype(BF16)
            x_out[r, :, lanes] = scanned
            x_wide[r, :, lanes] = scanned.astype(F32)
        coef = dot(x_out[r], x_proj[...]).astype(BF16)
        coef_out[r] = coef
        coef_wide[r] = coef.astype(F32)
        flipped = coef.T
        for k in range(2):
            scaled = (x_wide[r] * spread(into_row[k, r], heads_map[...])).astype(BF16)
            b_part = flipped[2 * k * state_size : (2 * k + 1) * state_size, :]
            at = pl.multiple_of((r % each) * 2 * state_size + k * state_size, state_size)
            state_row[r // each, pl.ds(at, state_size), :] = dot(b_part, scaled).astype(BF16)
        return carry

    loop(rows_n, lambda r: row_step(r, 0), UNROLL)
    size = rows_n * SUB
    own = own_column((LANES, size), SUB, SUB)

    half = state_own.shape[0]
    deep = SUB * state_size

    def col_step(j):
        for states, side in ((state_own, spot[0]), (state_other, 1 - spot[0])):
            g = side * half + j
            at = pl.ds(pl.multiple_of(g * SUB, SUB), SUB)
            x_group = x_wide[:, at, :].reshape(size, width)
            coef = coef_wide[:, at, :].reshape(size, LANES).astype(BF16)
            for k in range(2):
                scaled = (x_group * spread(into_col[k, g], heads_map[...])).astype(BF16)
                b_part = jnp.where(own, dot_nt(pick_b[k], coef), 0.0).astype(BF16)
                states[j, k * deep : (k + 1) * deep, :] = dot(b_part, scaled).astype(BF16)
            states[j, 2 * deep :, :] = half_col[g]

    loop(half, col_step, UNROLL // 2)


def conv_and_states(spot, inner, *rest):
    rows_n, cols_n, width = inner.shape
    half_row, half_col = rest[-2:]
    peers, tile_rows = half_row.shape[:2]
    groups, deep = half_col.shape[0] // 2, 2 * SUB * (LANES // 8) + half_col.shape[1]
    outs = (
        jax.ShapeDtypeStruct((rows_n, cols_n, width), BF16),
        jax.ShapeDtypeStruct((rows_n, cols_n, LANES), BF16),
        jax.ShapeDtypeStruct((peers, rows_n // peers * 2 * (LANES // 8) + tile_rows, width), BF16),
        jax.ShapeDtypeStruct((groups, deep, width), BF16),
        jax.ShapeDtypeStruct((groups, deep, width), BF16),
    )
    return call(
        conv_body,
        outs,
        [pl.BlockSpec(memory_space=pltpu.SMEM)] + [whole()] * 14,
        [
            pltpu.VMEM((rows_n + 2, cols_n, width), BF16),
            pltpu.VMEM((rows_n, cols_n, width), F32),
            pltpu.VMEM((rows_n, cols_n, LANES), F32),
            pltpu.VMEM((rows_n, 1, width), F32),
            pltpu.VMEM((rows_n, 1, width), F32),
        ],
        name="conv_states",
    )(spot, inner, *rest)


def c_at_b(wide, k):
    state_size = LANES // 8
    lane = lax.broadcasted_iota(jnp.int32, (1, LANES), 1)
    rolled = pltpu.roll(wide, LANES - state_size, 1)
    return jnp.where((lane // state_size) == 2 * k, rolled, 0.0).astype(BF16)


def inner_row_body(x_in, coef_in, into_row, out_row, heads_map, skip, total_out):
    rows_n, cols_n, width = x_in.shape
    t_row = lax.broadcasted_iota(jnp.int32, (cols_n, cols_n), 0)
    u_row = lax.broadcasted_iota(jnp.int32, (cols_n, cols_n), 1)
    masks = (t_row >= u_row, t_row <= u_row)

    def row_step(r):
        x_row = x_in[r].astype(F32)
        coef = coef_in[r]
        wide = coef.astype(F32)
        total = x_row * skip[...]
        for k in range(2):
            scores = dot_nt(c_at_b(wide, k), coef)
            mixing = jnp.where(masks[k], scores, 0.0).astype(BF16)
            scaled = (x_row * spread(into_row[k, r], heads_map[...])).astype(BF16)
            total = total + dot(mixing, scaled) * spread(out_row[k, r], heads_map[...])
        total_out[r] = total.astype(BF16)

    loop(rows_n, row_step, UNROLL)


def inner_row(x_in, coef_in, into_row, out_row, heads_map, skip):
    return call(
        inner_row_body, jax.ShapeDtypeStruct(x_in.shape, BF16), [whole()] * 6, name="inner_row"
    )(x_in, coef_in, into_row, out_row, heads_map, skip)


def inner_col_body(x_in, coef_in, into_col, out_col, heads_map, total_out, x_wide, coef_wide, acc):
    rows_n, cols_n, width = x_in.shape

    def widen(r):
        x_wide[r] = x_in[r].astype(F32)
        coef_wide[r] = coef_in[r].astype(F32)

    loop(rows_n, widen, UNROLL)
    size = rows_n * SUB
    t_col = lax.broadcasted_iota(jnp.int32, (size, size), 0)
    u_col = lax.broadcasted_iota(jnp.int32, (size, size), 1)
    same = (t_col & (SUB - 1)) == (u_col & (SUB - 1))
    masks = (same & (t_col >= u_col), same & (t_col <= u_col))

    def col_step(g):
        at = pl.ds(pl.multiple_of(g * SUB, SUB), SUB)
        x_group = x_wide[:, at, :].reshape(size, width)
        wide = coef_wide[:, at, :].reshape(size, LANES)
        coef = wide.astype(BF16)
        total = jnp.zeros((size, width), F32)
        for k in range(2):
            scores = dot_nt(c_at_b(wide, k + 2), coef)
            mixing = jnp.where(masks[k], scores, 0.0).astype(BF16)
            scaled = (x_group * spread(into_col[k, g], heads_map[...])).astype(BF16)
            total = total + dot(mixing, scaled) * spread(out_col[k, g], heads_map[...])
        acc[:, at, :] = total.reshape(rows_n, SUB, width)

    loop(cols_n // SUB, col_step, UNROLL)

    def emit(r):
        total_out[r] = acc[r].astype(BF16)

    loop(rows_n, emit, UNROLL)


def inner_col(x_in, coef_in, into_col, out_col, heads_map):
    return call(
        inner_col_body,
        jax.ShapeDtypeStruct(x_in.shape, BF16),
        [whole()] * 5,
        [
            pltpu.VMEM(x_in.shape, F32),
            pltpu.VMEM(coef_in.shape, F32),
            pltpu.VMEM(x_in.shape, F32),
        ],
        name="inner_col",
    )(x_in, coef_in, into_col, out_col, heads_map)


def half_of(tile, k, heads_map):
    return dot(tile[:, 16 * k : 16 * k + 16], heads_map)


def chain_body(states, heads_map, entering):
    peers = states.shape[0]
    state_size = LANES // 8
    width = states.shape[2]
    lines = entering.shape[1] // (2 * state_size)
    top = 2 * lines * state_size
    for k in range(2):
        order = range(peers) if k == 0 else range(peers - 1, -1, -1)
        before = [jnp.zeros((state_size, width), F32)] * lines
        for at in order:
            scale = half_of(states[at, top:, :LANES], k, heads_map[...])
            for line in range(lines):
                rows = slice((2 * line + k) * state_size, (2 * line + k + 1) * state_size)
                own = scale[line : line + 1]
                entering[at, rows, :] = (own * before[line]).astype(BF16)
                before[line] = own * (own * before[line] + states[at, rows, :].astype(F32))


def chain(states, heads_map, lines):
    peers, _, width = states.shape
    return call(
        chain_body,
        jax.ShapeDtypeStruct((peers, lines * 2 * (LANES // 8), width), BF16),
        [whole()] * 2,
        name="chain",
    )(states, heads_map)


def pair_halves(upper, lower, j, top, heads_map):
    low_rows = pltpu.roll(lower[j, top:, :LANES].astype(F32), SUB, 0)
    first = lax.broadcasted_iota(jnp.int32, low_rows.shape, 0) < SUB
    tile = jnp.where(first, upper[j, top:, :LANES].astype(F32), low_rows).astype(BF16)
    halves = []
    for k in range(2):
        both = half_of(tile, k, heads_map)
        halves.append((both[:SUB], both[SUB:]))
    return tile, halves


def lines_of(states, j, k, lines_shape):
    deep = lines_shape[0] * lines_shape[1]
    return states[j, k * deep : (k + 1) * deep, :].astype(F32).reshape(lines_shape)


def by_core(spot, run, own, got):
    @pl.when(spot[0] == 0)
    def _():
        run(own, got)

    @pl.when(spot[0] != 0)
    def _():
        run(got, own)


def chip_total_body(spot, own, got, heads_map, *sends):
    groups, rows, width = own.shape
    state_size = LANES // 8
    deep = SUB * state_size
    shape = (state_size, SUB, width)
    chips = len(sends) + 1

    def run(upper, lower):
        def step(j):
            tile, halves = pair_halves(upper, lower, j, 2 * deep, heads_map[...])
            (up_2, low_2), (up_3, low_3) = halves
            down = (low_2 * low_2 * up_2) * lines_of(upper, j, 0, shape) + low_2 * lines_of(lower, j, 0, shape)
            rise = (up_3 * up_3 * low_3) * lines_of(lower, j, 1, shape) + up_3 * lines_of(upper, j, 1, shape)
            for shift, send in enumerate(sends, 1):
                past_end = spot[1] + shift >= chips
                send[j, :deep, :] = jnp.where(past_end, rise, down).reshape(deep, width).astype(BF16)
                send[j, deep:, :] = jnp.zeros((rows - 2 * deep, width), BF16)
                send[j, deep:, :LANES] = tile

        loop(groups, step, 1)

    by_core(spot, run, own, got)


def chip_total(spot, own, got, heads_map, chips):
    groups, rows, width = own.shape
    send = jax.ShapeDtypeStruct((groups, rows - SUB * (LANES // 8), width), BF16)
    return call(
        chip_total_body,
        (send,) * (chips - 1),
        [pl.BlockSpec(memory_space=pltpu.SMEM)] + [whole()] * 3,
        name="chip_total",
    )(spot, own, got, heads_map)


def entering_body(spot, own, got, heads_map, *rest):
    receipts, (enter_own, enter_other) = rest[:-2], rest[-2:]
    groups, rows, width = own.shape
    state_size = LANES // 8
    deep = SUB * state_size
    shape = (state_size, SUB, width)
    chips = len(receipts) + 1

    def run(upper, lower, enter_upper, enter_lower):
        def step(j):
            _, halves = pair_halves(upper, lower, j, 2 * deep, heads_map[...])
            (up_2, low_2), (up_3, low_3) = halves
            states = [lines_of(receipt, j, 0, shape) for receipt in receipts]
            keeps = []
            for k in range(2):
                keep = []
                for receipt in receipts:
                    both = half_of(receipt[j, deep:, :LANES], k, heads_map[...])
                    chip = both[:SUB] * both[SUB:]
                    keep.append(chip * chip)
                keeps.append(keep)
            down = jnp.zeros(shape, F32)
            rise = jnp.zeros(shape, F32)
            keep_2 = jnp.ones((SUB, width), F32)
            keep_3 = jnp.ones((SUB, width), F32)
            for away in range(1, chips):
                above, below = away - 1, chips - away - 1
                down = down + jnp.where(spot[1] >= away, keep_2, 0.0) * states[above]
                rise = rise + jnp.where(spot[1] + away < chips, keep_3, 0.0) * states[below]
                keep_2 = keep_2 * keeps[0][above]
                keep_3 = keep_3 * keeps[1][below]
            lower_2 = low_2 * up_2 * (up_2 * down + lines_of(upper, j, 0, shape))
            upper_3 = up_3 * low_3 * (low_3 * rise + lines_of(lower, j, 1, shape))
            enter_upper[j, 0] = (up_2 * down).reshape(deep, width).astype(BF16)
            enter_upper[j, 1] = upper_3.reshape(deep, width).astype(BF16)
            enter_lower[j, 0] = lower_2.reshape(deep, width).astype(BF16)
            enter_lower[j, 1] = (low_3 * rise).reshape(deep, width).astype(BF16)

        loop(groups, step, 1)

    @pl.when(spot[0] == 0)
    def _():
        run(own, got, enter_own, enter_other)

    @pl.when(spot[0] != 0)
    def _():
        run(got, own, enter_other, enter_own)


def entering_states(spot, own, got, heads_map, receipts):
    groups, rows, width = own.shape
    enter = jax.ShapeDtypeStruct((groups, 2, SUB * (LANES // 8), width), BF16)
    return call(
        entering_body,
        (enter, enter),
        [pl.BlockSpec(memory_space=pltpu.SMEM)] + [whole()] * (3 + len(receipts)),
        name="entering",
    )(spot, own, got, heads_map, *receipts)


def half_tiles(total, units):
    k, heads, lines = total.shape
    high, low = two_parts(jnp.exp(-0.5 * total))
    both = jnp.pad(jnp.concatenate([high, low], axis=1), ((0, 0), (0, 16 - 2 * heads), (0, 0)))
    both = jnp.transpose(both, (2, 0, 1)).reshape(units, lines // units, k * 16)
    rows = -(-both.shape[1] // 16) * 16
    return jnp.pad(both, ((0, 0), (0, rows - both.shape[1]), (0, 0)))


def finish_body(
    spot, total_row, total_col, coef_in, enter_row, enter_own, enter_other, out_row, out_col, heads_map, pick_c, gate_in, grid, out_gain, out_w,
    mlp_gain, ff_in, ff_out, block_out, coef_wide, acc,
):
    rows_n, cols_n, width = total_row.shape
    state_size = LANES // 8
    half = enter_own.shape[0]

    def row_step(r, carry):
        coef = coef_in[r]
        wide = coef.astype(F32)
        coef_wide[r] = wide
        value = total_row[r].astype(F32) + total_col[r].astype(F32)
        for k in range(2):
            c_part = coef[:, (2 * k + 1) * state_size : (2 * k + 2) * state_size]
            value = value + dot(c_part, enter_row[r, k]) * spread(out_row[k, r], heads_map[...])
        acc[r] = value
        return carry

    loop(rows_n, lambda r: row_step(r, 0), UNROLL)
    size = rows_n * SUB
    own = own_column((size, LANES), SUB, SUB)

    def col_step(j):
        for enter, side in ((enter_own, spot[0]), (enter_other, 1 - spot[0])):
            g = side * half + j
            at = pl.ds(pl.multiple_of(g * SUB, SUB), SUB)
            coef = coef_wide[:, at, :].reshape(size, LANES).astype(BF16)
            value = acc[:, at, :].reshape(size, width)
            for k in range(2):
                c_part = jnp.where(own, dot(coef, pick_c[k]), 0.0).astype(BF16)
                value = value + dot(c_part, enter[j, k]) * spread(out_col[k, g], heads_map[...])
            acc[:, at, :] = value.reshape(rows_n, SUB, width)

    loop(half, col_step, UNROLL // 2)

    def last(r, carry):
        at = pl.ds(pl.multiple_of(r * cols_n, cols_n), cols_n)
        gated = (rms_scale(acc[r], out_gain[...]) * gate_in[at, :].astype(F32)).astype(BF16)
        middle = (dot(gated, out_w[...]) + grid[at, :].astype(F32)).astype(BF16)
        wide = middle.astype(F32)
        normed = rms_scale(wide, mlp_gain[...]).astype(BF16)
        hidden = dot(normed, ff_in[...])
        hidden = (hidden * (0.5 + 0.5 * lax.erf(hidden * (0.5**0.5)))).astype(BF16)
        block_out[r] = (dot(hidden, ff_out[...]) + wide).astype(BF16)
        return carry

    loop(rows_n, lambda r: last(r, 0), UNROLL)


def finish(spot, total, total_col, coef, *rest, channels):
    rows_n, cols_n, width = total.shape
    return call(
        finish_body,
        jax.ShapeDtypeStruct((rows_n, cols_n, channels), BF16),
        [pl.BlockSpec(memory_space=pltpu.SMEM)] + [whole()] * 17,
        [pltpu.VMEM(coef.shape, F32), pltpu.VMEM(total.shape, F32)],
        name="finish",
    )(spot, total, total_col, coef, *rest)


def shifted(block, axis, up):
    count = lax.axis_size(axis)
    pairs = [(i, i + 1) if up else (i + 1, i) for i in range(count - 1)]
    return lax.ppermute(block, axis, pairs)


def local(
    tile_feats, tile_cell, tile_mask, tile_count, background, norm_gain, in_x, in_z, conv_w, conv_bias, x_proj,
    skip_gain, decay_rate, out_gain, out_w, mlp_gain, ff_in, ff_out,
):
    heads, rows_n, cols_n = decay_rate.shape[1:]
    owners, slots, channels = tile_feats.shape[1:]
    width = in_x.shape[1]
    state_size = x_proj.shape[1] // 8
    cells_n = rows_n * cols_n

    values = jnp.where(tile_mask[0][..., None] == 1, tile_feats[0], background)
    live = jnp.arange(slots, dtype=jnp.int32)[None, :] < tile_count[0][:, None]
    marked = jnp.where(live, tile_cell[0], cells_n)
    where = jnp.stack([marked // 64, marked % 64], axis=-1).astype(BF16)
    where = jnp.pad(where, ((0, 0), (0, 0), (0, 62)))
    sent = jnp.concatenate([values, where], axis=-1)
    got = lax.all_to_all(sent, ("row", "col"), split_axis=0, concat_axis=0, tiled=True)
    into_row, out_row, into_col, out_col, total_row, total_col = decay_factors(decay_rate)
    half_row = half_tiles(total_row, lax.axis_size("col"))
    half_col = half_tiles(total_col, cols_n // SUB)
    half_row = jnp.pad(half_row, ((0, 0), (0, 0), (0, width - half_row.shape[2])))
    half_col = jnp.pad(half_col, ((0, 0), (0, 0), (0, width - half_col.shape[2])))
    line = lax.axis_index("row")
    spot = jnp.stack([line % 2, line // 2]).astype(jnp.int32)
    head_of = jnp.arange(width, dtype=jnp.int32) // (width // heads)
    part_of = jnp.arange(16, dtype=jnp.int32)
    heads_map = (
        ((part_of % heads)[:, None] == head_of[None, :]) & (part_of < 2 * heads)[:, None]
    ).astype(BF16)
    lane = jnp.arange(LANES, dtype=jnp.int32)
    picks = [
        (lane[:, None] == (m * state_size + lane // SUB)[None, :]).astype(BF16) for m in range(4, 8)
    ]
    pick_b = jnp.stack([picks[0].T, picks[2].T])
    pick_c = jnp.stack([picks[1], picks[3]])

    got = got.reshape(owners * slots, sent.shape[2])
    ready = (into_row, out_row, into_col, out_col, half_row, half_col, heads_map, pick_b, pick_c, spot)
    got, ready = lax.optimization_barrier((got, ready))
    into_row, out_row, into_col, out_col, half_row, half_col, heads_map, pick_b, pick_c, spot = ready
    cells = got[:, channels].astype(jnp.int32) * 64 + got[:, channels + 1].astype(jnp.int32)

    grid, inner, left_edge, right_edge = place(
        cells, got, norm_gain[None], in_x, rows_n, cols_n, channels
    )
    from_left = shifted(right_edge, "col", True).astype(BF16)
    from_right = shifted(left_edge, "col", False).astype(BF16)
    top = jnp.concatenate([inner[:cols_n], from_left[:1], from_right[:1]])
    bottom = jnp.concatenate([inner[cells_n - cols_n :], from_left[rows_n - 1 :], from_right[rows_n - 1 :]])
    above = shifted(bottom, "row", True)
    below = shifted(top, "row", False)
    left = jnp.concatenate([above[cols_n : cols_n + 1], from_left, below[cols_n : cols_n + 1]])[:, None].astype(F32)
    right = jnp.concatenate([above[cols_n + 1 :], from_right, below[cols_n + 1 :]])[:, None].astype(F32)

    x_in, coef, state_row, state_own, state_other = conv_and_states(
        spot, inner.reshape(rows_n, cols_n, width), above[:cols_n], below[:cols_n], left, right,
        conv_w.reshape(9, width), conv_bias[None], x_proj, into_row, into_col, heads_map, pick_b, half_row, half_col,
    )
    order = lax.optimization_barrier
    lines, peers = lax.axis_size("row"), lax.axis_size("col")
    chips = lines // 2
    twin = [(i, i ^ 1) for i in range(lines)]
    state_got = lax.ppermute(state_other, "row", twin)
    split_row = lax.all_to_all(state_row, "col", split_axis=0, concat_axis=0, tiled=True)
    gated = gate(grid, norm_gain[None], in_z)
    state_got, gated = order((state_got, gated))
    sends = chip_total(spot, state_own, state_got, heads_map, chips)
    receipts = [
        lax.ppermute(send, "row", [(i, (i + 2 * shift) % lines) for i in range(lines)])
        for shift, send in enumerate(sends, 1)
    ]
    x_row, sends = order((x_in, sends))
    total = inner_row(x_row, coef, into_row, out_row, heads_map, skip_gain[None])
    split_row, total = order((split_row, total))
    passed = chain(split_row, heads_map, rows_n // peers)
    enter_row = lax.all_to_all(passed, "col", split_axis=0, concat_axis=0, tiled=True)
    enter_row = enter_row.reshape(rows_n, 2, state_size, width)
    x_col, passed = order((x_in, passed))
    total_col = inner_col(x_col, coef, into_col, out_col, heads_map)
    receipts, total_col, enter_row = order((receipts, total_col, enter_row))
    enter_own, enter_other = entering_states(spot, state_own, state_got, heads_map, receipts)
    enter_other = lax.ppermute(enter_other, "row", twin)
    return finish(
        spot, total, total_col, coef, enter_row, enter_own, enter_other, out_row, out_col, heads_map, pick_c, gated, grid, out_gain[None], out_w,
        mlp_gain[None], ff_in, ff_out, channels=channels,
    )


def solution(mesh):
    spread_all = (
        P(("row", "col"), None, None, None),
        P(("row", "col"), None, None),
        P(("row", "col"), None, None),
        P(("row", "col"), None),
    )
    placed = spread_all + (P(),) * 8 + (P(None, None, "row", "col"),) + (P(),) * 5
    return jax.shard_map(
        local, mesh=mesh, in_specs=placed, out_specs=P("row", "col", None), check_vma=False
    )
```

```python
import functools
import jax
import jax.numpy as jnp
from jax import lax
from jax.experimental import pallas as pl
from jax.experimental.pallas import tpu as pltpu
from jax.sharding import PartitionSpec as P

F32 = jnp.float32
BF16 = jnp.bfloat16
BLOCK = 1024
UNROLL = 4
TOGETHER = 4
LAST_UNROLL = 1
LANES = 128
SUB = 8
VMEM_BYTES = 40 * 1024 * 1024


def whole():
    return pl.BlockSpec(memory_space=pltpu.VMEM)


KERNEL_US = dict(
    place_norm_project=12, gate=6, conv_states=31, row_scan=20, inner_col=16, chain=3, chip_total=5, entering=6, finish=25
)


def call(body, outs, ins, scratch=(), name=None):
    work = KERNEL_US[name] * 10**9
    return pl.pallas_call(
        body,
        cost_estimate=pl.CostEstimate(flops=work, bytes_accessed=work // 400, transcendentals=0),
        out_shape=outs,
        in_specs=ins,
        out_specs=jax.tree.map(lambda _: whole(), outs),
        scratch_shapes=list(scratch),
        compiler_params=pltpu.CompilerParams(vmem_limit_bytes=VMEM_BYTES),
        name=name,
    )


def loop(count, step, unroll=1):
    def body(i, carry):
        for j in range(unroll):
            step(i * unroll + j)
        return carry

    lax.fori_loop(0, count // unroll, body, 0)


def dot(a, b):
    return jnp.dot(a, b, preferred_element_type=F32)


def dot_nt(a, b):
    return lax.dot_general(a, b, (((1,), (1,)), ((), ())), preferred_element_type=F32)


def dot_tn(a, b):
    return lax.dot_general(a, b, (((0,), (0,)), ((), ())), preferred_element_type=F32)


def silu(values):
    half = 0.5 * values
    return half + half * jnp.tanh(half)


def rms_scale(values, gains):
    return values * lax.rsqrt(jnp.mean(values * values, axis=-1, keepdims=True) + 1e-06) * gains


def two_parts(values):
    high = lax.reduce_precision(values, 8, 7)
    return high.astype(BF16), (values - high).astype(BF16)


def factor_rows(values):
    high, low = two_parts(values)
    heads = values.shape[1]
    both = jnp.concatenate([high, low], axis=1)
    return jnp.pad(both, ((0, 0), (0, 16 - 2 * heads), (0, 0), (0, 0)))


def row_layout(parts):
    return jnp.transpose(parts, (0, 2, 1, 3))


def col_layout(parts):
    k, m, r, c = parts.shape
    parts = parts.reshape(k, m, r, c // SUB, SUB)
    return jnp.transpose(parts, (0, 3, 1, 2, 4)).reshape(k, c // SUB, m, r * SUB)


def decay_factors(decay):
    rows_n, cols_n = decay.shape[2:]
    upto_c = jnp.triu(jnp.ones((cols_n, cols_n), F32))
    upto_r = jnp.triu(jnp.ones((rows_n, rows_n), F32))
    exact = lax.Precision.HIGHEST
    cum = jnp.stack(
        [
            jnp.einsum("hru,ut->hrt", decay[0], upto_c, precision=exact),
            jnp.einsum("hru,ut->hrt", decay[1], upto_c.T, precision=exact),
            jnp.einsum("huc,ut->htc", decay[2], upto_r, precision=exact),
            jnp.einsum("huc,ut->htc", decay[3], upto_r.T, precision=exact),
        ]
    )
    total_row = jnp.sum(decay[:2], axis=3)
    total_col = jnp.sum(decay[2:], axis=2)
    mid = 0.5 * jnp.concatenate(
        [
            jnp.broadcast_to(total_row[..., None], decay[:2].shape),
            jnp.broadcast_to(total_col[:, :, None, :], decay[2:].shape),
        ]
    )
    weight = jnp.sqrt(-jnp.expm1(-2.0 * decay))
    into = factor_rows(weight * jnp.exp(cum - mid))
    out = factor_rows(jnp.exp(mid - cum))
    return (
        row_layout(into[:2]),
        row_layout(out[:2]),
        col_layout(into[2:]),
        col_layout(out[2:]),
        total_row,
        total_col,
    )


def place_body(cells, got, gain, in_x, grid_out, inner_out, left_out, right_out, *scratch):
    src, dst = scratch[:2], scratch[2:]
    slots = got.shape[0]
    channels = grid_out.shape[1]
    cells_n = grid_out.shape[0]
    cols_n = cells_n // left_out.shape[0]

    def fill(i, carry):
        at = pl.ds(pl.multiple_of(i * 256, 256), 256)
        for part in dst:
            part[at, :] = jnp.zeros((256, LANES), F32)
        return carry

    lax.fori_loop(0, cells_n // 256, fill, 0)

    def widen(i, carry):
        at = pl.ds(pl.multiple_of(i * 256, 256), 256)
        for m, part in enumerate(src):
            part[at, :] = got[at, m * LANES : (m + 1) * LANES].astype(F32)
        return carry

    lax.fori_loop(0, slots // 256, widen, 0)

    def place(i, carry):
        base = i * 16
        for j in range(16):
            cell = cells[base + j]
            for from_part, to_part in zip(src, dst):
                to_part[pl.ds(cell, 1), :] = from_part[pl.ds(base + j, 1), :]
        return carry

    lax.fori_loop(0, slots // 16, place, 0)

    def project(r, carry):
        at = pl.ds(pl.multiple_of(r * cols_n, cols_n), cols_n)
        tiles = jnp.concatenate([dst[0][at, :], dst[1][at, : channels - LANES]], axis=1)
        grid_out[at, :] = tiles.astype(BF16)
        normed = rms_scale(tiles, gain[...]).astype(BF16)
        inner = dot(normed, in_x[...]).astype(BF16)
        inner_out[at, :] = inner
        wide = inner.astype(F32)
        left_out[pl.ds(r, 1), :] = wide[:1]
        right_out[pl.ds(r, 1), :] = wide[cols_n - 1 :]
        return carry

    loop(cells_n // cols_n, lambda r: project(r, 0), UNROLL)


def place(cells, got, gain, in_x, rows_n, cols_n, channels):
    cells_n = rows_n * cols_n
    width = in_x.shape[1]
    outs = (
        jax.ShapeDtypeStruct((cells_n, channels), BF16),
        jax.ShapeDtypeStruct((cells_n, width), BF16),
        jax.ShapeDtypeStruct((rows_n, width), F32),
        jax.ShapeDtypeStruct((rows_n, width), F32),
    )
    return call(
        place_body,
        outs,
        [pl.BlockSpec(memory_space=pltpu.SMEM), whole(), whole(), whole()],
        [
            pltpu.VMEM((got.shape[0], LANES), F32),
            pltpu.VMEM((got.shape[0], LANES), F32),
            pltpu.VMEM((cells_n + SUB, LANES), F32),
            pltpu.VMEM((cells_n + SUB, LANES), F32),
        ],
        name="place_norm_project",
    )(cells, got, gain, in_x)


def gate_body(grid, gain, in_z, gate_out, *, block):
    def step(i, carry):
        at = pl.ds(pl.multiple_of(i * block, block), block)
        normed = rms_scale(grid[at, :].astype(F32), gain[...]).astype(BF16)
        gate = dot(normed, in_z[...]).astype(BF16).astype(F32)
        gate_out[at, :] = silu(gate).astype(BF16)
        return carry

    lax.fori_loop(0, grid.shape[0] // block, step, 0)


def gate(grid, gain, in_z):
    return call(
        functools.partial(gate_body, block=BLOCK),
        jax.ShapeDtypeStruct((grid.shape[0], in_z.shape[1]), BF16),
        [whole()] * 3,
        name="gate",
    )(grid, gain, in_z)


def spread(parts, heads_map):
    return dot_tn(parts, heads_map)


def own_column(shape, row_mod, col_mod):
    rows = lax.broadcasted_iota(jnp.int32, shape, 0)
    cols = lax.broadcasted_iota(jnp.int32, shape, 1)
    return (rows & (row_mod - 1)) == (cols & (col_mod - 1))


def conv_body(
    spot, inner, above, below, left, right, conv_w, conv_bias, x_proj, into_row, into_col, heads_map, pick_b,
    half_row, half_col, x_out, coef_out, state_row, state_own, state_other,
    padded, x_wide, coef_wide, left_sum, right_sum,
):
    rows_n, cols_n, width = inner.shape
    state_size = LANES // 8
    peers, tile_rows = half_row.shape[:2]
    each = rows_n // peers
    for q in range(peers):
        state_row[q, 2 * each * state_size :] = half_row[q]
    padded[0] = above[...]
    padded[rows_n + 1] = below[...]

    def move(r, carry):
        padded[r + 1] = inner[r]
        return carry

    lax.fori_loop(0, rows_n, move, 0)
    for edge, column, sums in ((left, 0, left_sum), (right, 2, right_sum)):
        total = jnp.zeros((rows_n, 1, width), F32)
        for i in range(3):
            total = total + edge[i : i + rows_n] * conv_w[3 * i + column : 3 * i + column + 1, :][None]
        sums[...] = total
    first = lax.broadcasted_iota(jnp.int32, (cols_n, LANES), 0) == 0
    last = lax.broadcasted_iota(jnp.int32, (cols_n, LANES), 0) == cols_n - 1

    def row_step(r, carry):
        for part in range(width // LANES):
            lanes = slice(part * LANES, (part + 1) * LANES)
            rows = [padded[r + i, :, lanes].astype(F32) for i in range(3)]
            sums = []
            for j in range(3):
                total = rows[0] * conv_w[j : j + 1, lanes]
                total = total + rows[1] * conv_w[3 + j : 4 + j, lanes]
                sums.append(total + rows[2] * conv_w[6 + j : 7 + j, lanes])
            from_left = jnp.where(first, left_sum[r, :, lanes], pltpu.roll(sums[0], 1, 0))
            from_right = jnp.where(
                last, right_sum[r, :, lanes], pltpu.roll(sums[2], cols_n - 1, 0)
            )
            value = conv_bias[:, lanes] + from_left + sums[1] + from_right
            scanned = silu(value).astype(BF16)
            x_out[r, :, lanes] = scanned
            x_wide[r, :, lanes] = scanned.astype(F32)
        coef = dot(x_out[r], x_proj[...]).astype(BF16)
        coef_out[r] = coef
        coef_wide[r] = coef.astype(F32)
        flipped = coef.T
        for k in range(2):
            scaled = (x_wide[r] * spread(into_row[k, r], heads_map[...])).astype(BF16)
            b_part = flipped[2 * k * state_size : (2 * k + 1) * state_size, :]
            at = pl.multiple_of((r % each) * 2 * state_size + k * state_size, state_size)
            state_row[r // each, pl.ds(at, state_size), :] = dot(b_part, scaled).astype(BF16)
        return carry

    loop(rows_n, lambda r: row_step(r, 0), UNROLL)
    size = rows_n * SUB
    own = own_column((LANES, size), SUB, SUB)

    half = state_own.shape[0]
    deep = SUB * state_size

    def col_step(j):
        for states, side in ((state_own, spot[0]), (state_other, 1 - spot[0])):
            g = side * half + j
            at = pl.ds(pl.multiple_of(g * SUB, SUB), SUB)
            x_group = x_wide[:, at, :].reshape(size, width)
            coef = coef_wide[:, at, :].reshape(size, LANES).astype(BF16)
            for k in range(2):
                scaled = (x_group * spread(into_col[k, g], heads_map[...])).astype(BF16)
                b_part = jnp.where(own, dot_nt(pick_b[k], coef), 0.0).astype(BF16)
                states[j, k * deep : (k + 1) * deep, :] = dot(b_part, scaled).astype(BF16)
            states[j, 2 * deep :, :] = half_col[g]

    loop(half, col_step, UNROLL // 2)


def conv_and_states(spot, inner, *rest):
    rows_n, cols_n, width = inner.shape
    half_row, half_col = rest[-2:]
    peers, tile_rows = half_row.shape[:2]
    groups, deep = half_col.shape[0] // 2, 2 * SUB * (LANES // 8) + half_col.shape[1]
    outs = (
        jax.ShapeDtypeStruct((rows_n, cols_n, width), BF16),
        jax.ShapeDtypeStruct((rows_n, cols_n, LANES), BF16),
        jax.ShapeDtypeStruct((peers, rows_n // peers * 2 * (LANES // 8) + tile_rows, width), BF16),
        jax.ShapeDtypeStruct((groups, deep, width), BF16),
        jax.ShapeDtypeStruct((groups, deep, width), BF16),
    )
    return call(
        conv_body,
        outs,
        [pl.BlockSpec(memory_space=pltpu.SMEM)] + [whole()] * 14,
        [
            pltpu.VMEM((rows_n + 2, cols_n, width), BF16),
            pltpu.VMEM((rows_n, cols_n, width), F32),
            pltpu.VMEM((rows_n, cols_n, LANES), F32),
            pltpu.VMEM((rows_n, 1, width), F32),
            pltpu.VMEM((rows_n, 1, width), F32),
        ],
        name="conv_states",
    )(spot, inner, *rest)


def c_at_b(wide, k):
    state_size = LANES // 8
    lane = lax.broadcasted_iota(jnp.int32, (1, LANES), 1)
    rolled = pltpu.roll(wide, LANES - state_size, 1)
    return jnp.where((lane // state_size) == 2 * k, rolled, 0.0).astype(BF16)


def row_scan_body(x_in, coef_in, enter_row, into_row, out_row, heads_map, skip, total_out):
    rows_n, cols_n, width = x_in.shape
    t_row = lax.broadcasted_iota(jnp.int32, (cols_n, cols_n), 0)
    u_row = lax.broadcasted_iota(jnp.int32, (cols_n, cols_n), 1)
    masks = (t_row >= u_row, t_row <= u_row)

    state_size = LANES // 8

    def row_step(r):
        x_row = x_in[r].astype(F32)
        coef = coef_in[r]
        wide = coef.astype(F32)
        total = x_row * skip[...]
        for k in range(2):
            scores = dot_nt(c_at_b(wide, k), coef)
            mixing = jnp.where(masks[k], scores, 0.0).astype(BF16)
            c_part = coef[:, (2 * k + 1) * state_size : (2 * k + 2) * state_size]
            scaled = (x_row * spread(into_row[k, r], heads_map[...])).astype(BF16)
            both = dot(
                jnp.concatenate([mixing, c_part], axis=1),
                jnp.concatenate([scaled, enter_row[r, k]], axis=0),
            )
            total = total + both * spread(out_row[k, r], heads_map[...])
        total_out[r] = total.astype(BF16)

    loop(rows_n, row_step, UNROLL)


def row_scan(x_in, *rest):
    return call(
        row_scan_body, jax.ShapeDtypeStruct(x_in.shape, BF16), [whole()] * 7, name="row_scan"
    )(x_in, *rest)


def inner_col_body(x_in, coef_in, into_col, out_col, heads_map, total_out, x_wide, coef_wide, acc):
    rows_n, cols_n, width = x_in.shape

    def widen(r):
        x_wide[r] = x_in[r].astype(F32)
        coef_wide[r] = coef_in[r].astype(F32)

    loop(rows_n, widen, UNROLL)
    size = rows_n * SUB
    t_col = lax.broadcasted_iota(jnp.int32, (size, size), 0)
    u_col = lax.broadcasted_iota(jnp.int32, (size, size), 1)
    same = (t_col & (SUB - 1)) == (u_col & (SUB - 1))
    masks = (same & (t_col >= u_col), same & (t_col <= u_col))

    def col_step(g):
        at = pl.ds(pl.multiple_of(g * SUB, SUB), SUB)
        x_group = x_wide[:, at, :].reshape(size, width)
        wide = coef_wide[:, at, :].reshape(size, LANES)
        coef = wide.astype(BF16)
        total = jnp.zeros((size, width), F32)
        for k in range(2):
            scores = dot_nt(c_at_b(wide, k + 2), coef)
            mixing = jnp.where(masks[k], scores, 0.0).astype(BF16)
            scaled = (x_group * spread(into_col[k, g], heads_map[...])).astype(BF16)
            total = total + dot(mixing, scaled) * spread(out_col[k, g], heads_map[...])
        acc[:, at, :] = total.reshape(rows_n, SUB, width)

    loop(cols_n // SUB, col_step, UNROLL)

    def emit(r):
        total_out[r] = acc[r].astype(BF16)

    loop(rows_n, emit, UNROLL)


def inner_col(x_in, coef_in, into_col, out_col, heads_map):
    return call(
        inner_col_body,
        jax.ShapeDtypeStruct(x_in.shape, BF16),
        [whole()] * 5,
        [
            pltpu.VMEM(x_in.shape, F32),
            pltpu.VMEM(coef_in.shape, F32),
            pltpu.VMEM(x_in.shape, F32),
        ],
        name="inner_col",
    )(x_in, coef_in, into_col, out_col, heads_map)


def half_of(tile, k, heads_map):
    return dot(tile[:, 16 * k : 16 * k + 16], heads_map)


def chain_body(states, heads_map, entering):
    peers = states.shape[0]
    state_size = LANES // 8
    width = states.shape[2]
    lines = entering.shape[1] // (2 * state_size)
    top = 2 * lines * state_size
    for k in range(2):
        order = range(peers) if k == 0 else range(peers - 1, -1, -1)
        before = [jnp.zeros((state_size, width), F32)] * lines
        for at in order:
            scale = half_of(states[at, top:, :LANES], k, heads_map[...])
            for line in range(lines):
                rows = slice((2 * line + k) * state_size, (2 * line + k + 1) * state_size)
                own = scale[line : line + 1]
                entering[at, rows, :] = (own * before[line]).astype(BF16)
                before[line] = own * (own * before[line] + states[at, rows, :].astype(F32))


def chain(states, heads_map, lines):
    peers, _, width = states.shape
    return call(
        chain_body,
        jax.ShapeDtypeStruct((peers, lines * 2 * (LANES // 8), width), BF16),
        [whole()] * 2,
        name="chain",
    )(states, heads_map)


def pair_halves(upper, lower, j, top, heads_map):
    low_rows = pltpu.roll(lower[j, top:, :LANES].astype(F32), SUB, 0)
    first = lax.broadcasted_iota(jnp.int32, low_rows.shape, 0) < SUB
    tile = jnp.where(first, upper[j, top:, :LANES].astype(F32), low_rows).astype(BF16)
    halves = []
    for k in range(2):
        both = half_of(tile, k, heads_map)
        halves.append((both[:SUB], both[SUB:]))
    return tile, halves


def lines_of(states, j, k, lines_shape):
    deep = lines_shape[0] * lines_shape[1]
    return states[j, k * deep : (k + 1) * deep, :].astype(F32).reshape(lines_shape)


def by_core(spot, run, own, got):
    @pl.when(spot[0] == 0)
    def _():
        run(own, got)

    @pl.when(spot[0] != 0)
    def _():
        run(got, own)


def chip_total_body(spot, own, got, heads_map, *sends):
    groups, rows, width = own.shape
    state_size = LANES // 8
    deep = SUB * state_size
    shape = (state_size, SUB, width)
    chips = len(sends) + 1

    def run(upper, lower):
        def step(j):
            tile, halves = pair_halves(upper, lower, j, 2 * deep, heads_map[...])
            (up_2, low_2), (up_3, low_3) = halves
            down = (low_2 * low_2 * up_2) * lines_of(upper, j, 0, shape) + low_2 * lines_of(lower, j, 0, shape)
            rise = (up_3 * up_3 * low_3) * lines_of(lower, j, 1, shape) + up_3 * lines_of(upper, j, 1, shape)
            for shift, send in enumerate(sends, 1):
                past_end = spot[1] + shift >= chips
                send[j, :deep, :] = jnp.where(past_end, rise, down).reshape(deep, width).astype(BF16)
                send[j, deep:, :] = jnp.zeros((rows - 2 * deep, width), BF16)
                send[j, deep:, :LANES] = tile

        loop(groups, step, 4)

    by_core(spot, run, own, got)


def chip_total(spot, own, got, heads_map, chips):
    groups, rows, width = own.shape
    send = jax.ShapeDtypeStruct((groups, rows - SUB * (LANES // 8), width), BF16)
    return call(
        chip_total_body,
        (send,) * (chips - 1),
        [pl.BlockSpec(memory_space=pltpu.SMEM)] + [whole()] * 3,
        name="chip_total",
    )(spot, own, got, heads_map)


def entering_body(spot, own, got, heads_map, *rest):
    receipts, (enter_own, enter_other) = rest[:-2], rest[-2:]
    groups, rows, width = own.shape
    state_size = LANES // 8
    deep = SUB * state_size
    shape = (state_size, SUB, width)
    chips = len(receipts) + 1

    def run(upper, lower, enter_upper, enter_lower):
        def step(j):
            _, halves = pair_halves(upper, lower, j, 2 * deep, heads_map[...])
            (up_2, low_2), (up_3, low_3) = halves
            states = [lines_of(receipt, j, 0, shape) for receipt in receipts]
            keeps = []
            for k in range(2):
                keep = []
                for receipt in receipts:
                    both = half_of(receipt[j, deep:, :LANES], k, heads_map[...])
                    chip = both[:SUB] * both[SUB:]
                    keep.append(chip * chip)
                keeps.append(keep)
            down = jnp.zeros(shape, F32)
            rise = jnp.zeros(shape, F32)
            keep_2 = jnp.ones((SUB, width), F32)
            keep_3 = jnp.ones((SUB, width), F32)
            for away in range(1, chips):
                above, below = away - 1, chips - away - 1
                down = down + jnp.where(spot[1] >= away, keep_2, 0.0) * states[above]
                rise = rise + jnp.where(spot[1] + away < chips, keep_3, 0.0) * states[below]
                keep_2 = keep_2 * keeps[0][above]
                keep_3 = keep_3 * keeps[1][below]
            lower_2 = low_2 * up_2 * (up_2 * down + lines_of(upper, j, 0, shape))
            upper_3 = up_3 * low_3 * (low_3 * rise + lines_of(lower, j, 1, shape))
            enter_upper[j, 0] = (up_2 * down).reshape(deep, width).astype(BF16)
            enter_upper[j, 1] = upper_3.reshape(deep, width).astype(BF16)
            enter_lower[j, 0] = lower_2.reshape(deep, width).astype(BF16)
            enter_lower[j, 1] = (low_3 * rise).reshape(deep, width).astype(BF16)

        loop(groups, step, 4)

    @pl.when(spot[0] == 0)
    def _():
        run(own, got, enter_own, enter_other)

    @pl.when(spot[0] != 0)
    def _():
        run(got, own, enter_other, enter_own)


def entering_states(spot, own, got, heads_map, receipts):
    groups, rows, width = own.shape
    enter = jax.ShapeDtypeStruct((groups, 2, SUB * (LANES // 8), width), BF16)
    return call(
        entering_body,
        (enter, enter),
        [pl.BlockSpec(memory_space=pltpu.SMEM)] + [whole()] * (3 + len(receipts)),
        name="entering",
    )(spot, own, got, heads_map, *receipts)


def half_tiles(total, units):
    k, heads, lines = total.shape
    high, low = two_parts(jnp.exp(-0.5 * total))
    both = jnp.pad(jnp.concatenate([high, low], axis=1), ((0, 0), (0, 16 - 2 * heads), (0, 0)))
    both = jnp.transpose(both, (2, 0, 1)).reshape(units, lines // units, k * 16)
    rows = -(-both.shape[1] // 16) * 16
    return jnp.pad(both, ((0, 0), (0, rows - both.shape[1]), (0, 0)))


def finish_body(
    spot, total_row, total_col, coef_in, enter_own, enter_other, out_col, heads_map, pick_c, gate_in, grid,
    out_gain, out_w, mlp_gain, ff_in, ff_out, block_out, coef_wide, acc,
):
    rows_n, cols_n, width = total_row.shape
    half = enter_own.shape[0]

    def widen(r):
        coef_wide[r] = coef_in[r].astype(F32)
        acc[r] = total_row[r].astype(F32) + total_col[r].astype(F32)

    loop(rows_n, widen, UNROLL)
    size = rows_n * SUB
    own = own_column((size, LANES), SUB, SUB)

    def col_step(j):
        for enter, side in ((enter_own, spot[0]), (enter_other, 1 - spot[0])):
            g = side * half + j
            at = pl.ds(pl.multiple_of(g * SUB, SUB), SUB)
            coef = coef_wide[:, at, :].reshape(size, LANES).astype(BF16)
            value = acc[:, at, :].reshape(size, width)
            for k in range(2):
                c_part = jnp.where(own, dot(coef, pick_c[k]), 0.0).astype(BF16)
                value = value + dot(c_part, enter[j, k]) * spread(out_col[k, g], heads_map[...])
            acc[:, at, :] = value.reshape(rows_n, SUB, width)

    loop(half, col_step, UNROLL // 2)
    deep = TOGETHER * cols_n

    def last(i):
        at = pl.ds(pl.multiple_of(i * deep, deep), deep)
        value = acc[pl.ds(i * TOGETHER, TOGETHER)].reshape(deep, width)
        gated = (rms_scale(value, out_gain[...]) * gate_in[at, :].astype(F32)).astype(BF16)
        middle = (dot_nt(gated, out_w[...]) + grid[at, :].astype(F32)).astype(BF16)
        wide = middle.astype(F32)
        normed = rms_scale(wide, mlp_gain[...]).astype(BF16)
        hidden = dot(normed, ff_in[...])
        hidden = (hidden * (0.5 + 0.5 * lax.erf(hidden * (0.5**0.5)))).astype(BF16)
        result = dot_nt(hidden, ff_out[...]) + wide
        for j in range(TOGETHER):
            block_out[i * TOGETHER + j] = result[j * cols_n : (j + 1) * cols_n].T.astype(BF16)

    loop(rows_n // TOGETHER, last, LAST_UNROLL)


def finish(spot, total, total_col, coef, *rest, channels):
    rows_n, cols_n, width = total.shape
    return call(
        finish_body,
        jax.ShapeDtypeStruct((rows_n, channels, cols_n), BF16),
        [pl.BlockSpec(memory_space=pltpu.SMEM)] + [whole()] * 15,
        [pltpu.VMEM(coef.shape, F32), pltpu.VMEM(total.shape, F32)],
        name="finish",
    )(spot, total, total_col, coef, *rest)


def shifted(block, axis, up):
    count = lax.axis_size(axis)
    pairs = [(i, i + 1) if up else (i + 1, i) for i in range(count - 1)]
    return lax.ppermute(block, axis, pairs)


def local(
    tile_feats, tile_cell, tile_mask, tile_count, background, norm_gain, in_x, in_z, conv_w, conv_bias, x_proj,
    skip_gain, decay_rate, out_gain, out_w, mlp_gain, ff_in, ff_out,
):
    heads, rows_n, cols_n = decay_rate.shape[1:]
    owners, slots, channels = tile_feats.shape[1:]
    width = in_x.shape[1]
    state_size = x_proj.shape[1] // 8
    cells_n = rows_n * cols_n

    values = jnp.where(tile_mask[0][..., None] == 1, tile_feats[0], background)
    live = jnp.arange(slots, dtype=jnp.int32)[None, :] < tile_count[0][:, None]
    marked = jnp.where(live, tile_cell[0], cells_n)
    where = jnp.stack([marked // 64, marked % 64], axis=-1).astype(BF16)
    where = jnp.pad(where, ((0, 0), (0, 0), (0, 62)))
    sent = jnp.concatenate([values, where], axis=-1)
    got = lax.all_to_all(sent, ("row", "col"), split_axis=0, concat_axis=0, tiled=True)
    into_row, out_row, into_col, out_col, total_row, total_col = decay_factors(decay_rate)
    half_row = half_tiles(total_row, lax.axis_size("col"))
    half_col = half_tiles(total_col, cols_n // SUB)
    half_row = jnp.pad(half_row, ((0, 0), (0, 0), (0, width - half_row.shape[2])))
    half_col = jnp.pad(half_col, ((0, 0), (0, 0), (0, width - half_col.shape[2])))
    line = lax.axis_index("row")
    spot = jnp.stack([line % 2, line // 2]).astype(jnp.int32)
    head_of = jnp.arange(width, dtype=jnp.int32) // (width // heads)
    part_of = jnp.arange(16, dtype=jnp.int32)
    heads_map = (
        ((part_of % heads)[:, None] == head_of[None, :]) & (part_of < 2 * heads)[:, None]
    ).astype(BF16)
    lane = jnp.arange(LANES, dtype=jnp.int32)
    picks = [
        (lane[:, None] == (m * state_size + lane // SUB)[None, :]).astype(BF16) for m in range(4, 8)
    ]
    pick_b = jnp.stack([picks[0].T, picks[2].T])
    pick_c = jnp.stack([picks[1], picks[3]])

    got = got.reshape(owners * slots, sent.shape[2])
    ready = (into_row, out_row, into_col, out_col, half_row, half_col, heads_map, pick_b, pick_c, spot)
    got, ready = lax.optimization_barrier((got, ready))
    into_row, out_row, into_col, out_col, half_row, half_col, heads_map, pick_b, pick_c, spot = ready
    cells = got[:, channels].astype(jnp.int32) * 64 + got[:, channels + 1].astype(jnp.int32)

    grid, inner, left_edge, right_edge = place(
        cells, got, norm_gain[None], in_x, rows_n, cols_n, channels
    )
    from_left = shifted(right_edge, "col", True).astype(BF16)
    from_right = shifted(left_edge, "col", False).astype(BF16)
    top = jnp.concatenate([inner[:cols_n], from_left[:1], from_right[:1]])
    bottom = jnp.concatenate([inner[cells_n - cols_n :], from_left[rows_n - 1 :], from_right[rows_n - 1 :]])
    above = shifted(bottom, "row", True)
    below = shifted(top, "row", False)
    left = jnp.concatenate([above[cols_n : cols_n + 1], from_left, below[cols_n : cols_n + 1]])[:, None].astype(F32)
    right = jnp.concatenate([above[cols_n + 1 :], from_right, below[cols_n + 1 :]])[:, None].astype(F32)

    x_in, coef, state_row, state_own, state_other = conv_and_states(
        spot, inner.reshape(rows_n, cols_n, width), above[:cols_n], below[:cols_n], left, right,
        conv_w.reshape(9, width), conv_bias[None], x_proj, into_row, into_col, heads_map, pick_b, half_row, half_col,
    )
    order = lax.optimization_barrier
    lines, peers = lax.axis_size("row"), lax.axis_size("col")
    chips = lines // 2
    twin = [(i, i ^ 1) for i in range(lines)]
    state_got = lax.ppermute(state_other, "row", twin)
    split_row = lax.all_to_all(state_row, "col", split_axis=0, concat_axis=0, tiled=True)
    sends = chip_total(spot, state_own, state_got, heads_map, chips)
    receipts = [
        lax.ppermute(send, "row", [(i, (i + 2 * shift) % lines) for i in range(lines)])
        for shift, send in enumerate(sends, 1)
    ]
    x_col, sends = order((x_in, sends))
    total_col = inner_col(x_col, coef, into_col, out_col, heads_map)
    split_row, total_col = order((split_row, total_col))
    passed = chain(split_row, heads_map, rows_n // peers)
    enter_row = lax.all_to_all(passed, "col", split_axis=0, concat_axis=0, tiled=True)
    enter_row = enter_row.reshape(rows_n, 2, state_size, width)
    grid_in, passed = order((grid, passed))
    gated = gate(grid_in, norm_gain[None], in_z)
    receipts, gated = order((receipts, gated))
    enter_own, enter_other = entering_states(spot, state_own, state_got, heads_map, receipts)
    x_row, enter_own, enter_other = order((x_in, enter_own, enter_other))
    enter_other = lax.ppermute(enter_other, "row", twin)
    total = row_scan(x_row, coef, enter_row, into_row, out_row, heads_map, skip_gain[None])
    block = finish(
        spot, total, total_col, coef, enter_own, enter_other, out_col, heads_map, pick_c, gated, grid,
        out_gain[None], out_w.T, mlp_gain[None], ff_in, ff_out.T, channels=channels,
    )
    return jnp.swapaxes(block, 1, 2)


def solution(mesh):
    spread_all = (
        P(("row", "col"), None, None, None),
        P(("row", "col"), None, None),
        P(("row", "col"), None, None),
        P(("row", "col"), None),
    )
    placed = spread_all + (P(),) * 8 + (P(None, None, "row", "col"),) + (P(),) * 5
    return jax.shard_map(
        local, mesh=mesh, in_specs=placed, out_specs=P("row", "col", None), check_vma=False
    )
```

```python
import functools
import jax
import jax.numpy as jnp
from jax import lax
from jax.experimental import pallas as pl
from jax.experimental.layout import Layout, with_layout_constraint
from jax.experimental.pallas import tpu as pltpu
from jax.sharding import PartitionSpec as P

F32 = jnp.float32
BF16 = jnp.bfloat16
BLOCK = 1024
UNROLL = 4
TOGETHER = 4
LAST_UNROLL = 1
LANES = 128
SUB = 8
KERNEL_MIB = dict(
    place_norm_project=20, gate=10, conv_states=32, row_scan=16, inner_col=28, chain=8, chip_total=10, entering=13, finish=34
)


def whole():
    return pl.BlockSpec(memory_space=pltpu.VMEM)


KERNEL_US = dict(
    place_norm_project=12, gate=6, conv_states=31, row_scan=20, inner_col=16, chain=3, chip_total=5, entering=6, finish=25
)


def call(body, outs, ins, scratch=(), name=None):
    work = KERNEL_US[name] * 10**9
    return pl.pallas_call(
        body,
        cost_estimate=pl.CostEstimate(flops=work, bytes_accessed=work // 400, transcendentals=0),
        out_shape=outs,
        in_specs=ins,
        out_specs=jax.tree.map(lambda _: whole(), outs),
        scratch_shapes=list(scratch),
        compiler_params=pltpu.CompilerParams(vmem_limit_bytes=KERNEL_MIB[name] * 1024 * 1024),
        name=name,
    )


def loop(count, step, unroll=1):
    def body(i, carry):
        for j in range(unroll):
            step(i * unroll + j)
        return carry

    lax.fori_loop(0, count // unroll, body, 0)


def dot(a, b):
    return jnp.dot(a, b, preferred_element_type=F32)


def dot_nt(a, b):
    return lax.dot_general(a, b, (((1,), (1,)), ((), ())), preferred_element_type=F32)


def dot_tn(a, b):
    return lax.dot_general(a, b, (((0,), (0,)), ((), ())), preferred_element_type=F32)


def silu(values):
    half = 0.5 * values
    return half + half * jnp.tanh(half)


def rms_scale(values, gains):
    return values * lax.rsqrt(jnp.mean(values * values, axis=-1, keepdims=True) + 1e-06) * gains


def two_parts(values):
    high = lax.reduce_precision(values, 8, 7)
    return high.astype(BF16), (values - high).astype(BF16)


def factor_rows(values):
    high, low = two_parts(values)
    heads = values.shape[1]
    both = jnp.concatenate([high, low], axis=1)
    return jnp.pad(both, ((0, 0), (0, 16 - 2 * heads), (0, 0), (0, 0)))


def row_layout(parts):
    return jnp.transpose(parts, (0, 2, 1, 3))


def col_layout(parts):
    k, m, r, c = parts.shape
    parts = parts.reshape(k, m, r, c // SUB, SUB)
    parts = jnp.transpose(parts, (0, 3, 1, 2, 4)).reshape(k, c // SUB, m, r * SUB)
    return with_layout_constraint(parts, Layout(major_to_minor=(0, 1, 2, 3)))


def decay_factors(decay):
    rows_n, cols_n = decay.shape[2:]
    upto_c = jnp.triu(jnp.ones((cols_n, cols_n), F32))
    upto_r = jnp.triu(jnp.ones((rows_n, rows_n), F32))
    exact = lax.Precision.HIGHEST
    cum = jnp.stack(
        [
            jnp.einsum("hru,ut->hrt", decay[0], upto_c, precision=exact),
            jnp.einsum("hru,ut->hrt", decay[1], upto_c.T, precision=exact),
            jnp.einsum("huc,ut->htc", decay[2], upto_r, precision=exact),
            jnp.einsum("huc,ut->htc", decay[3], upto_r.T, precision=exact),
        ]
    )
    total_row = jnp.sum(decay[:2], axis=3)
    total_col = jnp.sum(decay[2:], axis=2)
    mid = 0.5 * jnp.concatenate(
        [
            jnp.broadcast_to(total_row[..., None], decay[:2].shape),
            jnp.broadcast_to(total_col[:, :, None, :], decay[2:].shape),
        ]
    )
    weight = jnp.sqrt(-jnp.expm1(-2.0 * decay))
    into = factor_rows(weight * jnp.exp(cum - mid))
    out = factor_rows(jnp.exp(mid - cum))
    return (
        row_layout(into[:2]),
        row_layout(out[:2]),
        col_layout(into[2:]),
        col_layout(out[2:]),
        total_row,
        total_col,
    )


def place_body(cells, got, gain, in_x, grid_out, inner_out, left_out, right_out, *scratch):
    src, dst = scratch[:2], scratch[2:]
    slots = got.shape[0]
    channels = grid_out.shape[1]
    cells_n = grid_out.shape[0]
    cols_n = cells_n // left_out.shape[0]

    def fill(i, carry):
        at = pl.ds(pl.multiple_of(i * 256, 256), 256)
        for part in dst:
            part[at, :] = jnp.zeros((256, LANES), F32)
        return carry

    lax.fori_loop(0, cells_n // 256, fill, 0)

    def widen(i, carry):
        at = pl.ds(pl.multiple_of(i * 256, 256), 256)
        for m, part in enumerate(src):
            part[at, :] = got[at, m * LANES : (m + 1) * LANES].astype(F32)
        return carry

    lax.fori_loop(0, slots // 256, widen, 0)

    def place(i, carry):
        base = i * 16
        for j in range(16):
            cell = cells[base + j]
            for from_part, to_part in zip(src, dst):
                to_part[pl.ds(cell, 1), :] = from_part[pl.ds(base + j, 1), :]
        return carry

    lax.fori_loop(0, slots // 16, place, 0)

    def project(r, carry):
        at = pl.ds(pl.multiple_of(r * cols_n, cols_n), cols_n)
        tiles = jnp.concatenate([dst[0][at, :], dst[1][at, : channels - LANES]], axis=1)
        grid_out[at, :] = tiles.astype(BF16)
        normed = rms_scale(tiles, gain[...]).astype(BF16)
        inner = dot(normed, in_x[...]).astype(BF16)
        inner_out[at, :] = inner
        wide = inner.astype(F32)
        left_out[pl.ds(r, 1), :] = wide[:1]
        right_out[pl.ds(r, 1), :] = wide[cols_n - 1 :]
        return carry

    loop(cells_n // cols_n, lambda r: project(r, 0), UNROLL)


def place(cells, got, gain, in_x, rows_n, cols_n, channels):
    cells_n = rows_n * cols_n
    width = in_x.shape[1]
    outs = (
        jax.ShapeDtypeStruct((cells_n, channels), BF16),
        jax.ShapeDtypeStruct((cells_n, width), BF16),
        jax.ShapeDtypeStruct((rows_n, width), F32),
        jax.ShapeDtypeStruct((rows_n, width), F32),
    )
    return call(
        place_body,
        outs,
        [pl.BlockSpec(memory_space=pltpu.SMEM), whole(), whole(), whole()],
        [
            pltpu.VMEM((got.shape[0], LANES), F32),
            pltpu.VMEM((got.shape[0], LANES), F32),
            pltpu.VMEM((cells_n + SUB, LANES), F32),
            pltpu.VMEM((cells_n + SUB, LANES), F32),
        ],
        name="place_norm_project",
    )(cells, got, gain, in_x)


def gate_body(grid, gain, in_z, gate_out, *, block):
    def step(i, carry):
        at = pl.ds(pl.multiple_of(i * block, block), block)
        normed = rms_scale(grid[at, :].astype(F32), gain[...]).astype(BF16)
        gate = dot(normed, in_z[...]).astype(BF16).astype(F32)
        gate_out[at, :] = silu(gate).astype(BF16)
        return carry

    lax.fori_loop(0, grid.shape[0] // block, step, 0)


def gate(grid, gain, in_z):
    return call(
        functools.partial(gate_body, block=BLOCK),
        jax.ShapeDtypeStruct((grid.shape[0], in_z.shape[1]), BF16),
        [whole()] * 3,
        name="gate",
    )(grid, gain, in_z)


def spread(parts, heads_map):
    return dot_tn(parts, heads_map)


def own_column(shape, row_mod, col_mod):
    rows = lax.broadcasted_iota(jnp.int32, shape, 0)
    cols = lax.broadcasted_iota(jnp.int32, shape, 1)
    return (rows & (row_mod - 1)) == (cols & (col_mod - 1))


def conv_body(
    spot, inner, above, below, left, right, conv_w, conv_bias, x_proj, into_row, into_col, heads_map, pick_b,
    half_row, half_col, x_out, coef_out, state_row, state_own, state_other,
    padded, x_wide, coef_wide, left_sum, right_sum,
):
    rows_n, cols_n, width = inner.shape
    state_size = LANES // 8
    peers, tile_rows = half_row.shape[:2]
    each = rows_n // peers
    for q in range(peers):
        state_row[q, 2 * each * state_size :] = half_row[q]
    padded[0] = above[...]
    padded[rows_n + 1] = below[...]

    def move(r, carry):
        padded[r + 1] = inner[r]
        return carry

    lax.fori_loop(0, rows_n, move, 0)
    for edge, column, sums in ((left, 0, left_sum), (right, 2, right_sum)):
        total = jnp.zeros((rows_n, 1, width), F32)
        for i in range(3):
            total = total + edge[i : i + rows_n] * conv_w[3 * i + column : 3 * i + column + 1, :][None]
        sums[...] = total
    first = lax.broadcasted_iota(jnp.int32, (cols_n, LANES), 0) == 0
    last = lax.broadcasted_iota(jnp.int32, (cols_n, LANES), 0) == cols_n - 1

    def row_step(r, carry):
        for part in range(width // LANES):
            lanes = slice(part * LANES, (part + 1) * LANES)
            rows = [padded[r + i, :, lanes].astype(F32) for i in range(3)]
            sums = []
            for j in range(3):
                total = rows[0] * conv_w[j : j + 1, lanes]
                total = total + rows[1] * conv_w[3 + j : 4 + j, lanes]
                sums.append(total + rows[2] * conv_w[6 + j : 7 + j, lanes])
            from_left = jnp.where(first, left_sum[r, :, lanes], pltpu.roll(sums[0], 1, 0))
            from_right = jnp.where(
                last, right_sum[r, :, lanes], pltpu.roll(sums[2], cols_n - 1, 0)
            )
            value = conv_bias[:, lanes] + from_left + sums[1] + from_right
            scanned = silu(value).astype(BF16)
            x_out[r, :, lanes] = scanned
            x_wide[r, :, lanes] = scanned.astype(F32)
        coef = dot(x_out[r], x_proj[...]).astype(BF16)
        coef_out[r] = coef
        coef_wide[r] = coef.astype(F32)
        flipped = coef.T
        for k in range(2):
            scaled = (x_wide[r] * spread(into_row[k, r], heads_map[...])).astype(BF16)
            b_part = flipped[2 * k * state_size : (2 * k + 1) * state_size, :]
            at = pl.multiple_of((r % each) * 2 * state_size + k * state_size, state_size)
            state_row[r // each, pl.ds(at, state_size), :] = dot(b_part, scaled).astype(BF16)
        return carry

    loop(rows_n, lambda r: row_step(r, 0), UNROLL)
    size = rows_n * SUB
    own = own_column((LANES, size), SUB, SUB)

    half = state_own.shape[0]
    deep = SUB * state_size

    def col_step(j):
        for states, side in ((state_own, spot[0]), (state_other, 1 - spot[0])):
            g = side * half + j
            at = pl.ds(pl.multiple_of(g * SUB, SUB), SUB)
            x_group = x_wide[:, at, :].reshape(size, width)
            coef = coef_wide[:, at, :].reshape(size, LANES).astype(BF16)
            for k in range(2):
                scaled = (x_group * spread(into_col[k, g], heads_map[...])).astype(BF16)
                b_part = jnp.where(own, dot_nt(pick_b[k], coef), 0.0).astype(BF16)
                states[j, k * deep : (k + 1) * deep, :] = dot(b_part, scaled).astype(BF16)
            states[j, 2 * deep :, :] = half_col[g]

    loop(half, col_step, UNROLL // 2)


def conv_and_states(spot, inner, *rest):
    rows_n, cols_n, width = inner.shape
    half_row, half_col = rest[-2:]
    peers, tile_rows = half_row.shape[:2]
    groups, deep = half_col.shape[0] // 2, 2 * SUB * (LANES // 8) + half_col.shape[1]
    outs = (
        jax.ShapeDtypeStruct((rows_n, cols_n, width), BF16),
        jax.ShapeDtypeStruct((rows_n, cols_n, LANES), BF16),
        jax.ShapeDtypeStruct((peers, rows_n // peers * 2 * (LANES // 8) + tile_rows, width), BF16),
        jax.ShapeDtypeStruct((groups, deep, width), BF16),
        jax.ShapeDtypeStruct((groups, deep, width), BF16),
    )
    return call(
        conv_body,
        outs,
        [pl.BlockSpec(memory_space=pltpu.SMEM)] + [whole()] * 14,
        [
            pltpu.VMEM((rows_n + 2, cols_n, width), BF16),
            pltpu.VMEM((rows_n, cols_n, width), F32),
            pltpu.VMEM((rows_n, cols_n, LANES), F32),
            pltpu.VMEM((rows_n, 1, width), F32),
            pltpu.VMEM((rows_n, 1, width), F32),
        ],
        name="conv_states",
    )(spot, inner, *rest)


def c_at_b(wide, k):
    state_size = LANES // 8
    lane = lax.broadcasted_iota(jnp.int32, (1, LANES), 1)
    rolled = pltpu.roll(wide, LANES - state_size, 1)
    return jnp.where((lane // state_size) == 2 * k, rolled, 0.0).astype(BF16)


def row_scan_body(x_in, coef_in, enter_row, into_row, out_row, heads_map, skip, total_out):
    rows_n, cols_n, width = x_in.shape
    t_row = lax.broadcasted_iota(jnp.int32, (cols_n, cols_n), 0)
    u_row = lax.broadcasted_iota(jnp.int32, (cols_n, cols_n), 1)
    masks = (t_row >= u_row, t_row <= u_row)

    state_size = LANES // 8

    def row_step(r):
        x_row = x_in[r].astype(F32)
        coef = coef_in[r]
        wide = coef.astype(F32)
        total = x_row * skip[...]
        for k in range(2):
            scores = dot_nt(c_at_b(wide, k), coef)
            mixing = jnp.where(masks[k], scores, 0.0).astype(BF16)
            c_part = coef[:, (2 * k + 1) * state_size : (2 * k + 2) * state_size]
            scaled = (x_row * spread(into_row[k, r], heads_map[...])).astype(BF16)
            both = dot(
                jnp.concatenate([mixing, c_part], axis=1),
                jnp.concatenate([scaled, enter_row[r, k]], axis=0),
            )
            total = total + both * spread(out_row[k, r], heads_map[...])
        total_out[r] = total.astype(BF16)

    loop(rows_n, row_step, UNROLL)


def row_scan(x_in, *rest):
    return call(
        row_scan_body, jax.ShapeDtypeStruct(x_in.shape, BF16), [whole()] * 7, name="row_scan"
    )(x_in, *rest)


def inner_col_body(x_in, coef_in, into_col, out_col, heads_map, total_out, x_wide, coef_wide, acc):
    rows_n, cols_n, width = x_in.shape

    def widen(r):
        x_wide[r] = x_in[r].astype(F32)
        coef_wide[r] = coef_in[r].astype(F32)

    loop(rows_n, widen, UNROLL)
    size = rows_n * SUB
    t_col = lax.broadcasted_iota(jnp.int32, (size, size), 0)
    u_col = lax.broadcasted_iota(jnp.int32, (size, size), 1)
    same = (t_col & (SUB - 1)) == (u_col & (SUB - 1))
    masks = (same & (t_col >= u_col), same & (t_col <= u_col))

    def col_step(g):
        at = pl.ds(pl.multiple_of(g * SUB, SUB), SUB)
        x_group = x_wide[:, at, :].reshape(size, width)
        wide = coef_wide[:, at, :].reshape(size, LANES)
        coef = wide.astype(BF16)
        total = jnp.zeros((size, width), F32)
        for k in range(2):
            scores = dot_nt(c_at_b(wide, k + 2), coef)
            mixing = jnp.where(masks[k], scores, 0.0).astype(BF16)
            scaled = (x_group * spread(into_col[k, g], heads_map[...])).astype(BF16)
            total = total + dot(mixing, scaled) * spread(out_col[k, g], heads_map[...])
        acc[:, at, :] = total.reshape(rows_n, SUB, width)

    loop(cols_n // SUB, col_step, UNROLL)

    def emit(r):
        total_out[r] = acc[r].astype(BF16)

    loop(rows_n, emit, UNROLL)


def inner_col(x_in, coef_in, into_col, out_col, heads_map):
    return call(
        inner_col_body,
        jax.ShapeDtypeStruct(x_in.shape, BF16),
        [whole()] * 5,
        [
            pltpu.VMEM(x_in.shape, F32),
            pltpu.VMEM(coef_in.shape, F32),
            pltpu.VMEM(x_in.shape, F32),
        ],
        name="inner_col",
    )(x_in, coef_in, into_col, out_col, heads_map)


def half_of(tile, k, heads_map):
    return dot(tile[:, 16 * k : 16 * k + 16], heads_map)


def chain_body(states, heads_map, entering):
    peers = states.shape[0]
    state_size = LANES // 8
    width = states.shape[2]
    lines = entering.shape[1] // (2 * state_size)
    top = 2 * lines * state_size
    for k in range(2):
        order = range(peers) if k == 0 else range(peers - 1, -1, -1)
        before = [jnp.zeros((state_size, width), F32)] * lines
        for at in order:
            scale = half_of(states[at, top:, :LANES], k, heads_map[...])
            for line in range(lines):
                rows = slice((2 * line + k) * state_size, (2 * line + k + 1) * state_size)
                own = scale[line : line + 1]
                entering[at, rows, :] = (own * before[line]).astype(BF16)
                before[line] = own * (own * before[line] + states[at, rows, :].astype(F32))


def chain(states, heads_map, lines):
    peers, _, width = states.shape
    return call(
        chain_body,
        jax.ShapeDtypeStruct((peers, lines * 2 * (LANES // 8), width), BF16),
        [whole()] * 2,
        name="chain",
    )(states, heads_map)


def pair_halves(upper, lower, j, top, heads_map):
    low_rows = pltpu.roll(lower[j, top:, :LANES].astype(F32), SUB, 0)
    first = lax.broadcasted_iota(jnp.int32, low_rows.shape, 0) < SUB
    tile = jnp.where(first, upper[j, top:, :LANES].astype(F32), low_rows).astype(BF16)
    halves = []
    for k in range(2):
        both = half_of(tile, k, heads_map)
        halves.append((both[:SUB], both[SUB:]))
    return tile, halves


def lines_of(states, j, k, lines_shape):
    deep = lines_shape[0] * lines_shape[1]
    return states[j, k * deep : (k + 1) * deep, :].astype(F32).reshape(lines_shape)


def by_core(spot, run, own, got):
    @pl.when(spot[0] == 0)
    def _():
        run(own, got)

    @pl.when(spot[0] != 0)
    def _():
        run(got, own)


def chip_total_body(spot, own, got, heads_map, *sends):
    groups, rows, width = own.shape
    state_size = LANES // 8
    deep = SUB * state_size
    shape = (state_size, SUB, width)
    chips = len(sends) + 1

    def run(upper, lower):
        def step(j):
            tile, halves = pair_halves(upper, lower, j, 2 * deep, heads_map[...])
            (up_2, low_2), (up_3, low_3) = halves
            down = (low_2 * low_2 * up_2) * lines_of(upper, j, 0, shape) + low_2 * lines_of(lower, j, 0, shape)
            rise = (up_3 * up_3 * low_3) * lines_of(lower, j, 1, shape) + up_3 * lines_of(upper, j, 1, shape)
            for shift, send in enumerate(sends, 1):
                past_end = spot[1] + shift >= chips
                send[j, :deep, :] = jnp.where(past_end, rise, down).reshape(deep, width).astype(BF16)
                send[j, deep:, :] = jnp.zeros((rows - 2 * deep, width), BF16)
                send[j, deep:, :LANES] = tile

        loop(groups, step, 4)

    by_core(spot, run, own, got)


def chip_total(spot, own, got, heads_map, chips):
    groups, rows, width = own.shape
    send = jax.ShapeDtypeStruct((groups, rows - SUB * (LANES // 8), width), BF16)
    return call(
        chip_total_body,
        (send,) * (chips - 1),
        [pl.BlockSpec(memory_space=pltpu.SMEM)] + [whole()] * 3,
        name="chip_total",
    )(spot, own, got, heads_map)


def entering_body(spot, own, got, heads_map, *rest):
    receipts, (enter_own, enter_other) = rest[:-2], rest[-2:]
    groups, rows, width = own.shape
    state_size = LANES // 8
    deep = SUB * state_size
    shape = (state_size, SUB, width)
    chips = len(receipts) + 1

    def run(upper, lower, enter_upper, enter_lower):
        def step(j):
            _, halves = pair_halves(upper, lower, j, 2 * deep, heads_map[...])
            (up_2, low_2), (up_3, low_3) = halves
            states = [lines_of(receipt, j, 0, shape) for receipt in receipts]
            keeps = []
            for k in range(2):
                keep = []
                for receipt in receipts:
                    both = half_of(receipt[j, deep:, :LANES], k, heads_map[...])
                    chip = both[:SUB] * both[SUB:]
                    keep.append(chip * chip)
                keeps.append(keep)
            down = jnp.zeros(shape, F32)
            rise = jnp.zeros(shape, F32)
            keep_2 = jnp.ones((SUB, width), F32)
            keep_3 = jnp.ones((SUB, width), F32)
            for away in range(1, chips):
                above, below = away - 1, chips - away - 1
                down = down + jnp.where(spot[1] >= away, keep_2, 0.0) * states[above]
                rise = rise + jnp.where(spot[1] + away < chips, keep_3, 0.0) * states[below]
                keep_2 = keep_2 * keeps[0][above]
                keep_3 = keep_3 * keeps[1][below]
            lower_2 = low_2 * up_2 * (up_2 * down + lines_of(upper, j, 0, shape))
            upper_3 = up_3 * low_3 * (low_3 * rise + lines_of(lower, j, 1, shape))
            enter_upper[j, 0] = (up_2 * down).reshape(deep, width).astype(BF16)
            enter_upper[j, 1] = upper_3.reshape(deep, width).astype(BF16)
            enter_lower[j, 0] = lower_2.reshape(deep, width).astype(BF16)
            enter_lower[j, 1] = (low_3 * rise).reshape(deep, width).astype(BF16)

        loop(groups, step, 4)

    @pl.when(spot[0] == 0)
    def _():
        run(own, got, enter_own, enter_other)

    @pl.when(spot[0] != 0)
    def _():
        run(got, own, enter_other, enter_own)


def entering_states(spot, own, got, heads_map, receipts):
    groups, rows, width = own.shape
    enter = jax.ShapeDtypeStruct((groups, 2, SUB * (LANES // 8), width), BF16)
    return call(
        entering_body,
        (enter, enter),
        [pl.BlockSpec(memory_space=pltpu.SMEM)] + [whole()] * (3 + len(receipts)),
        name="entering",
    )(spot, own, got, heads_map, *receipts)


def half_tiles(total, units):
    k, heads, lines = total.shape
    high, low = two_parts(jnp.exp(-0.5 * total))
    both = jnp.pad(jnp.concatenate([high, low], axis=1), ((0, 0), (0, 16 - 2 * heads), (0, 0)))
    both = jnp.transpose(both, (2, 0, 1)).reshape(units, lines // units, k * 16)
    rows = -(-both.shape[1] // 16) * 16
    return jnp.pad(both, ((0, 0), (0, rows - both.shape[1]), (0, 0)))


def finish_body(
    spot, total_row, total_col, coef_in, enter_own, enter_other, out_col, heads_map, pick_c, gate_in, grid,
    out_gain, out_w, mlp_gain, ff_in, ff_out, block_out, coef_wide, acc,
):
    rows_n, cols_n, width = total_row.shape
    half = enter_own.shape[0]

    def widen(r):
        coef_wide[r] = coef_in[r].astype(F32)
        acc[r] = total_row[r].astype(F32) + total_col[r].astype(F32)

    loop(rows_n, widen, UNROLL)
    size = rows_n * SUB
    own = own_column((size, LANES), SUB, SUB)

    def col_step(j):
        for enter, side in ((enter_own, spot[0]), (enter_other, 1 - spot[0])):
            g = side * half + j
            at = pl.ds(pl.multiple_of(g * SUB, SUB), SUB)
            coef = coef_wide[:, at, :].reshape(size, LANES).astype(BF16)
            value = acc[:, at, :].reshape(size, width)
            for k in range(2):
                c_part = jnp.where(own, dot(coef, pick_c[k]), 0.0).astype(BF16)
                value = value + dot(c_part, enter[j, k]) * spread(out_col[k, g], heads_map[...])
            acc[:, at, :] = value.reshape(rows_n, SUB, width)

    loop(half, col_step, UNROLL // 2)
    deep = TOGETHER * cols_n

    def last(i):
        at = pl.ds(pl.multiple_of(i * deep, deep), deep)
        value = acc[pl.ds(i * TOGETHER, TOGETHER)].reshape(deep, width)
        gated = (rms_scale(value, out_gain[...]) * gate_in[at, :].astype(F32)).astype(BF16)
        middle = (dot_nt(gated, out_w[...]) + grid[at, :].astype(F32)).astype(BF16)
        wide = middle.astype(F32)
        normed = rms_scale(wide, mlp_gain[...]).astype(BF16)
        hidden = dot(normed, ff_in[...])
        hidden = (hidden * (0.5 + 0.5 * lax.erf(hidden * (0.5**0.5)))).astype(BF16)
        result = dot_nt(hidden, ff_out[...]) + wide
        for j in range(TOGETHER):
            block_out[i * TOGETHER + j] = result[j * cols_n : (j + 1) * cols_n].T.astype(BF16)

    loop(rows_n // TOGETHER, last, LAST_UNROLL)


def finish(spot, total, total_col, coef, *rest, channels):
    rows_n, cols_n, width = total.shape
    return call(
        finish_body,
        jax.ShapeDtypeStruct((rows_n, channels, cols_n), BF16),
        [pl.BlockSpec(memory_space=pltpu.SMEM)] + [whole()] * 15,
        [pltpu.VMEM(coef.shape, F32), pltpu.VMEM(total.shape, F32)],
        name="finish",
    )(spot, total, total_col, coef, *rest)


def shifted(block, axis, up):
    count = lax.axis_size(axis)
    pairs = [(i, i + 1) if up else (i + 1, i) for i in range(count - 1)]
    return lax.ppermute(block, axis, pairs)


def local(
    tile_feats, tile_cell, tile_mask, tile_count, background, norm_gain, in_x, in_z, conv_w, conv_bias, x_proj,
    skip_gain, decay_rate, out_gain, out_w, mlp_gain, ff_in, ff_out,
):
    heads, rows_n, cols_n = decay_rate.shape[1:]
    owners, slots, channels = tile_feats.shape[1:]
    width = in_x.shape[1]
    state_size = x_proj.shape[1] // 8
    cells_n = rows_n * cols_n

    feats = jnp.transpose(tile_feats[0], (1, 2, 0))
    values = jnp.where(tile_mask[0].T[:, None, :] == 1, feats, background[None, :, None])
    live = jnp.arange(slots, dtype=jnp.int32)[:, None] < tile_count
    marked = jnp.where(live, tile_cell[0].T, cells_n)
    where = jnp.stack([marked // 64, marked % 64], axis=1).astype(BF16)
    filler = jnp.zeros((slots, 2 * LANES - channels - 2, owners), BF16)
    sent = jnp.concatenate([values, where, filler], axis=1)
    sent = with_layout_constraint(sent, Layout(major_to_minor=(0, 1, 2)))
    sent = lax.optimization_barrier(sent)
    sent = jnp.transpose(sent, (2, 0, 1))
    got = lax.all_to_all(sent, ("row", "col"), split_axis=0, concat_axis=0, tiled=True)
    into_row, out_row, into_col, out_col, total_row, total_col = decay_factors(decay_rate)
    half_row = half_tiles(total_row, lax.axis_size("col"))
    half_col = half_tiles(total_col, cols_n // SUB)
    half_row = jnp.pad(half_row, ((0, 0), (0, 0), (0, width - half_row.shape[2])))
    half_col = jnp.pad(half_col, ((0, 0), (0, 0), (0, width - half_col.shape[2])))
    line = lax.axis_index("row")
    spot = jnp.stack([line % 2, line // 2]).astype(jnp.int32)
    head_of = jnp.arange(width, dtype=jnp.int32) // (width // heads)
    part_of = jnp.arange(16, dtype=jnp.int32)
    heads_map = (
        ((part_of % heads)[:, None] == head_of[None, :]) & (part_of < 2 * heads)[:, None]
    ).astype(BF16)
    lane = jnp.arange(LANES, dtype=jnp.int32)
    picks = [
        (lane[:, None] == (m * state_size + lane // SUB)[None, :]).astype(BF16) for m in range(4, 8)
    ]
    pick_b = jnp.stack([picks[0].T, picks[2].T])
    pick_c = jnp.stack([picks[1], picks[3]])

    got = got.reshape(owners * slots, sent.shape[2])
    ready = (into_row, out_row, into_col, out_col, half_row, half_col, heads_map, pick_b, pick_c, spot)
    got, ready = lax.optimization_barrier((got, ready))
    into_row, out_row, into_col, out_col, half_row, half_col, heads_map, pick_b, pick_c, spot = ready
    cells = got[:, channels].astype(jnp.int32) * 64 + got[:, channels + 1].astype(jnp.int32)

    grid, inner, left_edge, right_edge = place(
        cells, got, norm_gain[None], in_x, rows_n, cols_n, channels
    )
    from_left = shifted(right_edge, "col", True).astype(BF16)
    from_right = shifted(left_edge, "col", False).astype(BF16)
    top = jnp.concatenate([inner[:cols_n], from_left[:1], from_right[:1]])
    bottom = jnp.concatenate([inner[cells_n - cols_n :], from_left[rows_n - 1 :], from_right[rows_n - 1 :]])
    above = shifted(bottom, "row", True)
    below = shifted(top, "row", False)
    left = jnp.concatenate([above[cols_n : cols_n + 1], from_left, below[cols_n : cols_n + 1]])[:, None].astype(F32)
    right = jnp.concatenate([above[cols_n + 1 :], from_right, below[cols_n + 1 :]])[:, None].astype(F32)

    x_in, coef, state_row, state_own, state_other = conv_and_states(
        spot, inner.reshape(rows_n, cols_n, width), above[:cols_n], below[:cols_n], left, right,
        conv_w.reshape(9, width), conv_bias[None], x_proj, into_row, into_col, heads_map, pick_b, half_row, half_col,
    )
    order = lax.optimization_barrier
    lines, peers = lax.axis_size("row"), lax.axis_size("col")
    chips = lines // 2
    twin = [(i, i ^ 1) for i in range(lines)]
    state_got = lax.ppermute(state_other, "row", twin)
    split_row = lax.all_to_all(state_row, "col", split_axis=0, concat_axis=0, tiled=True)
    sends = chip_total(spot, state_own, state_got, heads_map, chips)
    receipts = [
        lax.ppermute(send, "row", [(i, (i + 2 * shift) % lines) for i in range(lines)])
        for shift, send in enumerate(sends, 1)
    ]
    x_col, sends = order((x_in, sends))
    total_col = inner_col(x_col, coef, into_col, out_col, heads_map)
    split_row, total_col = order((split_row, total_col))
    passed = chain(split_row, heads_map, rows_n // peers)
    enter_row = lax.all_to_all(passed, "col", split_axis=0, concat_axis=0, tiled=True)
    enter_row = enter_row.reshape(rows_n, 2, state_size, width)
    grid_in, passed = order((grid, passed))
    gated = gate(grid_in, norm_gain[None], in_z)
    receipts, gated = order((receipts, gated))
    enter_own, enter_other = entering_states(spot, state_own, state_got, heads_map, receipts)
    x_row, enter_own, enter_other = order((x_in, enter_own, enter_other))
    enter_other = lax.ppermute(enter_other, "row", twin)
    total = row_scan(x_row, coef, enter_row, into_row, out_row, heads_map, skip_gain[None])
    block = finish(
        spot, total, total_col, coef, enter_own, enter_other, out_col, heads_map, pick_c, gated, grid,
        out_gain[None], out_w.T, mlp_gain[None], ff_in, ff_out.T, channels=channels,
    )
    return jnp.swapaxes(block, 1, 2)


def solution(mesh):
    spread_all = (
        P(("row", "col"), None, None, None),
        P(("row", "col"), None, None),
        P(("row", "col"), None, None),
        P(("row", "col"), None),
    )
    placed = spread_all + (P(),) * 8 + (P(None, None, "row", "col"),) + (P(),) * 5
    return jax.shard_map(
        local, mesh=mesh, in_specs=placed, out_specs=P("row", "col", None), check_vma=False
    )
```

```python
import functools
import jax
import jax.numpy as jnp
from jax import lax
from jax.experimental import pallas as pl
from jax.experimental.layout import Layout, with_layout_constraint
from jax.experimental.pallas import tpu as pltpu
from jax.sharding import PartitionSpec as P

F32 = jnp.float32
BF16 = jnp.bfloat16
BLOCK = 1024
UNROLL = 4
TOGETHER = 4
LAST_UNROLL = 1
LANES = 128
SUB = 8
KERNEL_MIB = dict(
    place_norm_project=20, gate=10, conv_states=32, row_scan=16, inner_col=28, chain=8, chip_total=10, entering=13, finish=34
)


def whole():
    return pl.BlockSpec(memory_space=pltpu.VMEM)


KERNEL_US = dict(
    place_norm_project=12, gate=6, conv_states=31, row_scan=20, inner_col=16, chain=3, chip_total=5, entering=6, finish=25
)


def hbm():
    return pl.BlockSpec(memory_space=pltpu.HBM)


def call(body, outs, ins, scratch=(), name=None, out_specs=None):
    work = KERNEL_US[name] * 10**9
    return pl.pallas_call(
        body,
        cost_estimate=pl.CostEstimate(flops=work, bytes_accessed=work // 400, transcendentals=0),
        out_shape=outs,
        in_specs=ins,
        out_specs=out_specs or jax.tree.map(lambda _: whole(), outs),
        scratch_shapes=list(scratch),
        compiler_params=pltpu.CompilerParams(vmem_limit_bytes=KERNEL_MIB[name] * 1024 * 1024),
        name=name,
    )


def loop(count, step, unroll=1):
    def body(i, carry):
        for j in range(unroll):
            step(i * unroll + j)
        return carry

    lax.fori_loop(0, count // unroll, body, 0)


def dot(a, b):
    return jnp.dot(a, b, preferred_element_type=F32)


def dot_nt(a, b):
    return lax.dot_general(a, b, (((1,), (1,)), ((), ())), preferred_element_type=F32)


def dot_tn(a, b):
    return lax.dot_general(a, b, (((0,), (0,)), ((), ())), preferred_element_type=F32)


def silu(values):
    half = 0.5 * values
    return half + half * jnp.tanh(half)


def rms_scale(values, gains):
    return values * lax.rsqrt(jnp.mean(values * values, axis=-1, keepdims=True) + 1e-06) * gains


def two_parts(values):
    high = lax.reduce_precision(values, 8, 7)
    return high.astype(BF16), (values - high).astype(BF16)


def factor_rows(values):
    high, low = two_parts(values)
    heads = values.shape[1]
    both = jnp.concatenate([high, low], axis=1)
    return jnp.pad(both, ((0, 0), (0, 16 - 2 * heads), (0, 0), (0, 0)))


def row_layout(parts):
    return jnp.transpose(parts, (0, 2, 1, 3))


def col_layout(parts):
    k, m, r, c = parts.shape
    parts = parts.reshape(k, m, r, c // SUB, SUB)
    parts = jnp.transpose(parts, (0, 3, 1, 2, 4)).reshape(k, c // SUB, m, r * SUB)
    return with_layout_constraint(parts, Layout(major_to_minor=(0, 1, 2, 3)))


def decay_factors(decay):
    rows_n, cols_n = decay.shape[2:]
    upto_c = jnp.triu(jnp.ones((cols_n, cols_n), F32))
    upto_r = jnp.triu(jnp.ones((rows_n, rows_n), F32))
    exact = lax.Precision.HIGHEST
    cum = jnp.stack(
        [
            jnp.einsum("hru,ut->hrt", decay[0], upto_c, precision=exact),
            jnp.einsum("hru,ut->hrt", decay[1], upto_c.T, precision=exact),
            jnp.einsum("huc,ut->htc", decay[2], upto_r, precision=exact),
            jnp.einsum("huc,ut->htc", decay[3], upto_r.T, precision=exact),
        ]
    )
    total_row = jnp.sum(decay[:2], axis=3)
    total_col = jnp.sum(decay[2:], axis=2)
    mid = 0.5 * jnp.concatenate(
        [
            jnp.broadcast_to(total_row[..., None], decay[:2].shape),
            jnp.broadcast_to(total_col[:, :, None, :], decay[2:].shape),
        ]
    )
    weight = jnp.sqrt(-jnp.expm1(-2.0 * decay))
    into = factor_rows(weight * jnp.exp(cum - mid))
    out = factor_rows(jnp.exp(mid - cum))
    return (
        row_layout(into[:2]),
        row_layout(out[:2]),
        col_layout(into[2:]),
        col_layout(out[2:]),
        total_row,
        total_col,
    )


def place_body(cells, got, gain, in_x, grid_out, inner_out, left_out, right_out, *scratch):
    src, dst = scratch[:2], scratch[2:]
    slots = got.shape[0]
    channels = grid_out.shape[1]
    cells_n = grid_out.shape[0]
    cols_n = cells_n // left_out.shape[0]

    def fill(i, carry):
        at = pl.ds(pl.multiple_of(i * 256, 256), 256)
        for part in dst:
            part[at, :] = jnp.zeros((256, LANES), F32)
        return carry

    lax.fori_loop(0, cells_n // 256, fill, 0)

    def widen(i, carry):
        at = pl.ds(pl.multiple_of(i * 256, 256), 256)
        for m, part in enumerate(src):
            part[at, :] = got[at, m * LANES : (m + 1) * LANES].astype(F32)
        return carry

    lax.fori_loop(0, slots // 256, widen, 0)

    def place(i, carry):
        base = i * 16
        for j in range(16):
            cell = cells[base + j]
            for from_part, to_part in zip(src, dst):
                to_part[pl.ds(cell, 1), :] = from_part[pl.ds(base + j, 1), :]
        return carry

    lax.fori_loop(0, slots // 16, place, 0)

    def project(r, carry):
        at = pl.ds(pl.multiple_of(r * cols_n, cols_n), cols_n)
        tiles = jnp.concatenate([dst[0][at, :], dst[1][at, : channels - LANES]], axis=1)
        grid_out[at, :] = tiles.astype(BF16)
        normed = rms_scale(tiles, gain[...]).astype(BF16)
        inner = dot(normed, in_x[...]).astype(BF16)
        inner_out[at, :] = inner
        wide = inner.astype(F32)
        left_out[pl.ds(r, 1), :] = wide[:1]
        right_out[pl.ds(r, 1), :] = wide[cols_n - 1 :]
        return carry

    loop(cells_n // cols_n, lambda r: project(r, 0), UNROLL)


def place(cells, got, gain, in_x, rows_n, cols_n, channels):
    cells_n = rows_n * cols_n
    width = in_x.shape[1]
    outs = (
        jax.ShapeDtypeStruct((cells_n, channels), BF16),
        jax.ShapeDtypeStruct((cells_n, width), BF16),
        jax.ShapeDtypeStruct((rows_n, width), F32),
        jax.ShapeDtypeStruct((rows_n, width), F32),
    )
    return call(
        place_body,
        outs,
        [pl.BlockSpec(memory_space=pltpu.SMEM), whole(), whole(), whole()],
        [
            pltpu.VMEM((got.shape[0], LANES), F32),
            pltpu.VMEM((got.shape[0], LANES), F32),
            pltpu.VMEM((cells_n + SUB, LANES), F32),
            pltpu.VMEM((cells_n + SUB, LANES), F32),
        ],
        name="place_norm_project",
    )(cells, got, gain, in_x)


def gate_body(grid, gain, in_z, gate_out, *, block):
    def step(i, carry):
        at = pl.ds(pl.multiple_of(i * block, block), block)
        normed = rms_scale(grid[at, :].astype(F32), gain[...]).astype(BF16)
        gate = dot(normed, in_z[...]).astype(BF16).astype(F32)
        gate_out[at, :] = silu(gate).astype(BF16)
        return carry

    lax.fori_loop(0, grid.shape[0] // block, step, 0)


def gate(grid, gain, in_z):
    return call(
        functools.partial(gate_body, block=BLOCK),
        jax.ShapeDtypeStruct((grid.shape[0], in_z.shape[1]), BF16),
        [whole()] * 3,
        name="gate",
    )(grid, gain, in_z)


def spread(parts, heads_map):
    return dot_tn(parts, heads_map)


def own_column(shape, row_mod, col_mod):
    rows = lax.broadcasted_iota(jnp.int32, shape, 0)
    cols = lax.broadcasted_iota(jnp.int32, shape, 1)
    return (rows & (row_mod - 1)) == (cols & (col_mod - 1))


def conv_body(
    spot, inner, above, below, left, right, conv_w, conv_bias, x_proj, into_row, into_col, heads_map, pick_b,
    half_row, half_col, x_hbm, coef_hbm, state_row, own_hbm, other_hbm,
    padded, x_wide, coef_wide, left_sum, right_sum, x_out, coef_out, state_own, state_other, done,
):
    rows_n, cols_n, width = inner.shape
    state_size = LANES // 8
    peers, tile_rows = half_row.shape[:2]
    each = rows_n // peers
    for q in range(peers):
        state_row[q, 2 * each * state_size :] = half_row[q]
    padded[0] = above[...]
    padded[rows_n + 1] = below[...]

    def move(r, carry):
        padded[r + 1] = inner[r]
        return carry

    lax.fori_loop(0, rows_n, move, 0)
    for edge, column, sums in ((left, 0, left_sum), (right, 2, right_sum)):
        total = jnp.zeros((rows_n, 1, width), F32)
        for i in range(3):
            total = total + edge[i : i + rows_n] * conv_w[3 * i + column : 3 * i + column + 1, :][None]
        sums[...] = total
    first = lax.broadcasted_iota(jnp.int32, (cols_n, LANES), 0) == 0
    last = lax.broadcasted_iota(jnp.int32, (cols_n, LANES), 0) == cols_n - 1

    def row_step(r, carry):
        for part in range(width // LANES):
            lanes = slice(part * LANES, (part + 1) * LANES)
            rows = [padded[r + i, :, lanes].astype(F32) for i in range(3)]
            sums = []
            for j in range(3):
                total = rows[0] * conv_w[j : j + 1, lanes]
                total = total + rows[1] * conv_w[3 + j : 4 + j, lanes]
                sums.append(total + rows[2] * conv_w[6 + j : 7 + j, lanes])
            from_left = jnp.where(first, left_sum[r, :, lanes], pltpu.roll(sums[0], 1, 0))
            from_right = jnp.where(
                last, right_sum[r, :, lanes], pltpu.roll(sums[2], cols_n - 1, 0)
            )
            value = conv_bias[:, lanes] + from_left + sums[1] + from_right
            scanned = silu(value).astype(BF16)
            x_out[r, :, lanes] = scanned
            x_wide[r, :, lanes] = scanned.astype(F32)
        coef = dot(x_out[r], x_proj[...]).astype(BF16)
        coef_out[r] = coef
        coef_wide[r] = coef.astype(F32)
        flipped = coef.T
        for k in range(2):
            scaled = (x_wide[r] * spread(into_row[k, r], heads_map[...])).astype(BF16)
            b_part = flipped[2 * k * state_size : (2 * k + 1) * state_size, :]
            at = pl.multiple_of((r % each) * 2 * state_size + k * state_size, state_size)
            state_row[r // each, pl.ds(at, state_size), :] = dot(b_part, scaled).astype(BF16)
        return carry

    loop(rows_n, lambda r: row_step(r, 0), UNROLL)
    size = rows_n * SUB
    own = own_column((LANES, size), SUB, SUB)

    copies = [
        pltpu.make_async_copy(held, out, done.at[m])
        for m, (held, out) in enumerate(
            ((x_out, x_hbm), (coef_out, coef_hbm), (state_other, other_hbm), (state_own, own_hbm))
        )
    ]
    copies[0].start()
    copies[1].start()
    half = state_own.shape[0]
    deep = SUB * state_size

    def column_states(states, side):
        def col_step(j):
            g = side * half + j
            at = pl.ds(pl.multiple_of(g * SUB, SUB), SUB)
            x_group = x_wide[:, at, :].reshape(size, width)
            coef = coef_wide[:, at, :].reshape(size, LANES).astype(BF16)
            for k in range(2):
                scaled = (x_group * spread(into_col[k, g], heads_map[...])).astype(BF16)
                b_part = jnp.where(own, dot_nt(pick_b[k], coef), 0.0).astype(BF16)
                states[j, k * deep : (k + 1) * deep, :] = dot(b_part, scaled).astype(BF16)
            states[j, 2 * deep :, :] = half_col[g]

        loop(half, col_step, UNROLL)

    column_states(state_other, 1 - spot[0])
    copies[2].start()
    column_states(state_own, spot[0])
    copies[3].start()
    for copy in copies:
        copy.wait()


def conv_and_states(spot, inner, *rest):
    rows_n, cols_n, width = inner.shape
    half_row, half_col = rest[-2:]
    peers, tile_rows = half_row.shape[:2]
    groups, deep = half_col.shape[0] // 2, 2 * SUB * (LANES // 8) + half_col.shape[1]
    outs = (
        jax.ShapeDtypeStruct((rows_n, cols_n, width), BF16),
        jax.ShapeDtypeStruct((rows_n, cols_n, LANES), BF16),
        jax.ShapeDtypeStruct((peers, rows_n // peers * 2 * (LANES // 8) + tile_rows, width), BF16),
        jax.ShapeDtypeStruct((groups, deep, width), BF16),
        jax.ShapeDtypeStruct((groups, deep, width), BF16),
    )
    return call(
        conv_body,
        outs,
        [pl.BlockSpec(memory_space=pltpu.SMEM)] + [whole()] * 14,
        [
            pltpu.VMEM((rows_n + 2, cols_n, width), BF16),
            pltpu.VMEM((rows_n, cols_n, width), F32),
            pltpu.VMEM((rows_n, cols_n, LANES), F32),
            pltpu.VMEM((rows_n, 1, width), F32),
            pltpu.VMEM((rows_n, 1, width), F32),
            pltpu.VMEM((rows_n, cols_n, width), BF16),
            pltpu.VMEM((rows_n, cols_n, LANES), BF16),
            pltpu.VMEM((groups, deep, width), BF16),
            pltpu.VMEM((groups, deep, width), BF16),
            pltpu.SemaphoreType.DMA((4,)),
        ],
        name="conv_states",
        out_specs=(hbm(), hbm(), whole(), hbm(), hbm()),
    )(spot, inner, *rest)


def c_at_b(wide, k):
    state_size = LANES // 8
    lane = lax.broadcasted_iota(jnp.int32, (1, LANES), 1)
    rolled = pltpu.roll(wide, LANES - state_size, 1)
    return jnp.where((lane // state_size) == 2 * k, rolled, 0.0).astype(BF16)


def row_scan_body(x_in, coef_in, enter_row, into_row, out_row, heads_map, skip, total_out):
    rows_n, cols_n, width = x_in.shape
    t_row = lax.broadcasted_iota(jnp.int32, (cols_n, cols_n), 0)
    u_row = lax.broadcasted_iota(jnp.int32, (cols_n, cols_n), 1)
    masks = (t_row >= u_row, t_row <= u_row)

    state_size = LANES // 8

    def row_step(r):
        x_row = x_in[r].astype(F32)
        coef = coef_in[r]
        wide = coef.astype(F32)
        total = x_row * skip[...]
        for k in range(2):
            scores = dot_nt(c_at_b(wide, k), coef)
            mixing = jnp.where(masks[k], scores, 0.0).astype(BF16)
            c_part = coef[:, (2 * k + 1) * state_size : (2 * k + 2) * state_size]
            scaled = (x_row * spread(into_row[k, r], heads_map[...])).astype(BF16)
            both = dot(
                jnp.concatenate([mixing, c_part], axis=1),
                jnp.concatenate([scaled, enter_row[r, k]], axis=0),
            )
            total = total + both * spread(out_row[k, r], heads_map[...])
        total_out[r] = total.astype(BF16)

    loop(rows_n, row_step, UNROLL)


def row_scan(x_in, *rest):
    return call(
        row_scan_body, jax.ShapeDtypeStruct(x_in.shape, BF16), [whole()] * 7, name="row_scan"
    )(x_in, *rest)


def inner_col_body(x_in, coef_in, into_col, out_col, heads_map, total_out, x_wide, coef_wide, acc):
    rows_n, cols_n, width = x_in.shape

    def widen(r):
        x_wide[r] = x_in[r].astype(F32)
        coef_wide[r] = coef_in[r].astype(F32)

    loop(rows_n, widen, UNROLL)
    size = rows_n * SUB
    t_col = lax.broadcasted_iota(jnp.int32, (size, size), 0)
    u_col = lax.broadcasted_iota(jnp.int32, (size, size), 1)
    same = (t_col & (SUB - 1)) == (u_col & (SUB - 1))
    masks = (same & (t_col >= u_col), same & (t_col <= u_col))

    def col_step(g):
        at = pl.ds(pl.multiple_of(g * SUB, SUB), SUB)
        x_group = x_wide[:, at, :].reshape(size, width)
        wide = coef_wide[:, at, :].reshape(size, LANES)
        coef = wide.astype(BF16)
        total = jnp.zeros((size, width), F32)
        for k in range(2):
            scores = dot_nt(c_at_b(wide, k + 2), coef)
            mixing = jnp.where(masks[k], scores, 0.0).astype(BF16)
            scaled = (x_group * spread(into_col[k, g], heads_map[...])).astype(BF16)
            total = total + dot(mixing, scaled) * spread(out_col[k, g], heads_map[...])
        acc[:, at, :] = total.reshape(rows_n, SUB, width)

    loop(cols_n // SUB, col_step, UNROLL)

    def emit(r):
        total_out[r] = acc[r].astype(BF16)

    loop(rows_n, emit, UNROLL)


def inner_col(x_in, coef_in, into_col, out_col, heads_map):
    return call(
        inner_col_body,
        jax.ShapeDtypeStruct(x_in.shape, BF16),
        [whole()] * 5,
        [
            pltpu.VMEM(x_in.shape, F32),
            pltpu.VMEM(coef_in.shape, F32),
            pltpu.VMEM(x_in.shape, F32),
        ],
        name="inner_col",
    )(x_in, coef_in, into_col, out_col, heads_map)


def half_of(tile, k, heads_map):
    return dot(tile[:, 16 * k : 16 * k + 16], heads_map)


def chain_body(states, heads_map, entering):
    peers = states.shape[0]
    state_size = LANES // 8
    width = states.shape[2]
    lines = entering.shape[1] // (2 * state_size)
    top = 2 * lines * state_size
    for k in range(2):
        order = range(peers) if k == 0 else range(peers - 1, -1, -1)
        before = [jnp.zeros((state_size, width), F32)] * lines
        for at in order:
            scale = half_of(states[at, top:, :LANES], k, heads_map[...])
            for line in range(lines):
                rows = slice((2 * line + k) * state_size, (2 * line + k + 1) * state_size)
                own = scale[line : line + 1]
                entering[at, rows, :] = (own * before[line]).astype(BF16)
                before[line] = own * (own * before[line] + states[at, rows, :].astype(F32))


def chain(states, heads_map, lines):
    peers, _, width = states.shape
    return call(
        chain_body,
        jax.ShapeDtypeStruct((peers, lines * 2 * (LANES // 8), width), BF16),
        [whole()] * 2,
        name="chain",
    )(states, heads_map)


def pair_halves(upper, lower, j, top, heads_map):
    low_rows = pltpu.roll(lower[j, top:, :LANES].astype(F32), SUB, 0)
    first = lax.broadcasted_iota(jnp.int32, low_rows.shape, 0) < SUB
    tile = jnp.where(first, upper[j, top:, :LANES].astype(F32), low_rows).astype(BF16)
    halves = []
    for k in range(2):
        both = half_of(tile, k, heads_map)
        halves.append((both[:SUB], both[SUB:]))
    return tile, halves


def lines_of(states, j, k, lines_shape):
    deep = lines_shape[0] * lines_shape[1]
    return states[j, k * deep : (k + 1) * deep, :].astype(F32).reshape(lines_shape)


def by_core(spot, run, own, got):
    @pl.when(spot[0] == 0)
    def _():
        run(own, got)

    @pl.when(spot[0] != 0)
    def _():
        run(got, own)


def chip_total_body(spot, own, got, heads_map, *sends):
    groups, rows, width = own.shape
    state_size = LANES // 8
    deep = SUB * state_size
    shape = (state_size, SUB, width)
    chips = len(sends) + 1

    def run(upper, lower):
        def step(j):
            tile, halves = pair_halves(upper, lower, j, 2 * deep, heads_map[...])
            (up_2, low_2), (up_3, low_3) = halves
            down = (low_2 * low_2 * up_2) * lines_of(upper, j, 0, shape) + low_2 * lines_of(lower, j, 0, shape)
            rise = (up_3 * up_3 * low_3) * lines_of(lower, j, 1, shape) + up_3 * lines_of(upper, j, 1, shape)
            for shift, send in enumerate(sends, 1):
                past_end = spot[1] + shift >= chips
                send[j, :deep, :] = jnp.where(past_end, rise, down).reshape(deep, width).astype(BF16)
                send[j, deep:, :] = jnp.zeros((rows - 2 * deep, width), BF16)
                send[j, deep:, :LANES] = tile

        loop(groups, step, 4)

    by_core(spot, run, own, got)


def chip_total(spot, own, got, heads_map, chips):
    groups, rows, width = own.shape
    send = jax.ShapeDtypeStruct((groups, rows - SUB * (LANES // 8), width), BF16)
    return call(
        chip_total_body,
        (send,) * (chips - 1),
        [pl.BlockSpec(memory_space=pltpu.SMEM)] + [whole()] * 3,
        name="chip_total",
    )(spot, own, got, heads_map)


def entering_body(spot, own, got, heads_map, *rest):
    receipts, (enter_own, enter_other) = rest[:-2], rest[-2:]
    groups, rows, width = own.shape
    state_size = LANES // 8
    deep = SUB * state_size
    shape = (state_size, SUB, width)
    chips = len(receipts) + 1

    def run(upper, lower, enter_upper, enter_lower):
        def step(j):
            _, halves = pair_halves(upper, lower, j, 2 * deep, heads_map[...])
            (up_2, low_2), (up_3, low_3) = halves
            states = [lines_of(receipt, j, 0, shape) for receipt in receipts]
            keeps = []
            for k in range(2):
                keep = []
                for receipt in receipts:
                    both = half_of(receipt[j, deep:, :LANES], k, heads_map[...])
                    chip = both[:SUB] * both[SUB:]
                    keep.append(chip * chip)
                keeps.append(keep)
            down = jnp.zeros(shape, F32)
            rise = jnp.zeros(shape, F32)
            keep_2 = jnp.ones((SUB, width), F32)
            keep_3 = jnp.ones((SUB, width), F32)
            for away in range(1, chips):
                above, below = away - 1, chips - away - 1
                down = down + jnp.where(spot[1] >= away, keep_2, 0.0) * states[above]
                rise = rise + jnp.where(spot[1] + away < chips, keep_3, 0.0) * states[below]
                keep_2 = keep_2 * keeps[0][above]
                keep_3 = keep_3 * keeps[1][below]
            lower_2 = low_2 * up_2 * (up_2 * down + lines_of(upper, j, 0, shape))
            upper_3 = up_3 * low_3 * (low_3 * rise + lines_of(lower, j, 1, shape))
            enter_upper[j, 0] = (up_2 * down).reshape(deep, width).astype(BF16)
            enter_upper[j, 1] = upper_3.reshape(deep, width).astype(BF16)
            enter_lower[j, 0] = lower_2.reshape(deep, width).astype(BF16)
            enter_lower[j, 1] = (low_3 * rise).reshape(deep, width).astype(BF16)

        loop(groups, step, 4)

    @pl.when(spot[0] == 0)
    def _():
        run(own, got, enter_own, enter_other)

    @pl.when(spot[0] != 0)
    def _():
        run(got, own, enter_other, enter_own)


def entering_states(spot, own, got, heads_map, receipts):
    groups, rows, width = own.shape
    enter = jax.ShapeDtypeStruct((groups, 2, SUB * (LANES // 8), width), BF16)
    return call(
        entering_body,
        (enter, enter),
        [pl.BlockSpec(memory_space=pltpu.SMEM)] + [whole()] * (3 + len(receipts)),
        name="entering",
    )(spot, own, got, heads_map, *receipts)


def half_tiles(total, units):
    k, heads, lines = total.shape
    high, low = two_parts(jnp.exp(-0.5 * total))
    both = jnp.pad(jnp.concatenate([high, low], axis=1), ((0, 0), (0, 16 - 2 * heads), (0, 0)))
    both = jnp.transpose(both, (2, 0, 1)).reshape(units, lines // units, k * 16)
    rows = -(-both.shape[1] // 16) * 16
    return jnp.pad(both, ((0, 0), (0, rows - both.shape[1]), (0, 0)))


def finish_body(
    spot, total_row, total_col, coef_in, enter_own, enter_other, out_col, heads_map, pick_c, gate_in, grid,
    out_gain, out_w, mlp_gain, ff_in, ff_out, block_out, coef_wide, acc,
):
    rows_n, cols_n, width = total_row.shape
    half = enter_own.shape[0]

    def widen(r):
        coef_wide[r] = coef_in[r].astype(F32)
        acc[r] = total_row[r].astype(F32) + total_col[r].astype(F32)

    loop(rows_n, widen, UNROLL)
    size = rows_n * SUB
    own = own_column((size, LANES), SUB, SUB)

    def col_step(j):
        for enter, side in ((enter_own, spot[0]), (enter_other, 1 - spot[0])):
            g = side * half + j
            at = pl.ds(pl.multiple_of(g * SUB, SUB), SUB)
            coef = coef_wide[:, at, :].reshape(size, LANES).astype(BF16)
            value = acc[:, at, :].reshape(size, width)
            for k in range(2):
                c_part = jnp.where(own, dot(coef, pick_c[k]), 0.0).astype(BF16)
                value = value + dot(c_part, enter[j, k]) * spread(out_col[k, g], heads_map[...])
            acc[:, at, :] = value.reshape(rows_n, SUB, width)

    loop(half, col_step, UNROLL // 2)
    deep = TOGETHER * cols_n

    def last(i):
        at = pl.ds(pl.multiple_of(i * deep, deep), deep)
        value = acc[pl.ds(i * TOGETHER, TOGETHER)].reshape(deep, width)
        gated = (rms_scale(value, out_gain[...]) * gate_in[at, :].astype(F32)).astype(BF16)
        middle = (dot_nt(gated, out_w[...]) + grid[at, :].astype(F32)).astype(BF16)
        wide = middle.astype(F32)
        normed = rms_scale(wide, mlp_gain[...]).astype(BF16)
        hidden = dot(normed, ff_in[...])
        hidden = (hidden * (0.5 + 0.5 * lax.erf(hidden * (0.5**0.5)))).astype(BF16)
        result = dot_nt(hidden, ff_out[...]) + wide
        for j in range(TOGETHER):
            block_out[i * TOGETHER + j] = result[j * cols_n : (j + 1) * cols_n].T.astype(BF16)

    loop(rows_n // TOGETHER, last, LAST_UNROLL)


def finish(spot, total, total_col, coef, *rest, channels):
    rows_n, cols_n, width = total.shape
    return call(
        finish_body,
        jax.ShapeDtypeStruct((rows_n, channels, cols_n), BF16),
        [pl.BlockSpec(memory_space=pltpu.SMEM)] + [whole()] * 15,
        [pltpu.VMEM(coef.shape, F32), pltpu.VMEM(total.shape, F32)],
        name="finish",
    )(spot, total, total_col, coef, *rest)


def shifted(block, axis, up):
    count = lax.axis_size(axis)
    pairs = [(i, i + 1) if up else (i + 1, i) for i in range(count - 1)]
    return lax.ppermute(block, axis, pairs)


def local(
    tile_feats, tile_cell, tile_mask, tile_count, background, norm_gain, in_x, in_z, conv_w, conv_bias, x_proj,
    skip_gain, decay_rate, out_gain, out_w, mlp_gain, ff_in, ff_out,
):
    heads, rows_n, cols_n = decay_rate.shape[1:]
    owners, slots, channels = tile_feats.shape[1:]
    width = in_x.shape[1]
    state_size = x_proj.shape[1] // 8
    cells_n = rows_n * cols_n

    feats = jnp.transpose(tile_feats[0], (1, 2, 0))
    values = jnp.where(tile_mask[0].T[:, None, :] == 1, feats, background[None, :, None])
    live = jnp.arange(slots, dtype=jnp.int32)[:, None] < tile_count
    marked = jnp.where(live, tile_cell[0].T, cells_n)
    where = jnp.stack([marked // 64, marked % 64], axis=1).astype(BF16)
    filler = jnp.zeros((slots, 2 * LANES - channels - 2, owners), BF16)
    sent = jnp.concatenate([values, where, filler], axis=1)
    sent = with_layout_constraint(sent, Layout(major_to_minor=(0, 1, 2)))
    sent = lax.optimization_barrier(sent)
    sent = jnp.transpose(sent, (2, 0, 1))
    got = lax.all_to_all(sent, ("row", "col"), split_axis=0, concat_axis=0, tiled=True)
    into_row, out_row, into_col, out_col, total_row, total_col = decay_factors(decay_rate)
    half_row = half_tiles(total_row, lax.axis_size("col"))
    half_col = half_tiles(total_col, cols_n // SUB)
    half_row = jnp.pad(half_row, ((0, 0), (0, 0), (0, width - half_row.shape[2])))
    half_col = jnp.pad(half_col, ((0, 0), (0, 0), (0, width - half_col.shape[2])))
    line = lax.axis_index("row")
    spot = jnp.stack([line % 2, line // 2]).astype(jnp.int32)
    head_of = jnp.arange(width, dtype=jnp.int32) // (width // heads)
    part_of = jnp.arange(16, dtype=jnp.int32)
    heads_map = (
        ((part_of % heads)[:, None] == head_of[None, :]) & (part_of < 2 * heads)[:, None]
    ).astype(BF16)
    lane = jnp.arange(LANES, dtype=jnp.int32)
    picks = [
        (lane[:, None] == (m * state_size + lane // SUB)[None, :]).astype(BF16) for m in range(4, 8)
    ]
    pick_b = jnp.stack([picks[0].T, picks[2].T])
    pick_c = jnp.stack([picks[1], picks[3]])

    got = got.reshape(owners * slots, sent.shape[2])
    ready = (into_row, out_row, into_col, out_col, half_row, half_col, heads_map, pick_b, pick_c, spot)
    got, ready = lax.optimization_barrier((got, ready))
    into_row, out_row, into_col, out_col, half_row, half_col, heads_map, pick_b, pick_c, spot = ready
    cells = got[:, channels].astype(jnp.int32) * 64 + got[:, channels + 1].astype(jnp.int32)

    grid, inner, left_edge, right_edge = place(
        cells, got, norm_gain[None], in_x, rows_n, cols_n, channels
    )
    from_left = shifted(right_edge, "col", True).astype(BF16)
    from_right = shifted(left_edge, "col", False).astype(BF16)
    top = jnp.concatenate([inner[:cols_n], from_left[:1], from_right[:1]])
    bottom = jnp.concatenate([inner[cells_n - cols_n :], from_left[rows_n - 1 :], from_right[rows_n - 1 :]])
    above = shifted(bottom, "row", True)
    below = shifted(top, "row", False)
    left = jnp.concatenate([above[cols_n : cols_n + 1], from_left, below[cols_n : cols_n + 1]])[:, None].astype(F32)
    right = jnp.concatenate([above[cols_n + 1 :], from_right, below[cols_n + 1 :]])[:, None].astype(F32)

    x_in, coef, state_row, state_own, state_other = conv_and_states(
        spot, inner.reshape(rows_n, cols_n, width), above[:cols_n], below[:cols_n], left, right,
        conv_w.reshape(9, width), conv_bias[None], x_proj, into_row, into_col, heads_map, pick_b, half_row, half_col,
    )
    order = lax.optimization_barrier
    lines, peers = lax.axis_size("row"), lax.axis_size("col")
    chips = lines // 2
    twin = [(i, i ^ 1) for i in range(lines)]
    state_got = lax.ppermute(state_other, "row", twin)
    split_row = lax.all_to_all(state_row, "col", split_axis=0, concat_axis=0, tiled=True)
    sends = chip_total(spot, state_own, state_got, heads_map, chips)
    receipts = [
        lax.ppermute(send, "row", [(i, (i + 2 * shift) % lines) for i in range(lines)])
        for shift, send in enumerate(sends, 1)
    ]
    split_row, sends = order((split_row, sends))
    passed = chain(split_row, heads_map, rows_n // peers)
    enter_row = lax.all_to_all(passed, "col", split_axis=0, concat_axis=0, tiled=True)
    enter_row = enter_row.reshape(rows_n, 2, state_size, width)
    x_col, passed = order((x_in, passed))
    total_col = inner_col(x_col, coef, into_col, out_col, heads_map)
    grid_in, total_col = order((grid, total_col))
    gated = gate(grid_in, norm_gain[None], in_z)
    x_row, gated = order((x_in, gated))
    total = row_scan(x_row, coef, enter_row, into_row, out_row, heads_map, skip_gain[None])
    receipts, total = order((receipts, total))
    enter_own, enter_other = entering_states(spot, state_own, state_got, heads_map, receipts)
    enter_other = lax.ppermute(enter_other, "row", twin)
    block = finish(
        spot, total, total_col, coef, enter_own, enter_other, out_col, heads_map, pick_c, gated, grid,
        out_gain[None], out_w.T, mlp_gain[None], ff_in, ff_out.T, channels=channels,
    )
    return jnp.swapaxes(block, 1, 2)


def solution(mesh):
    spread_all = (
        P(("row", "col"), None, None, None),
        P(("row", "col"), None, None),
        P(("row", "col"), None, None),
        P(("row", "col"), None),
    )
    placed = spread_all + (P(),) * 8 + (P(None, None, "row", "col"),) + (P(),) * 5
    return jax.shard_map(
        local, mesh=mesh, in_specs=placed, out_specs=P("row", "col", None), check_vma=False
    )
```

```python
import functools
import jax
import jax.numpy as jnp
from jax import lax
from jax.experimental import pallas as pl
from jax.experimental.layout import Layout, with_layout_constraint
from jax.experimental.pallas import tpu as pltpu
from jax.sharding import PartitionSpec as P

F32 = jnp.float32
BF16 = jnp.bfloat16
BLOCK = 1024
UNROLL = 4
TOGETHER = 4
LAST_UNROLL = 1
LANES = 128
SUB = 8
KERNEL_MIB = dict(
    place_norm_project=20, gate=10, conv_states=32, row_scan=16, inner_col=28, chain=8, chip_total=10, entering=13, finish=34
)


def whole():
    return pl.BlockSpec(memory_space=pltpu.VMEM)


KERNEL_US = dict(
    place_norm_project=12, gate=6, conv_states=31, row_scan=20, inner_col=16, chain=3, chip_total=5, entering=6, finish=25
)


def hbm():
    return pl.BlockSpec(memory_space=pltpu.HBM)


def call(body, outs, ins, scratch=(), name=None, out_specs=None):
    work = KERNEL_US[name] * 10**7
    return pl.pallas_call(
        body,
        cost_estimate=pl.CostEstimate(flops=work, bytes_accessed=work // 400, transcendentals=0),
        out_shape=outs,
        in_specs=ins,
        out_specs=out_specs or jax.tree.map(lambda _: whole(), outs),
        scratch_shapes=list(scratch),
        compiler_params=pltpu.CompilerParams(vmem_limit_bytes=KERNEL_MIB[name] * 1024 * 1024),
        name=name,
    )


def loop(count, step, unroll=1):
    def body(i, carry):
        for j in range(unroll):
            step(i * unroll + j)
        return carry

    lax.fori_loop(0, count // unroll, body, 0)


def dot(a, b):
    return jnp.dot(a, b, preferred_element_type=F32)


def dot_nt(a, b):
    return lax.dot_general(a, b, (((1,), (1,)), ((), ())), preferred_element_type=F32)


def dot_tn(a, b):
    return lax.dot_general(a, b, (((0,), (0,)), ((), ())), preferred_element_type=F32)


def silu(values):
    half = 0.5 * values
    return half + half * jnp.tanh(half)


def rms_scale(values, gains):
    return values * lax.rsqrt(jnp.mean(values * values, axis=-1, keepdims=True) + 1e-06) * gains


def two_parts(values):
    high = lax.reduce_precision(values, 8, 7)
    return high.astype(BF16), (values - high).astype(BF16)


def factor_rows(values):
    high, low = two_parts(values)
    heads = values.shape[1]
    both = jnp.concatenate([high, low], axis=1)
    return jnp.pad(both, ((0, 0), (0, 16 - 2 * heads), (0, 0), (0, 0)))


def row_layout(parts):
    return jnp.transpose(parts, (0, 2, 1, 3))


def col_layout(parts):
    k, m, r, c = parts.shape
    parts = parts.reshape(k, m, r, c // SUB, SUB)
    parts = jnp.transpose(parts, (0, 3, 1, 2, 4)).reshape(k, c // SUB, m, r * SUB)
    return with_layout_constraint(parts, Layout(major_to_minor=(0, 1, 2, 3)))


def decay_factors(decay):
    rows_n, cols_n = decay.shape[2:]
    upto_c = jnp.triu(jnp.ones((cols_n, cols_n), F32))
    upto_r = jnp.triu(jnp.ones((rows_n, rows_n), F32))
    exact = lax.Precision.HIGHEST
    cum = jnp.stack(
        [
            jnp.einsum("hru,ut->hrt", decay[0], upto_c, precision=exact),
            jnp.einsum("hru,ut->hrt", decay[1], upto_c.T, precision=exact),
            jnp.einsum("huc,ut->htc", decay[2], upto_r, precision=exact),
            jnp.einsum("huc,ut->htc", decay[3], upto_r.T, precision=exact),
        ]
    )
    total_row = jnp.sum(decay[:2], axis=3)
    total_col = jnp.sum(decay[2:], axis=2)
    mid = 0.5 * jnp.concatenate(
        [
            jnp.broadcast_to(total_row[..., None], decay[:2].shape),
            jnp.broadcast_to(total_col[:, :, None, :], decay[2:].shape),
        ]
    )
    weight = jnp.sqrt(-jnp.expm1(-2.0 * decay))
    into = factor_rows(weight * jnp.exp(cum - mid))
    out = factor_rows(jnp.exp(mid - cum))
    return (
        row_layout(into[:2]),
        row_layout(out[:2]),
        col_layout(into[2:]),
        col_layout(out[2:]),
        total_row,
        total_col,
    )


def place_body(cells, got, gain, in_x, grid_out, inner_out, left_out, right_out, *scratch):
    src, dst = scratch[:2], scratch[2:]
    slots = got.shape[0]
    channels = grid_out.shape[1]
    cells_n = grid_out.shape[0]
    cols_n = cells_n // left_out.shape[0]

    def fill(i, carry):
        at = pl.ds(pl.multiple_of(i * 256, 256), 256)
        for part in dst:
            part[at, :] = jnp.zeros((256, LANES), F32)
        return carry

    lax.fori_loop(0, cells_n // 256, fill, 0)

    def widen(i, carry):
        at = pl.ds(pl.multiple_of(i * 256, 256), 256)
        for m, part in enumerate(src):
            part[at, :] = got[at, m * LANES : (m + 1) * LANES].astype(F32)
        return carry

    lax.fori_loop(0, slots // 256, widen, 0)

    def place(i, carry):
        base = i * 16
        for j in range(16):
            cell = cells[base + j]
            for from_part, to_part in zip(src, dst):
                to_part[pl.ds(cell, 1), :] = from_part[pl.ds(base + j, 1), :]
        return carry

    lax.fori_loop(0, slots // 16, place, 0)

    def project(r, carry):
        at = pl.ds(pl.multiple_of(r * cols_n, cols_n), cols_n)
        tiles = jnp.concatenate([dst[0][at, :], dst[1][at, : channels - LANES]], axis=1)
        grid_out[at, :] = tiles.astype(BF16)
        normed = rms_scale(tiles, gain[...]).astype(BF16)
        inner = dot(normed, in_x[...]).astype(BF16)
        inner_out[at, :] = inner
        wide = inner.astype(F32)
        left_out[pl.ds(r, 1), :] = wide[:1]
        right_out[pl.ds(r, 1), :] = wide[cols_n - 1 :]
        return carry

    loop(cells_n // cols_n, lambda r: project(r, 0), UNROLL)


def place(cells, got, gain, in_x, rows_n, cols_n, channels):
    cells_n = rows_n * cols_n
    width = in_x.shape[1]
    outs = (
        jax.ShapeDtypeStruct((cells_n, channels), BF16),
        jax.ShapeDtypeStruct((cells_n, width), BF16),
        jax.ShapeDtypeStruct((rows_n, width), F32),
        jax.ShapeDtypeStruct((rows_n, width), F32),
    )
    return call(
        place_body,
        outs,
        [pl.BlockSpec(memory_space=pltpu.SMEM), whole(), whole(), whole()],
        [
            pltpu.VMEM((got.shape[0], LANES), F32),
            pltpu.VMEM((got.shape[0], LANES), F32),
            pltpu.VMEM((cells_n + SUB, LANES), F32),
            pltpu.VMEM((cells_n + SUB, LANES), F32),
        ],
        name="place_norm_project",
    )(cells, got, gain, in_x)


def gate_body(grid, gain, in_z, gate_out, *, block):
    def step(i, carry):
        at = pl.ds(pl.multiple_of(i * block, block), block)
        normed = rms_scale(grid[at, :].astype(F32), gain[...]).astype(BF16)
        gate = dot(normed, in_z[...]).astype(BF16).astype(F32)
        gate_out[at, :] = silu(gate).astype(BF16)
        return carry

    lax.fori_loop(0, grid.shape[0] // block, step, 0)


def gate(grid, gain, in_z):
    return call(
        functools.partial(gate_body, block=BLOCK),
        jax.ShapeDtypeStruct((grid.shape[0], in_z.shape[1]), BF16),
        [whole()] * 3,
        name="gate",
    )(grid, gain, in_z)


def spread(parts, heads_map):
    return dot_tn(parts, heads_map)


def own_column(shape, row_mod, col_mod):
    rows = lax.broadcasted_iota(jnp.int32, shape, 0)
    cols = lax.broadcasted_iota(jnp.int32, shape, 1)
    return (rows & (row_mod - 1)) == (cols & (col_mod - 1))


def conv_body(
    spot, inner, above, below, left, right, conv_w, conv_bias, x_proj, into_row, into_col, heads_map, pick_b,
    half_row, half_col, x_hbm, coef_hbm, state_row, own_hbm, other_hbm,
    padded, x_wide, coef_wide, left_sum, right_sum, x_out, coef_out, state_own, state_other, done,
):
    rows_n, cols_n, width = inner.shape
    state_size = LANES // 8
    peers, tile_rows = half_row.shape[:2]
    each = rows_n // peers
    for q in range(peers):
        state_row[q, 2 * each * state_size :] = half_row[q]
    padded[0] = above[...]
    padded[rows_n + 1] = below[...]

    def move(r, carry):
        padded[r + 1] = inner[r]
        return carry

    lax.fori_loop(0, rows_n, move, 0)
    for edge, column, sums in ((left, 0, left_sum), (right, 2, right_sum)):
        total = jnp.zeros((rows_n, 1, width), F32)
        for i in range(3):
            total = total + edge[i : i + rows_n] * conv_w[3 * i + column : 3 * i + column + 1, :][None]
        sums[...] = total
    first = lax.broadcasted_iota(jnp.int32, (cols_n, LANES), 0) == 0
    last = lax.broadcasted_iota(jnp.int32, (cols_n, LANES), 0) == cols_n - 1

    def row_step(r, carry):
        for part in range(width // LANES):
            lanes = slice(part * LANES, (part + 1) * LANES)
            rows = [padded[r + i, :, lanes].astype(F32) for i in range(3)]
            sums = []
            for j in range(3):
                total = rows[0] * conv_w[j : j + 1, lanes]
                total = total + rows[1] * conv_w[3 + j : 4 + j, lanes]
                sums.append(total + rows[2] * conv_w[6 + j : 7 + j, lanes])
            from_left = jnp.where(first, left_sum[r, :, lanes], pltpu.roll(sums[0], 1, 0))
            from_right = jnp.where(
                last, right_sum[r, :, lanes], pltpu.roll(sums[2], cols_n - 1, 0)
            )
            value = conv_bias[:, lanes] + from_left + sums[1] + from_right
            scanned = silu(value).astype(BF16)
            x_out[r, :, lanes] = scanned
            x_wide[r, :, lanes] = scanned.astype(F32)
        coef = dot(x_out[r], x_proj[...]).astype(BF16)
        coef_out[r] = coef
        coef_wide[r] = coef.astype(F32)
        flipped = coef.T
        for k in range(2):
            scaled = (x_wide[r] * spread(into_row[k, r], heads_map[...])).astype(BF16)
            b_part = flipped[2 * k * state_size : (2 * k + 1) * state_size, :]
            at = pl.multiple_of((r % each) * 2 * state_size + k * state_size, state_size)
            state_row[r // each, pl.ds(at, state_size), :] = dot(b_part, scaled).astype(BF16)
        return carry

    loop(rows_n, lambda r: row_step(r, 0), UNROLL)
    size = rows_n * SUB
    own = own_column((LANES, size), SUB, SUB)

    copies = [
        pltpu.make_async_copy(held, out, done.at[m])
        for m, (held, out) in enumerate(
            ((x_out, x_hbm), (coef_out, coef_hbm), (state_other, other_hbm), (state_own, own_hbm))
        )
    ]
    copies[0].start()
    copies[1].start()
    half = state_own.shape[0]
    deep = SUB * state_size

    def column_states(states, side):
        def col_step(j):
            g = side * half + j
            at = pl.ds(pl.multiple_of(g * SUB, SUB), SUB)
            x_group = x_wide[:, at, :].reshape(size, width)
            coef = coef_wide[:, at, :].reshape(size, LANES).astype(BF16)
            for k in range(2):
                scaled = (x_group * spread(into_col[k, g], heads_map[...])).astype(BF16)
                b_part = jnp.where(own, dot_nt(pick_b[k], coef), 0.0).astype(BF16)
                states[j, k * deep : (k + 1) * deep, :] = dot(b_part, scaled).astype(BF16)
            states[j, 2 * deep :, :] = half_col[g]

        loop(half, col_step, UNROLL)

    column_states(state_other, 1 - spot[0])
    copies[2].start()
    column_states(state_own, spot[0])
    copies[3].start()
    for copy in copies:
        copy.wait()


def conv_and_states(spot, inner, *rest):
    rows_n, cols_n, width = inner.shape
    half_row, half_col = rest[-2:]
    peers, tile_rows = half_row.shape[:2]
    groups, deep = half_col.shape[0] // 2, 2 * SUB * (LANES // 8) + half_col.shape[1]
    outs = (
        jax.ShapeDtypeStruct((rows_n, cols_n, width), BF16),
        jax.ShapeDtypeStruct((rows_n, cols_n, LANES), BF16),
        jax.ShapeDtypeStruct((peers, rows_n // peers * 2 * (LANES // 8) + tile_rows, width), BF16),
        jax.ShapeDtypeStruct((groups, deep, width), BF16),
        jax.ShapeDtypeStruct((groups, deep, width), BF16),
    )
    return call(
        conv_body,
        outs,
        [pl.BlockSpec(memory_space=pltpu.SMEM)] + [whole()] * 14,
        [
            pltpu.VMEM((rows_n + 2, cols_n, width), BF16),
            pltpu.VMEM((rows_n, cols_n, width), F32),
            pltpu.VMEM((rows_n, cols_n, LANES), F32),
            pltpu.VMEM((rows_n, 1, width), F32),
            pltpu.VMEM((rows_n, 1, width), F32),
            pltpu.VMEM((rows_n, cols_n, width), BF16),
            pltpu.VMEM((rows_n, cols_n, LANES), BF16),
            pltpu.VMEM((groups, deep, width), BF16),
            pltpu.VMEM((groups, deep, width), BF16),
            pltpu.SemaphoreType.DMA((4,)),
        ],
        name="conv_states",
        out_specs=(hbm(), hbm(), whole(), hbm(), hbm()),
    )(spot, inner, *rest)


def c_at_b(wide, k):
    state_size = LANES // 8
    lane = lax.broadcasted_iota(jnp.int32, (1, LANES), 1)
    rolled = pltpu.roll(wide, LANES - state_size, 1)
    return jnp.where((lane // state_size) == 2 * k, rolled, 0.0).astype(BF16)


def row_scan_body(x_in, coef_in, enter_row, into_row, out_row, heads_map, skip, total_out):
    rows_n, cols_n, width = x_in.shape
    t_row = lax.broadcasted_iota(jnp.int32, (cols_n, cols_n), 0)
    u_row = lax.broadcasted_iota(jnp.int32, (cols_n, cols_n), 1)
    masks = (t_row >= u_row, t_row <= u_row)

    state_size = LANES // 8

    def row_step(r):
        x_row = x_in[r].astype(F32)
        coef = coef_in[r]
        wide = coef.astype(F32)
        total = x_row * skip[...]
        for k in range(2):
            scores = dot_nt(c_at_b(wide, k), coef)
            mixing = jnp.where(masks[k], scores, 0.0).astype(BF16)
            c_part = coef[:, (2 * k + 1) * state_size : (2 * k + 2) * state_size]
            scaled = (x_row * spread(into_row[k, r], heads_map[...])).astype(BF16)
            both = dot(
                jnp.concatenate([mixing, c_part], axis=1),
                jnp.concatenate([scaled, enter_row[r, k]], axis=0),
            )
            total = total + both * spread(out_row[k, r], heads_map[...])
        total_out[r] = total.astype(BF16)

    loop(rows_n, row_step, UNROLL)


def row_scan(x_in, *rest):
    return call(
        row_scan_body, jax.ShapeDtypeStruct(x_in.shape, BF16), [whole()] * 7, name="row_scan"
    )(x_in, *rest)


def inner_col_body(x_in, coef_in, into_col, out_col, heads_map, total_out, x_wide, coef_wide, acc):
    rows_n, cols_n, width = x_in.shape

    def widen(r):
        x_wide[r] = x_in[r].astype(F32)
        coef_wide[r] = coef_in[r].astype(F32)

    loop(rows_n, widen, UNROLL)
    size = rows_n * SUB
    t_col = lax.broadcasted_iota(jnp.int32, (size, size), 0)
    u_col = lax.broadcasted_iota(jnp.int32, (size, size), 1)
    same = (t_col & (SUB - 1)) == (u_col & (SUB - 1))
    masks = (same & (t_col >= u_col), same & (t_col <= u_col))

    def col_step(g):
        at = pl.ds(pl.multiple_of(g * SUB, SUB), SUB)
        x_group = x_wide[:, at, :].reshape(size, width)
        wide = coef_wide[:, at, :].reshape(size, LANES)
        coef = wide.astype(BF16)
        total = jnp.zeros((size, width), F32)
        for k in range(2):
            scores = dot_nt(c_at_b(wide, k + 2), coef)
            mixing = jnp.where(masks[k], scores, 0.0).astype(BF16)
            scaled = (x_group * spread(into_col[k, g], heads_map[...])).astype(BF16)
            total = total + dot(mixing, scaled) * spread(out_col[k, g], heads_map[...])
        acc[:, at, :] = total.reshape(rows_n, SUB, width)

    loop(cols_n // SUB, col_step, UNROLL)

    def emit(r):
        total_out[r] = acc[r].astype(BF16)

    loop(rows_n, emit, UNROLL)


def inner_col(x_in, coef_in, into_col, out_col, heads_map):
    return call(
        inner_col_body,
        jax.ShapeDtypeStruct(x_in.shape, BF16),
        [whole()] * 5,
        [
            pltpu.VMEM(x_in.shape, F32),
            pltpu.VMEM(coef_in.shape, F32),
            pltpu.VMEM(x_in.shape, F32),
        ],
        name="inner_col",
    )(x_in, coef_in, into_col, out_col, heads_map)


def half_of(tile, k, heads_map):
    return dot(tile[:, 16 * k : 16 * k + 16], heads_map)


def chain_body(states, heads_map, entering):
    peers = states.shape[0]
    state_size = LANES // 8
    width = states.shape[2]
    lines = entering.shape[1] // (2 * state_size)
    top = 2 * lines * state_size
    for k in range(2):
        order = range(peers) if k == 0 else range(peers - 1, -1, -1)
        before = [jnp.zeros((state_size, width), F32)] * lines
        for at in order:
            scale = half_of(states[at, top:, :LANES], k, heads_map[...])
            for line in range(lines):
                rows = slice((2 * line + k) * state_size, (2 * line + k + 1) * state_size)
                own = scale[line : line + 1]
                entering[at, rows, :] = (own * before[line]).astype(BF16)
                before[line] = own * (own * before[line] + states[at, rows, :].astype(F32))


def chain(states, heads_map, lines):
    peers, _, width = states.shape
    return call(
        chain_body,
        jax.ShapeDtypeStruct((peers, lines * 2 * (LANES // 8), width), BF16),
        [whole()] * 2,
        name="chain",
    )(states, heads_map)


def pair_halves(upper, lower, j, top, heads_map):
    low_rows = pltpu.roll(lower[j, top:, :LANES].astype(F32), SUB, 0)
    first = lax.broadcasted_iota(jnp.int32, low_rows.shape, 0) < SUB
    tile = jnp.where(first, upper[j, top:, :LANES].astype(F32), low_rows).astype(BF16)
    halves = []
    for k in range(2):
        both = half_of(tile, k, heads_map)
        halves.append((both[:SUB], both[SUB:]))
    return tile, halves


def lines_of(states, j, k, lines_shape):
    deep = lines_shape[0] * lines_shape[1]
    return states[j, k * deep : (k + 1) * deep, :].astype(F32).reshape(lines_shape)


def by_core(spot, run, own, got):
    @pl.when(spot[0] == 0)
    def _():
        run(own, got)

    @pl.when(spot[0] != 0)
    def _():
        run(got, own)


def chip_total_body(spot, own, got, heads_map, *sends):
    groups, rows, width = own.shape
    state_size = LANES // 8
    deep = SUB * state_size
    shape = (state_size, SUB, width)
    chips = len(sends) + 1

    def run(upper, lower):
        def step(j):
            tile, halves = pair_halves(upper, lower, j, 2 * deep, heads_map[...])
            (up_2, low_2), (up_3, low_3) = halves
            down = (low_2 * low_2 * up_2) * lines_of(upper, j, 0, shape) + low_2 * lines_of(lower, j, 0, shape)
            rise = (up_3 * up_3 * low_3) * lines_of(lower, j, 1, shape) + up_3 * lines_of(upper, j, 1, shape)
            for shift, send in enumerate(sends, 1):
                past_end = spot[1] + shift >= chips
                send[j, :deep, :] = jnp.where(past_end, rise, down).reshape(deep, width).astype(BF16)
                send[j, deep:, :] = jnp.zeros((rows - 2 * deep, width), BF16)
                send[j, deep:, :LANES] = tile

        loop(groups, step, 4)

    by_core(spot, run, own, got)


def chip_total(spot, own, got, heads_map, chips):
    groups, rows, width = own.shape
    send = jax.ShapeDtypeStruct((groups, rows - SUB * (LANES // 8), width), BF16)
    return call(
        chip_total_body,
        (send,) * (chips - 1),
        [pl.BlockSpec(memory_space=pltpu.SMEM)] + [whole()] * 3,
        name="chip_total",
    )(spot, own, got, heads_map)


def entering_body(spot, own, got, heads_map, *rest):
    receipts, (enter_own, enter_other) = rest[:-2], rest[-2:]
    groups, rows, width = own.shape
    state_size = LANES // 8
    deep = SUB * state_size
    shape = (state_size, SUB, width)
    chips = len(receipts) + 1

    def run(upper, lower, enter_upper, enter_lower):
        def step(j):
            _, halves = pair_halves(upper, lower, j, 2 * deep, heads_map[...])
            (up_2, low_2), (up_3, low_3) = halves
            states = [lines_of(receipt, j, 0, shape) for receipt in receipts]
            keeps = []
            for k in range(2):
                keep = []
                for receipt in receipts:
                    both = half_of(receipt[j, deep:, :LANES], k, heads_map[...])
                    chip = both[:SUB] * both[SUB:]
                    keep.append(chip * chip)
                keeps.append(keep)
            down = jnp.zeros(shape, F32)
            rise = jnp.zeros(shape, F32)
            keep_2 = jnp.ones((SUB, width), F32)
            keep_3 = jnp.ones((SUB, width), F32)
            for away in range(1, chips):
                above, below = away - 1, chips - away - 1
                down = down + jnp.where(spot[1] >= away, keep_2, 0.0) * states[above]
                rise = rise + jnp.where(spot[1] + away < chips, keep_3, 0.0) * states[below]
                keep_2 = keep_2 * keeps[0][above]
                keep_3 = keep_3 * keeps[1][below]
            lower_2 = low_2 * up_2 * (up_2 * down + lines_of(upper, j, 0, shape))
            upper_3 = up_3 * low_3 * (low_3 * rise + lines_of(lower, j, 1, shape))
            enter_upper[j, 0] = (up_2 * down).reshape(deep, width).astype(BF16)
            enter_upper[j, 1] = upper_3.reshape(deep, width).astype(BF16)
            enter_lower[j, 0] = lower_2.reshape(deep, width).astype(BF16)
            enter_lower[j, 1] = (low_3 * rise).reshape(deep, width).astype(BF16)

        loop(groups, step, 4)

    @pl.when(spot[0] == 0)
    def _():
        run(own, got, enter_own, enter_other)

    @pl.when(spot[0] != 0)
    def _():
        run(got, own, enter_other, enter_own)


def entering_states(spot, own, got, heads_map, receipts):
    groups, rows, width = own.shape
    enter = jax.ShapeDtypeStruct((groups, 2, SUB * (LANES // 8), width), BF16)
    return call(
        entering_body,
        (enter, enter),
        [pl.BlockSpec(memory_space=pltpu.SMEM)] + [whole()] * (3 + len(receipts)),
        name="entering",
    )(spot, own, got, heads_map, *receipts)


def half_tiles(total, units):
    k, heads, lines = total.shape
    high, low = two_parts(jnp.exp(-0.5 * total))
    both = jnp.pad(jnp.concatenate([high, low], axis=1), ((0, 0), (0, 16 - 2 * heads), (0, 0)))
    both = jnp.transpose(both, (2, 0, 1)).reshape(units, lines // units, k * 16)
    rows = -(-both.shape[1] // 16) * 16
    return jnp.pad(both, ((0, 0), (0, rows - both.shape[1]), (0, 0)))


def finish_body(
    spot, total_row, total_col, coef_in, enter_own, enter_other, out_col, heads_map, pick_c, gate_in, grid,
    out_gain, out_w, mlp_gain, ff_in, ff_out, block_out, coef_wide, acc,
):
    rows_n, cols_n, width = total_row.shape
    half = enter_own.shape[0]

    def widen(r):
        coef_wide[r] = coef_in[r].astype(F32)
        acc[r] = total_row[r].astype(F32) + total_col[r].astype(F32)

    loop(rows_n, widen, UNROLL)
    size = rows_n * SUB
    own = own_column((size, LANES), SUB, SUB)

    def col_step(j):
        for enter, side in ((enter_own, spot[0]), (enter_other, 1 - spot[0])):
            g = side * half + j
            at = pl.ds(pl.multiple_of(g * SUB, SUB), SUB)
            coef = coef_wide[:, at, :].reshape(size, LANES).astype(BF16)
            value = acc[:, at, :].reshape(size, width)
            for k in range(2):
                c_part = jnp.where(own, dot(coef, pick_c[k]), 0.0).astype(BF16)
                value = value + dot(c_part, enter[j, k]) * spread(out_col[k, g], heads_map[...])
            acc[:, at, :] = value.reshape(rows_n, SUB, width)

    loop(half, col_step, UNROLL // 2)
    deep = TOGETHER * cols_n

    def last(i):
        at = pl.ds(pl.multiple_of(i * deep, deep), deep)
        value = acc[pl.ds(i * TOGETHER, TOGETHER)].reshape(deep, width)
        gated = (rms_scale(value, out_gain[...]) * gate_in[at, :].astype(F32)).astype(BF16)
        middle = (dot_nt(gated, out_w[...]) + grid[at, :].astype(F32)).astype(BF16)
        wide = middle.astype(F32)
        normed = rms_scale(wide, mlp_gain[...]).astype(BF16)
        hidden = dot(normed, ff_in[...])
        hidden = (hidden * (0.5 + 0.5 * lax.erf(hidden * (0.5**0.5)))).astype(BF16)
        result = dot_nt(hidden, ff_out[...]) + wide
        for j in range(TOGETHER):
            block_out[i * TOGETHER + j] = result[j * cols_n : (j + 1) * cols_n].T.astype(BF16)

    loop(rows_n // TOGETHER, last, LAST_UNROLL)


def finish(spot, total, total_col, coef, *rest, channels):
    rows_n, cols_n, width = total.shape
    return call(
        finish_body,
        jax.ShapeDtypeStruct((rows_n, channels, cols_n), BF16),
        [pl.BlockSpec(memory_space=pltpu.SMEM)] + [whole()] * 15,
        [pltpu.VMEM(coef.shape, F32), pltpu.VMEM(total.shape, F32)],
        name="finish",
    )(spot, total, total_col, coef, *rest)


def shifted(block, axis, up):
    count = lax.axis_size(axis)
    pairs = [(i, i + 1) if up else (i + 1, i) for i in range(count - 1)]
    return lax.ppermute(block, axis, pairs)


def local(
    tile_feats, tile_cell, tile_mask, tile_count, background, norm_gain, in_x, in_z, conv_w, conv_bias, x_proj,
    skip_gain, decay_rate, out_gain, out_w, mlp_gain, ff_in, ff_out,
):
    heads, rows_n, cols_n = decay_rate.shape[1:]
    owners, slots, channels = tile_feats.shape[1:]
    width = in_x.shape[1]
    state_size = x_proj.shape[1] // 8
    cells_n = rows_n * cols_n

    feats = jnp.transpose(tile_feats[0], (1, 2, 0))
    values = jnp.where(tile_mask[0].T[:, None, :] == 1, feats, background[None, :, None])
    live = jnp.arange(slots, dtype=jnp.int32)[:, None] < tile_count
    marked = jnp.where(live, tile_cell[0].T, cells_n)
    where = jnp.stack([marked // 64, marked % 64], axis=1).astype(BF16)
    filler = jnp.zeros((slots, 2 * LANES - channels - 2, owners), BF16)
    sent = jnp.concatenate([values, where, filler], axis=1)
    sent = with_layout_constraint(sent, Layout(major_to_minor=(0, 1, 2)))
    sent = lax.optimization_barrier(sent)
    sent = jnp.transpose(sent, (2, 0, 1))
    got = lax.all_to_all(sent, ("row", "col"), split_axis=0, concat_axis=0, tiled=True)
    into_row, out_row, into_col, out_col, total_row, total_col = decay_factors(decay_rate)
    half_row = half_tiles(total_row, lax.axis_size("col"))
    half_col = half_tiles(total_col, cols_n // SUB)
    half_row = jnp.pad(half_row, ((0, 0), (0, 0), (0, width - half_row.shape[2])))
    half_col = jnp.pad(half_col, ((0, 0), (0, 0), (0, width - half_col.shape[2])))
    line = lax.axis_index("row")
    spot = jnp.stack([line % 2, line // 2]).astype(jnp.int32)
    head_of = jnp.arange(width, dtype=jnp.int32) // (width // heads)
    part_of = jnp.arange(16, dtype=jnp.int32)
    heads_map = (
        ((part_of % heads)[:, None] == head_of[None, :]) & (part_of < 2 * heads)[:, None]
    ).astype(BF16)
    lane = jnp.arange(LANES, dtype=jnp.int32)
    picks = [
        (lane[:, None] == (m * state_size + lane // SUB)[None, :]).astype(BF16) for m in range(4, 8)
    ]
    pick_b = jnp.stack([picks[0].T, picks[2].T])
    pick_c = jnp.stack([picks[1], picks[3]])

    got = got.reshape(owners * slots, sent.shape[2])
    ready = (into_row, out_row, into_col, out_col, half_row, half_col, heads_map, pick_b, pick_c, spot)
    got, ready = lax.optimization_barrier((got, ready))
    into_row, out_row, into_col, out_col, half_row, half_col, heads_map, pick_b, pick_c, spot = ready
    cells = got[:, channels].astype(jnp.int32) * 64 + got[:, channels + 1].astype(jnp.int32)

    grid, inner, left_edge, right_edge = place(
        cells, got, norm_gain[None], in_x, rows_n, cols_n, channels
    )
    from_left = shifted(right_edge, "col", True).astype(BF16)
    from_right = shifted(left_edge, "col", False).astype(BF16)
    top = jnp.concatenate([inner[:cols_n], from_left[:1], from_right[:1]])
    bottom = jnp.concatenate([inner[cells_n - cols_n :], from_left[rows_n - 1 :], from_right[rows_n - 1 :]])
    above = shifted(bottom, "row", True)
    below = shifted(top, "row", False)
    left = jnp.concatenate([above[cols_n : cols_n + 1], from_left, below[cols_n : cols_n + 1]])[:, None].astype(F32)
    right = jnp.concatenate([above[cols_n + 1 :], from_right, below[cols_n + 1 :]])[:, None].astype(F32)

    x_in, coef, state_row, state_own, state_other = conv_and_states(
        spot, inner.reshape(rows_n, cols_n, width), above[:cols_n], below[:cols_n], left, right,
        conv_w.reshape(9, width), conv_bias[None], x_proj, into_row, into_col, heads_map, pick_b, half_row, half_col,
    )
    order = lax.optimization_barrier
    lines, peers = lax.axis_size("row"), lax.axis_size("col")
    chips = lines // 2
    twin = [(i, i ^ 1) for i in range(lines)]
    state_got = lax.ppermute(state_other, "row", twin)
    split_row = lax.all_to_all(state_row, "col", split_axis=0, concat_axis=0, tiled=True)
    sends = chip_total(spot, state_own, state_got, heads_map, chips)
    receipts = [
        lax.ppermute(send, "row", [(i, (i + 2 * shift) % lines) for i in range(lines)])
        for shift, send in enumerate(sends, 1)
    ]
    grid_in, sends = order((grid, sends))
    gated = gate(grid_in, norm_gain[None], in_z)
    split_row, gated = order((split_row, gated))
    passed = chain(split_row, heads_map, rows_n // peers)
    enter_row = lax.all_to_all(passed, "col", split_axis=0, concat_axis=0, tiled=True)
    enter_row = enter_row.reshape(rows_n, 2, state_size, width)
    x_col, passed = order((x_in, passed))
    total_col = inner_col(x_col, coef, into_col, out_col, heads_map)
    x_row, total_col = order((x_in, total_col))
    total = row_scan(x_row, coef, enter_row, into_row, out_row, heads_map, skip_gain[None])
    receipts, total = order((receipts, total))
    enter_own, enter_other = entering_states(spot, state_own, state_got, heads_map, receipts)
    enter_other = lax.ppermute(enter_other, "row", twin)
    block = finish(
        spot, total, total_col, coef, enter_own, enter_other, out_col, heads_map, pick_c, gated, grid,
        out_gain[None], out_w.T, mlp_gain[None], ff_in, ff_out.T, channels=channels,
    )
    return jnp.swapaxes(block, 1, 2)


def solution(mesh):
    spread_all = (
        P(("row", "col"), None, None, None),
        P(("row", "col"), None, None),
        P(("row", "col"), None, None),
        P(("row", "col"), None),
    )
    placed = spread_all + (P(),) * 8 + (P(None, None, "row", "col"),) + (P(),) * 5
    return jax.shard_map(
        local, mesh=mesh, in_specs=placed, out_specs=P("row", "col", None), check_vma=False
    )
```

```python
import functools
import jax
import jax.numpy as jnp
from jax import lax
from jax.experimental import pallas as pl
from jax.experimental.layout import Layout, with_layout_constraint
from jax.experimental.pallas import tpu as pltpu
from jax.sharding import PartitionSpec as P

F32 = jnp.float32
BF16 = jnp.bfloat16
BLOCK = 1024
UNROLL = 8
TOGETHER = 4
LAST_UNROLL = 1
LANES = 128
SUB = 8
KERNEL_MIB = dict(
    place_norm_project=20, gate=10, conv_states=32, row_scan=16, inner_col=28, chain=8, chip_total=10, entering=13, finish=34
)


def whole():
    return pl.BlockSpec(memory_space=pltpu.VMEM)


KERNEL_US = dict(
    place_norm_project=12, gate=6, conv_states=31, row_scan=20, inner_col=16, chain=3, chip_total=5, entering=6, finish=25
)


def hbm():
    return pl.BlockSpec(memory_space=pltpu.HBM)


def call(body, outs, ins, scratch=(), name=None, out_specs=None):
    work = KERNEL_US[name] * 10**7
    return pl.pallas_call(
        body,
        cost_estimate=pl.CostEstimate(flops=work, bytes_accessed=work // 400, transcendentals=0),
        out_shape=outs,
        in_specs=ins,
        out_specs=out_specs or jax.tree.map(lambda _: whole(), outs),
        scratch_shapes=list(scratch),
        compiler_params=pltpu.CompilerParams(vmem_limit_bytes=KERNEL_MIB[name] * 1024 * 1024),
        name=name,
    )


def loop(count, step, unroll=1):
    def body(i, carry):
        for j in range(unroll):
            step(i * unroll + j)
        return carry

    lax.fori_loop(0, count // unroll, body, 0)


def dot(a, b):
    return jnp.dot(a, b, preferred_element_type=F32)


def dot_nt(a, b):
    return lax.dot_general(a, b, (((1,), (1,)), ((), ())), preferred_element_type=F32)


def dot_tn(a, b):
    return lax.dot_general(a, b, (((0,), (0,)), ((), ())), preferred_element_type=F32)


def silu(values):
    half = 0.5 * values
    return half + half * jnp.tanh(half)


def rms_scale(values, gains):
    return values * lax.rsqrt(jnp.mean(values * values, axis=-1, keepdims=True) + 1e-06) * gains


def two_parts(values):
    high = lax.reduce_precision(values, 8, 7)
    return high.astype(BF16), (values - high).astype(BF16)


def factor_rows(values):
    high, low = two_parts(values)
    heads = values.shape[1]
    both = jnp.concatenate([high, low], axis=1)
    return jnp.pad(both, ((0, 0), (0, 16 - 2 * heads), (0, 0), (0, 0)))


def row_layout(parts):
    k, m, r, c = parts.shape
    return jnp.transpose(parts, (2, 0, 1, 3)).reshape(r, k * m, c)


def col_layout(parts):
    k, m, r, c = parts.shape
    parts = parts.reshape(k, m, r, c // SUB, SUB)
    parts = jnp.transpose(parts, (3, 0, 1, 2, 4)).reshape(c // SUB, k * m, r * SUB)
    return with_layout_constraint(parts, Layout(major_to_minor=(0, 1, 2)))


def decay_factors(decay):
    rows_n, cols_n = decay.shape[2:]
    upto_c = jnp.triu(jnp.ones((cols_n, cols_n), F32))
    upto_r = jnp.triu(jnp.ones((rows_n, rows_n), F32))
    exact = lax.Precision.HIGHEST
    cum = jnp.stack(
        [
            jnp.einsum("hru,ut->hrt", decay[0], upto_c, precision=exact),
            jnp.einsum("hru,ut->hrt", decay[1], upto_c.T, precision=exact),
            jnp.einsum("huc,ut->htc", decay[2], upto_r, precision=exact),
            jnp.einsum("huc,ut->htc", decay[3], upto_r.T, precision=exact),
        ]
    )
    total_row = jnp.sum(decay[:2], axis=3)
    total_col = jnp.sum(decay[2:], axis=2)
    mid = 0.5 * jnp.concatenate(
        [
            jnp.broadcast_to(total_row[..., None], decay[:2].shape),
            jnp.broadcast_to(total_col[:, :, None, :], decay[2:].shape),
        ]
    )
    weight = jnp.sqrt(-jnp.expm1(-2.0 * decay))
    into = factor_rows(weight * jnp.exp(cum - mid))
    out = factor_rows(jnp.exp(mid - cum))
    return (
        row_layout(into[:2]),
        row_layout(out[:2]),
        col_layout(into[2:]),
        col_layout(out[2:]),
        total_row,
        total_col,
    )


def place_body(cells, got, gain, in_x, grid_out, inner_out, left_out, right_out, *scratch):
    src, dst = scratch[:2], scratch[2:]
    slots = got.shape[0]
    channels = grid_out.shape[1]
    cells_n = grid_out.shape[0]
    cols_n = cells_n // left_out.shape[0]

    def fill(i, carry):
        at = pl.ds(pl.multiple_of(i * 256, 256), 256)
        for part in dst:
            part[at, :] = jnp.zeros((256, LANES), F32)
        return carry

    lax.fori_loop(0, cells_n // 256, fill, 0)

    def widen(i, carry):
        at = pl.ds(pl.multiple_of(i * 256, 256), 256)
        for m, part in enumerate(src):
            part[at, :] = got[at, m * LANES : (m + 1) * LANES].astype(F32)
        return carry

    lax.fori_loop(0, slots // 256, widen, 0)

    def place(i, carry):
        base = i * 16
        for j in range(16):
            cell = cells[base + j]
            for from_part, to_part in zip(src, dst):
                to_part[pl.ds(cell, 1), :] = from_part[pl.ds(base + j, 1), :]
        return carry

    lax.fori_loop(0, slots // 16, place, 0)

    def project(r, carry):
        at = pl.ds(pl.multiple_of(r * cols_n, cols_n), cols_n)
        tiles = jnp.concatenate([dst[0][at, :], dst[1][at, : channels - LANES]], axis=1)
        grid_out[at, :] = tiles.astype(BF16)
        normed = rms_scale(tiles, gain[...]).astype(BF16)
        inner = dot(normed, in_x[...]).astype(BF16)
        inner_out[at, :] = inner
        wide = inner.astype(F32)
        left_out[pl.ds(r, 1), :] = wide[:1]
        right_out[pl.ds(r, 1), :] = wide[cols_n - 1 :]
        return carry

    loop(cells_n // cols_n, lambda r: project(r, 0), UNROLL)


def place(cells, got, gain, in_x, rows_n, cols_n, channels):
    cells_n = rows_n * cols_n
    width = in_x.shape[1]
    outs = (
        jax.ShapeDtypeStruct((cells_n, channels), BF16),
        jax.ShapeDtypeStruct((cells_n, width), BF16),
        jax.ShapeDtypeStruct((rows_n, width), F32),
        jax.ShapeDtypeStruct((rows_n, width), F32),
    )
    return call(
        place_body,
        outs,
        [pl.BlockSpec(memory_space=pltpu.SMEM), whole(), whole(), whole()],
        [
            pltpu.VMEM((got.shape[0], LANES), F32),
            pltpu.VMEM((got.shape[0], LANES), F32),
            pltpu.VMEM((cells_n + SUB, LANES), F32),
            pltpu.VMEM((cells_n + SUB, LANES), F32),
        ],
        name="place_norm_project",
    )(cells, got, gain, in_x)


def gate_body(grid, gain, in_z, gate_out, *, block):
    def step(i, carry):
        at = pl.ds(pl.multiple_of(i * block, block), block)
        normed = rms_scale(grid[at, :].astype(F32), gain[...]).astype(BF16)
        gate = dot(normed, in_z[...]).astype(BF16).astype(F32)
        gate_out[at, :] = silu(gate).astype(BF16)
        return carry

    lax.fori_loop(0, grid.shape[0] // block, step, 0)


def gate(grid, gain, in_z):
    return call(
        functools.partial(gate_body, block=BLOCK),
        jax.ShapeDtypeStruct((grid.shape[0], in_z.shape[1]), BF16),
        [whole()] * 3,
        name="gate",
    )(grid, gain, in_z)


def spread(parts, heads_map):
    both = dot_tn(parts, heads_map)
    width = both.shape[1] // 2
    return both[:, :width], both[:, width:]


def own_column(shape, row_mod, col_mod):
    rows = lax.broadcasted_iota(jnp.int32, shape, 0)
    cols = lax.broadcasted_iota(jnp.int32, shape, 1)
    return (rows & (row_mod - 1)) == (cols & (col_mod - 1))


def conv_body(
    spot, inner, above, below, left, right, conv_w, conv_bias, x_proj, into_row, into_col, heads_map, pick_b,
    half_row, half_col, x_hbm, coef_hbm, state_row, own_hbm, other_hbm,
    padded, x_wide, coef_wide, left_sum, right_sum, x_out, coef_out, state_own, state_other, done,
):
    rows_n, cols_n, width = inner.shape
    state_size = LANES // 8
    peers, tile_rows = half_row.shape[:2]
    each = rows_n // peers
    for q in range(peers):
        state_row[q, 2 * each * state_size :] = half_row[q]
    padded[0] = above[...]
    padded[rows_n + 1] = below[...]

    def move(r, carry):
        padded[r + 1] = inner[r]
        return carry

    lax.fori_loop(0, rows_n, move, 0)
    for edge, column, sums in ((left, 0, left_sum), (right, 2, right_sum)):
        total = jnp.zeros((rows_n, 1, width), F32)
        for i in range(3):
            total = total + edge[i : i + rows_n] * conv_w[3 * i + column : 3 * i + column + 1, :][None]
        sums[...] = total
    first = lax.broadcasted_iota(jnp.int32, (cols_n, LANES), 0) == 0
    last = lax.broadcasted_iota(jnp.int32, (cols_n, LANES), 0) == cols_n - 1

    def row_step(r, carry):
        for part in range(width // LANES):
            lanes = slice(part * LANES, (part + 1) * LANES)
            rows = [padded[r + i, :, lanes].astype(F32) for i in range(3)]
            sums = []
            for j in range(3):
                total = rows[0] * conv_w[j : j + 1, lanes]
                total = total + rows[1] * conv_w[3 + j : 4 + j, lanes]
                sums.append(total + rows[2] * conv_w[6 + j : 7 + j, lanes])
            from_left = jnp.where(first, left_sum[r, :, lanes], pltpu.roll(sums[0], 1, 0))
            from_right = jnp.where(
                last, right_sum[r, :, lanes], pltpu.roll(sums[2], cols_n - 1, 0)
            )
            value = conv_bias[:, lanes] + from_left + sums[1] + from_right
            scanned = silu(value).astype(BF16)
            x_out[r, :, lanes] = scanned
            x_wide[r, :, lanes] = scanned.astype(F32)
        coef = dot(x_out[r], x_proj[...]).astype(BF16)
        coef_out[r] = coef
        coef_wide[r] = coef.astype(F32)
        flipped = coef.T
        into = spread(into_row[r], heads_map[...])
        for k in range(2):
            scaled = (x_wide[r] * into[k]).astype(BF16)
            b_part = flipped[2 * k * state_size : (2 * k + 1) * state_size, :]
            at = pl.multiple_of((r % each) * 2 * state_size + k * state_size, state_size)
            state_row[r // each, pl.ds(at, state_size), :] = dot(b_part, scaled).astype(BF16)
        return carry

    loop(rows_n, lambda r: row_step(r, 0), UNROLL)
    size = rows_n * SUB
    own = own_column((LANES, size), SUB, SUB)

    copies = [
        pltpu.make_async_copy(held, out, done.at[m])
        for m, (held, out) in enumerate(
            ((x_out, x_hbm), (coef_out, coef_hbm), (state_other, other_hbm), (state_own, own_hbm))
        )
    ]
    copies[0].start()
    copies[1].start()
    half = state_own.shape[0]
    deep = SUB * state_size

    def column_states(states, side):
        def col_step(j):
            g = side * half + j
            at = pl.ds(pl.multiple_of(g * SUB, SUB), SUB)
            x_group = x_wide[:, at, :].reshape(size, width)
            coef = coef_wide[:, at, :].reshape(size, LANES).astype(BF16)
            into = spread(into_col[g], heads_map[...])
            for k in range(2):
                scaled = (x_group * into[k]).astype(BF16)
                b_part = jnp.where(own, dot_nt(pick_b[k], coef), 0.0).astype(BF16)
                states[j, k * deep : (k + 1) * deep, :] = dot(b_part, scaled).astype(BF16)
            states[j, 2 * deep :, :] = half_col[g]

        loop(half, col_step, UNROLL)

    column_states(state_other, 1 - spot[0])
    copies[2].start()
    column_states(state_own, spot[0])
    copies[3].start()
    for copy in copies:
        copy.wait()


def conv_and_states(spot, inner, *rest):
    rows_n, cols_n, width = inner.shape
    half_row, half_col = rest[-2:]
    peers, tile_rows = half_row.shape[:2]
    groups, deep = half_col.shape[0] // 2, 2 * SUB * (LANES // 8) + half_col.shape[1]
    outs = (
        jax.ShapeDtypeStruct((rows_n, cols_n, width), BF16),
        jax.ShapeDtypeStruct((rows_n, cols_n, LANES), BF16),
        jax.ShapeDtypeStruct((peers, rows_n // peers * 2 * (LANES // 8) + tile_rows, width), BF16),
        jax.ShapeDtypeStruct((groups, deep, width), BF16),
        jax.ShapeDtypeStruct((groups, deep, width), BF16),
    )
    return call(
        conv_body,
        outs,
        [pl.BlockSpec(memory_space=pltpu.SMEM)] + [whole()] * 14,
        [
            pltpu.VMEM((rows_n + 2, cols_n, width), BF16),
            pltpu.VMEM((rows_n, cols_n, width), F32),
            pltpu.VMEM((rows_n, cols_n, LANES), F32),
            pltpu.VMEM((rows_n, 1, width), F32),
            pltpu.VMEM((rows_n, 1, width), F32),
            pltpu.VMEM((rows_n, cols_n, width), BF16),
            pltpu.VMEM((rows_n, cols_n, LANES), BF16),
            pltpu.VMEM((groups, deep, width), BF16),
            pltpu.VMEM((groups, deep, width), BF16),
            pltpu.SemaphoreType.DMA((4,)),
        ],
        name="conv_states",
        out_specs=(hbm(), hbm(), whole(), hbm(), hbm()),
    )(spot, inner, *rest)


def c_at_b(wide, k):
    state_size = LANES // 8
    lane = lax.broadcasted_iota(jnp.int32, (1, LANES), 1)
    rolled = pltpu.roll(wide, LANES - state_size, 1)
    return jnp.where((lane // state_size) == 2 * k, rolled, 0.0).astype(BF16)


def row_scan_body(x_in, coef_in, enter_row, into_row, out_row, heads_map, skip, total_out):
    rows_n, cols_n, width = x_in.shape
    t_row = lax.broadcasted_iota(jnp.int32, (cols_n, cols_n), 0)
    u_row = lax.broadcasted_iota(jnp.int32, (cols_n, cols_n), 1)
    masks = (t_row >= u_row, t_row <= u_row)

    state_size = LANES // 8

    def row_step(r):
        x_row = x_in[r].astype(F32)
        coef = coef_in[r]
        wide = coef.astype(F32)
        total = x_row * skip[...]
        into = spread(into_row[r], heads_map[...])
        out = spread(out_row[r], heads_map[...])
        for k in range(2):
            scores = dot_nt(c_at_b(wide, k), coef)
            mixing = jnp.where(masks[k], scores, 0.0).astype(BF16)
            c_part = coef[:, (2 * k + 1) * state_size : (2 * k + 2) * state_size]
            scaled = (x_row * into[k]).astype(BF16)
            both = dot(
                jnp.concatenate([mixing, c_part], axis=1),
                jnp.concatenate([scaled, enter_row[r, k]], axis=0),
            )
            total = total + both * out[k]
        total_out[r] = total.astype(BF16)

    loop(rows_n, row_step, UNROLL)


def row_scan(x_in, *rest):
    return call(
        row_scan_body, jax.ShapeDtypeStruct(x_in.shape, BF16), [whole()] * 7, name="row_scan"
    )(x_in, *rest)


def inner_col_body(x_in, coef_in, into_col, out_col, heads_map, total_out, x_wide, coef_wide, acc):
    rows_n, cols_n, width = x_in.shape

    def widen(r):
        x_wide[r] = x_in[r].astype(F32)
        coef_wide[r] = coef_in[r].astype(F32)

    loop(rows_n, widen, UNROLL)
    size = rows_n * SUB
    t_col = lax.broadcasted_iota(jnp.int32, (size, size), 0)
    u_col = lax.broadcasted_iota(jnp.int32, (size, size), 1)
    same = (t_col & (SUB - 1)) == (u_col & (SUB - 1))
    masks = (same & (t_col >= u_col), same & (t_col <= u_col))

    def col_step(g):
        at = pl.ds(pl.multiple_of(g * SUB, SUB), SUB)
        x_group = x_wide[:, at, :].reshape(size, width)
        wide = coef_wide[:, at, :].reshape(size, LANES)
        coef = wide.astype(BF16)
        total = jnp.zeros((size, width), F32)
        into = spread(into_col[g], heads_map[...])
        out = spread(out_col[g], heads_map[...])
        for k in range(2):
            scores = dot_nt(c_at_b(wide, k + 2), coef)
            mixing = jnp.where(masks[k], scores, 0.0).astype(BF16)
            scaled = (x_group * into[k]).astype(BF16)
            total = total + dot(mixing, scaled) * out[k]
        acc[:, at, :] = total.reshape(rows_n, SUB, width)

    loop(cols_n // SUB, col_step, UNROLL)

    def emit(r):
        total_out[r] = acc[r].astype(BF16)

    loop(rows_n, emit, UNROLL)


def inner_col(x_in, coef_in, into_col, out_col, heads_map):
    return call(
        inner_col_body,
        jax.ShapeDtypeStruct(x_in.shape, BF16),
        [whole()] * 5,
        [
            pltpu.VMEM(x_in.shape, F32),
            pltpu.VMEM(coef_in.shape, F32),
            pltpu.VMEM(x_in.shape, F32),
        ],
        name="inner_col",
    )(x_in, coef_in, into_col, out_col, heads_map)


def half_of(tile, k, heads_map):
    return dot(tile[:, 16 * k : 16 * k + 16], heads_map[:16, : heads_map.shape[1] // 2])


def chain_body(states, heads_map, entering):
    peers = states.shape[0]
    state_size = LANES // 8
    width = states.shape[2]
    lines = entering.shape[1] // (2 * state_size)
    top = 2 * lines * state_size
    for k in range(2):
        order = range(peers) if k == 0 else range(peers - 1, -1, -1)
        before = [jnp.zeros((state_size, width), F32)] * lines
        for at in order:
            scale = half_of(states[at, top:, :LANES], k, heads_map[...])
            for line in range(lines):
                rows = slice((2 * line + k) * state_size, (2 * line + k + 1) * state_size)
                own = scale[line : line + 1]
                entering[at, rows, :] = (own * before[line]).astype(BF16)
                before[line] = own * (own * before[line] + states[at, rows, :].astype(F32))


def chain(states, heads_map, lines):
    peers, _, width = states.shape
    return call(
        chain_body,
        jax.ShapeDtypeStruct((peers, lines * 2 * (LANES // 8), width), BF16),
        [whole()] * 2,
        name="chain",
    )(states, heads_map)


def pair_halves(upper, lower, j, top, heads_map):
    low_rows = pltpu.roll(lower[j, top:, :LANES].astype(F32), SUB, 0)
    first = lax.broadcasted_iota(jnp.int32, low_rows.shape, 0) < SUB
    tile = jnp.where(first, upper[j, top:, :LANES].astype(F32), low_rows).astype(BF16)
    halves = []
    for k in range(2):
        both = half_of(tile, k, heads_map)
        halves.append((both[:SUB], both[SUB:]))
    return tile, halves


def lines_of(states, j, k, lines_shape):
    deep = lines_shape[0] * lines_shape[1]
    return states[j, k * deep : (k + 1) * deep, :].astype(F32).reshape(lines_shape)


def by_core(spot, run, own, got):
    @pl.when(spot[0] == 0)
    def _():
        run(own, got)

    @pl.when(spot[0] != 0)
    def _():
        run(got, own)


def chip_total_body(spot, own, got, heads_map, *sends):
    groups, rows, width = own.shape
    state_size = LANES // 8
    deep = SUB * state_size
    shape = (state_size, SUB, width)
    chips = len(sends) + 1

    def run(upper, lower):
        def step(j):
            tile, halves = pair_halves(upper, lower, j, 2 * deep, heads_map[...])
            (up_2, low_2), (up_3, low_3) = halves
            down = (low_2 * low_2 * up_2) * lines_of(upper, j, 0, shape) + low_2 * lines_of(lower, j, 0, shape)
            rise = (up_3 * up_3 * low_3) * lines_of(lower, j, 1, shape) + up_3 * lines_of(upper, j, 1, shape)
            for shift, send in enumerate(sends, 1):
                past_end = spot[1] + shift >= chips
                send[j, :deep, :] = jnp.where(past_end, rise, down).reshape(deep, width).astype(BF16)
                send[j, deep:, :] = jnp.zeros((rows - 2 * deep, width), BF16)
                send[j, deep:, :LANES] = tile

        loop(groups, step, 4)

    by_core(spot, run, own, got)


def chip_total(spot, own, got, heads_map, chips):
    groups, rows, width = own.shape
    send = jax.ShapeDtypeStruct((groups, rows - SUB * (LANES // 8), width), BF16)
    return call(
        chip_total_body,
        (send,) * (chips - 1),
        [pl.BlockSpec(memory_space=pltpu.SMEM)] + [whole()] * 3,
        name="chip_total",
    )(spot, own, got, heads_map)


def entering_body(spot, own, got, heads_map, *rest):
    receipts, (enter_own, enter_other) = rest[:-2], rest[-2:]
    groups, rows, width = own.shape
    state_size = LANES // 8
    deep = SUB * state_size
    shape = (state_size, SUB, width)
    chips = len(receipts) + 1

    def run(upper, lower, enter_upper, enter_lower):
        def step(j):
            _, halves = pair_halves(upper, lower, j, 2 * deep, heads_map[...])
            (up_2, low_2), (up_3, low_3) = halves
            states = [lines_of(receipt, j, 0, shape) for receipt in receipts]
            keeps = []
            for k in range(2):
                keep = []
                for receipt in receipts:
                    both = half_of(receipt[j, deep:, :LANES], k, heads_map[...])
                    chip = both[:SUB] * both[SUB:]
                    keep.append(chip * chip)
                keeps.append(keep)
            down = jnp.zeros(shape, F32)
            rise = jnp.zeros(shape, F32)
            keep_2 = jnp.ones((SUB, width), F32)
            keep_3 = jnp.ones((SUB, width), F32)
            for away in range(1, chips):
                above, below = away - 1, chips - away - 1
                down = down + jnp.where(spot[1] >= away, keep_2, 0.0) * states[above]
                rise = rise + jnp.where(spot[1] + away < chips, keep_3, 0.0) * states[below]
                keep_2 = keep_2 * keeps[0][above]
                keep_3 = keep_3 * keeps[1][below]
            lower_2 = low_2 * up_2 * (up_2 * down + lines_of(upper, j, 0, shape))
            upper_3 = up_3 * low_3 * (low_3 * rise + lines_of(lower, j, 1, shape))
            enter_upper[j, 0] = (up_2 * down).reshape(deep, width).astype(BF16)
            enter_upper[j, 1] = upper_3.reshape(deep, width).astype(BF16)
            enter_lower[j, 0] = lower_2.reshape(deep, width).astype(BF16)
            enter_lower[j, 1] = (low_3 * rise).reshape(deep, width).astype(BF16)

        loop(groups, step, 4)

    @pl.when(spot[0] == 0)
    def _():
        run(own, got, enter_own, enter_other)

    @pl.when(spot[0] != 0)
    def _():
        run(got, own, enter_other, enter_own)


def entering_states(spot, own, got, heads_map, receipts):
    groups, rows, width = own.shape
    enter = jax.ShapeDtypeStruct((groups, 2, SUB * (LANES // 8), width), BF16)
    return call(
        entering_body,
        (enter, enter),
        [pl.BlockSpec(memory_space=pltpu.SMEM)] + [whole()] * (3 + len(receipts)),
        name="entering",
    )(spot, own, got, heads_map, *receipts)


def half_tiles(total, units):
    k, heads, lines = total.shape
    high, low = two_parts(jnp.exp(-0.5 * total))
    both = jnp.pad(jnp.concatenate([high, low], axis=1), ((0, 0), (0, 16 - 2 * heads), (0, 0)))
    both = jnp.transpose(both, (2, 0, 1)).reshape(units, lines // units, k * 16)
    rows = -(-both.shape[1] // 16) * 16
    return jnp.pad(both, ((0, 0), (0, rows - both.shape[1]), (0, 0)))


def finish_body(
    spot, total_row, total_col, coef_in, enter_own, enter_other, out_col, heads_map, pick_c, gate_in, grid,
    out_gain, out_w, mlp_gain, ff_in, ff_out, block_out, coef_wide, acc,
):
    rows_n, cols_n, width = total_row.shape
    half = enter_own.shape[0]

    def widen(r):
        coef_wide[r] = coef_in[r].astype(F32)
        acc[r] = total_row[r].astype(F32) + total_col[r].astype(F32)

    loop(rows_n, widen, UNROLL)
    size = rows_n * SUB
    own = own_column((size, LANES), SUB, SUB)

    def col_step(j):
        for enter, side in ((enter_own, spot[0]), (enter_other, 1 - spot[0])):
            g = side * half + j
            at = pl.ds(pl.multiple_of(g * SUB, SUB), SUB)
            coef = coef_wide[:, at, :].reshape(size, LANES).astype(BF16)
            value = acc[:, at, :].reshape(size, width)
            out = spread(out_col[g], heads_map[...])
            c_both = dot(coef, pick_c[...])
            for k in range(2):
                c_part = jnp.where(own, c_both[:, k * LANES : (k + 1) * LANES], 0.0).astype(BF16)
                value = value + dot(c_part, enter[j, k]) * out[k]
            acc[:, at, :] = value.reshape(rows_n, SUB, width)

    loop(half, col_step, UNROLL // 2)
    deep = TOGETHER * cols_n

    def last(i):
        at = pl.ds(pl.multiple_of(i * deep, deep), deep)
        value = acc[pl.ds(i * TOGETHER, TOGETHER)].reshape(deep, width)
        gated = (rms_scale(value, out_gain[...]) * gate_in[at, :].astype(F32)).astype(BF16)
        middle = (dot_nt(gated, out_w[...]) + grid[at, :].astype(F32)).astype(BF16)
        wide = middle.astype(F32)
        normed = rms_scale(wide, mlp_gain[...]).astype(BF16)
        hidden = dot(normed, ff_in[...])
        hidden = (hidden * (0.5 + 0.5 * lax.erf(hidden * (0.5**0.5)))).astype(BF16)
        result = dot_nt(hidden, ff_out[...]) + wide
        for j in range(TOGETHER):
            block_out[i * TOGETHER + j] = result[j * cols_n : (j + 1) * cols_n].T.astype(BF16)

    loop(rows_n // TOGETHER, last, LAST_UNROLL)


def finish(spot, total, total_col, coef, *rest, channels):
    rows_n, cols_n, width = total.shape
    return call(
        finish_body,
        jax.ShapeDtypeStruct((rows_n, channels, cols_n), BF16),
        [pl.BlockSpec(memory_space=pltpu.SMEM)] + [whole()] * 15,
        [pltpu.VMEM(coef.shape, F32), pltpu.VMEM(total.shape, F32)],
        name="finish",
    )(spot, total, total_col, coef, *rest)


def shifted(block, axis, up):
    count = lax.axis_size(axis)
    pairs = [(i, i + 1) if up else (i + 1, i) for i in range(count - 1)]
    return lax.ppermute(block, axis, pairs)


def local(
    tile_feats, tile_cell, tile_mask, tile_count, background, norm_gain, in_x, in_z, conv_w, conv_bias, x_proj,
    skip_gain, decay_rate, out_gain, out_w, mlp_gain, ff_in, ff_out,
):
    heads, rows_n, cols_n = decay_rate.shape[1:]
    owners, slots, channels = tile_feats.shape[1:]
    width = in_x.shape[1]
    state_size = x_proj.shape[1] // 8
    cells_n = rows_n * cols_n

    feats = jnp.transpose(tile_feats[0], (1, 2, 0))
    values = jnp.where(tile_mask[0].T[:, None, :] == 1, feats, background[None, :, None])
    live = jnp.arange(slots, dtype=jnp.int32)[:, None] < tile_count
    marked = jnp.where(live, tile_cell[0].T, cells_n)
    where = jnp.stack([marked // 64, marked % 64], axis=1).astype(BF16)
    filler = jnp.zeros((slots, 2 * LANES - channels - 2, owners), BF16)
    sent = jnp.concatenate([values, where, filler], axis=1)
    sent = with_layout_constraint(sent, Layout(major_to_minor=(0, 1, 2)))
    sent = lax.optimization_barrier(sent)
    sent = jnp.transpose(sent, (2, 0, 1))
    got = lax.all_to_all(sent, ("row", "col"), split_axis=0, concat_axis=0, tiled=True)
    into_row, out_row, into_col, out_col, total_row, total_col = decay_factors(decay_rate)
    half_row = half_tiles(total_row, lax.axis_size("col"))
    half_col = half_tiles(total_col, cols_n // SUB)
    half_row = jnp.pad(half_row, ((0, 0), (0, 0), (0, width - half_row.shape[2])))
    half_col = jnp.pad(half_col, ((0, 0), (0, 0), (0, width - half_col.shape[2])))
    line = lax.axis_index("row")
    spot = jnp.stack([line % 2, line // 2]).astype(jnp.int32)
    head_of = jnp.arange(2 * width, dtype=jnp.int32) // (width // heads)
    part_of = jnp.arange(32, dtype=jnp.int32)
    head_at = part_of // 16 * heads + part_of % 16 % heads
    heads_map = ((head_at[:, None] == head_of[None, :]) & (part_of % 16 < 2 * heads)[:, None]).astype(BF16)
    lane = jnp.arange(LANES, dtype=jnp.int32)
    picks = [
        (lane[:, None] == (m * state_size + lane // SUB)[None, :]).astype(BF16) for m in range(4, 8)
    ]
    pick_b = jnp.stack([picks[0].T, picks[2].T])
    pick_c = jnp.concatenate([picks[1], picks[3]], axis=1)

    got = got.reshape(owners * slots, sent.shape[2])
    ready = (into_row, out_row, into_col, out_col, half_row, half_col, heads_map, pick_b, pick_c, spot)
    got, ready = lax.optimization_barrier((got, ready))
    into_row, out_row, into_col, out_col, half_row, half_col, heads_map, pick_b, pick_c, spot = ready
    cells = got[:, channels].astype(jnp.int32) * 64 + got[:, channels + 1].astype(jnp.int32)

    grid, inner, left_edge, right_edge = place(
        cells, got, norm_gain[None], in_x, rows_n, cols_n, channels
    )
    from_left = shifted(right_edge, "col", True).astype(BF16)
    from_right = shifted(left_edge, "col", False).astype(BF16)
    top = jnp.concatenate([inner[:cols_n], from_left[:1], from_right[:1]])
    bottom = jnp.concatenate([inner[cells_n - cols_n :], from_left[rows_n - 1 :], from_right[rows_n - 1 :]])
    above = shifted(bottom, "row", True)
    below = shifted(top, "row", False)
    left = jnp.concatenate([above[cols_n : cols_n + 1], from_left, below[cols_n : cols_n + 1]])[:, None].astype(F32)
    right = jnp.concatenate([above[cols_n + 1 :], from_right, below[cols_n + 1 :]])[:, None].astype(F32)

    x_in, coef, state_row, state_own, state_other = conv_and_states(
        spot, inner.reshape(rows_n, cols_n, width), above[:cols_n], below[:cols_n], left, right,
        conv_w.reshape(9, width), conv_bias[None], x_proj, into_row, into_col, heads_map, pick_b, half_row, half_col,
    )
    order = lax.optimization_barrier
    lines, peers = lax.axis_size("row"), lax.axis_size("col")
    chips = lines // 2
    twin = [(i, i ^ 1) for i in range(lines)]
    state_got = lax.ppermute(state_other, "row", twin)
    split_row = lax.all_to_all(state_row, "col", split_axis=0, concat_axis=0, tiled=True)
    sends = chip_total(spot, state_own, state_got, heads_map, chips)
    receipts = [
        lax.ppermute(send, "row", [(i, (i + 2 * shift) % lines) for i in range(lines)])
        for shift, send in enumerate(sends, 1)
    ]
    grid_in, sends = order((grid, sends))
    gated = gate(grid_in, norm_gain[None], in_z)
    split_row, gated = order((split_row, gated))
    passed = chain(split_row, heads_map, rows_n // peers)
    enter_row = lax.all_to_all(passed, "col", split_axis=0, concat_axis=0, tiled=True)
    enter_row = enter_row.reshape(rows_n, 2, state_size, width)
    x_col, passed = order((x_in, passed))
    total_col = inner_col(x_col, coef, into_col, out_col, heads_map)
    x_row, total_col = order((x_in, total_col))
    total = row_scan(x_row, coef, enter_row, into_row, out_row, heads_map, skip_gain[None])
    receipts, total = order((receipts, total))
    enter_own, enter_other = entering_states(spot, state_own, state_got, heads_map, receipts)
    enter_other = lax.ppermute(enter_other, "row", twin)
    block = finish(
        spot, total, total_col, coef, enter_own, enter_other, out_col, heads_map, pick_c, gated, grid,
        out_gain[None], out_w.T, mlp_gain[None], ff_in, ff_out.T, channels=channels,
    )
    return jnp.swapaxes(block, 1, 2)


def solution(mesh):
    spread_all = (
        P(("row", "col"), None, None, None),
        P(("row", "col"), None, None),
        P(("row", "col"), None, None),
        P(("row", "col"), None),
    )
    placed = spread_all + (P(),) * 8 + (P(None, None, "row", "col"),) + (P(),) * 5
    return jax.shard_map(
        local, mesh=mesh, in_specs=placed, out_specs=P("row", "col", None), check_vma=False
    )
```

```python
import functools
import jax
import jax.numpy as jnp
from jax import lax
from jax.experimental import pallas as pl
from jax.experimental.layout import Layout, with_layout_constraint
from jax.experimental.pallas import tpu as pltpu
from jax.sharding import PartitionSpec as P

F32 = jnp.float32
BF16 = jnp.bfloat16
BLOCK = 1024
UNROLL = 8
TOGETHER = 4
LAST_UNROLL = 1
LANES = 128
SUB = 8
KERNEL_MIB = dict(
    place_norm_project=20, gate=10, conv_states=32, row_scan=57, inner_col=57, chain=8, chip_total=10, entering=13, finish=34
)


def whole():
    return pl.BlockSpec(memory_space=pltpu.VMEM)


KERNEL_US = dict(
    place_norm_project=12, gate=6, conv_states=31, row_scan=20, inner_col=16, chain=3, chip_total=5, entering=6, finish=25
)


def hbm():
    return pl.BlockSpec(memory_space=pltpu.HBM)


def block(shape, dim, size):
    where = tuple(size if at == dim else length for at, length in enumerate(shape))
    return pl.BlockSpec(where, lambda i: tuple(i if at == dim else 0 for at in range(len(shape))))


def same(shape):
    return pl.BlockSpec(shape, lambda i: (0,) * len(shape))


def call(body, outs, ins, scratch=(), name=None, out_specs=None, grid=()):
    work = KERNEL_US[name] * 10**7
    return pl.pallas_call(
        body,
        cost_estimate=pl.CostEstimate(flops=work, bytes_accessed=work // 400, transcendentals=0),
        out_shape=outs,
        grid=grid,
        in_specs=ins,
        out_specs=out_specs or jax.tree.map(lambda _: whole(), outs),
        scratch_shapes=list(scratch),
        compiler_params=pltpu.CompilerParams(vmem_limit_bytes=KERNEL_MIB[name] * 1024 * 1024),
        name=name,
    )


def loop(count, step, unroll=1):
    def body(i, carry):
        for j in range(unroll):
            step(i * unroll + j)
        return carry

    lax.fori_loop(0, count // unroll, body, 0)


def dot(a, b):
    return jnp.dot(a, b, preferred_element_type=F32)


def dot_nt(a, b):
    return lax.dot_general(a, b, (((1,), (1,)), ((), ())), preferred_element_type=F32)


def dot_tn(a, b):
    return lax.dot_general(a, b, (((0,), (0,)), ((), ())), preferred_element_type=F32)


def silu(values):
    half = 0.5 * values
    return half + half * jnp.tanh(half)


def rms_scale(values, gains):
    return values * lax.rsqrt(jnp.mean(values * values, axis=-1, keepdims=True) + 1e-06) * gains


def two_parts(values):
    high = lax.reduce_precision(values, 8, 7)
    return high.astype(BF16), (values - high).astype(BF16)


def factor_rows(values):
    high, low = two_parts(values)
    heads = values.shape[1]
    both = jnp.concatenate([high, low], axis=1)
    return jnp.pad(both, ((0, 0), (0, 16 - 2 * heads), (0, 0), (0, 0)))


def row_layout(parts):
    k, m, r, c = parts.shape
    return jnp.transpose(parts, (2, 0, 1, 3)).reshape(r, k * m, c)


def col_layout(parts):
    k, m, r, c = parts.shape
    parts = parts.reshape(k, m, r, c // SUB, SUB)
    parts = jnp.transpose(parts, (3, 0, 1, 2, 4)).reshape(c // SUB, k * m, r * SUB)
    return with_layout_constraint(parts, Layout(major_to_minor=(0, 1, 2)))


def decay_factors(decay):
    rows_n, cols_n = decay.shape[2:]
    upto_c = jnp.triu(jnp.ones((cols_n, cols_n), F32))
    upto_r = jnp.triu(jnp.ones((rows_n, rows_n), F32))
    exact = lax.Precision.HIGHEST
    cum = jnp.stack(
        [
            jnp.einsum("hru,ut->hrt", decay[0], upto_c, precision=exact),
            jnp.einsum("hru,ut->hrt", decay[1], upto_c.T, precision=exact),
            jnp.einsum("huc,ut->htc", decay[2], upto_r, precision=exact),
            jnp.einsum("huc,ut->htc", decay[3], upto_r.T, precision=exact),
        ]
    )
    total_row = jnp.sum(decay[:2], axis=3)
    total_col = jnp.sum(decay[2:], axis=2)
    mid = 0.5 * jnp.concatenate(
        [
            jnp.broadcast_to(total_row[..., None], decay[:2].shape),
            jnp.broadcast_to(total_col[:, :, None, :], decay[2:].shape),
        ]
    )
    weight = jnp.sqrt(-jnp.expm1(-2.0 * decay))
    into = factor_rows(weight * jnp.exp(cum - mid))
    out = factor_rows(jnp.exp(mid - cum))
    return (
        row_layout(into[:2]),
        row_layout(out[:2]),
        col_layout(into[2:]),
        col_layout(out[2:]),
        total_row,
        total_col,
    )


def place_body(cells, got, gain, in_x, grid_out, inner_out, left_out, right_out, *scratch):
    src, dst = scratch[:2], scratch[2:]
    slots = got.shape[0]
    channels = grid_out.shape[1]
    cells_n = grid_out.shape[0]
    cols_n = cells_n // left_out.shape[0]

    def fill(i, carry):
        at = pl.ds(pl.multiple_of(i * 256, 256), 256)
        for part in dst:
            part[at, :] = jnp.zeros((256, LANES), F32)
        return carry

    lax.fori_loop(0, cells_n // 256, fill, 0)

    def widen(i, carry):
        at = pl.ds(pl.multiple_of(i * 256, 256), 256)
        for m, part in enumerate(src):
            part[at, :] = got[at, m * LANES : (m + 1) * LANES].astype(F32)
        return carry

    lax.fori_loop(0, slots // 256, widen, 0)

    def place(i, carry):
        base = i * 16
        for j in range(16):
            cell = cells[base + j]
            for from_part, to_part in zip(src, dst):
                to_part[pl.ds(cell, 1), :] = from_part[pl.ds(base + j, 1), :]
        return carry

    lax.fori_loop(0, slots // 16, place, 0)

    def project(r, carry):
        at = pl.ds(pl.multiple_of(r * cols_n, cols_n), cols_n)
        tiles = jnp.concatenate([dst[0][at, :], dst[1][at, : channels - LANES]], axis=1)
        grid_out[at, :] = tiles.astype(BF16)
        normed = rms_scale(tiles, gain[...]).astype(BF16)
        inner = dot(normed, in_x[...]).astype(BF16)
        inner_out[at, :] = inner
        wide = inner.astype(F32)
        left_out[pl.ds(r, 1), :] = wide[:1]
        right_out[pl.ds(r, 1), :] = wide[cols_n - 1 :]
        return carry

    loop(cells_n // cols_n, lambda r: project(r, 0), UNROLL)


def place(cells, got, gain, in_x, rows_n, cols_n, channels):
    cells_n = rows_n * cols_n
    width = in_x.shape[1]
    outs = (
        jax.ShapeDtypeStruct((cells_n, channels), BF16),
        jax.ShapeDtypeStruct((cells_n, width), BF16),
        jax.ShapeDtypeStruct((rows_n, width), F32),
        jax.ShapeDtypeStruct((rows_n, width), F32),
    )
    return call(
        place_body,
        outs,
        [pl.BlockSpec(memory_space=pltpu.SMEM), whole(), whole(), whole()],
        [
            pltpu.VMEM((got.shape[0], LANES), F32),
            pltpu.VMEM((got.shape[0], LANES), F32),
            pltpu.VMEM((cells_n + SUB, LANES), F32),
            pltpu.VMEM((cells_n + SUB, LANES), F32),
        ],
        name="place_norm_project",
    )(cells, got, gain, in_x)


def gate_body(grid, gain, in_z, gate_out, *, block):
    def step(i, carry):
        at = pl.ds(pl.multiple_of(i * block, block), block)
        normed = rms_scale(grid[at, :].astype(F32), gain[...]).astype(BF16)
        gate = dot(normed, in_z[...]).astype(BF16).astype(F32)
        gate_out[at, :] = silu(gate).astype(BF16)
        return carry

    lax.fori_loop(0, grid.shape[0] // block, step, 0)


def gate(grid, gain, in_z):
    return call(
        functools.partial(gate_body, block=BLOCK),
        jax.ShapeDtypeStruct((grid.shape[0], in_z.shape[1]), BF16),
        [whole()] * 3,
        name="gate",
    )(grid, gain, in_z)


def spread(parts, heads_map):
    both = dot_tn(parts, heads_map)
    width = both.shape[1] // 2
    return both[:, :width], both[:, width:]


def own_column(shape, row_mod, col_mod):
    rows = lax.broadcasted_iota(jnp.int32, shape, 0)
    cols = lax.broadcasted_iota(jnp.int32, shape, 1)
    return (rows & (row_mod - 1)) == (cols & (col_mod - 1))


def conv_body(
    spot, inner, above, below, left, right, conv_w, conv_bias, x_proj, into_row, into_col, heads_map, pick_b,
    half_row, half_col, x_hbm, coef_hbm, state_row, own_hbm, other_hbm,
    padded, x_wide, coef_wide, left_sum, right_sum, x_out, coef_out, state_own, state_other, done,
):
    rows_n, cols_n, width = inner.shape
    state_size = LANES // 8
    peers, tile_rows = half_row.shape[:2]
    each = rows_n // peers
    for q in range(peers):
        state_row[q, 2 * each * state_size :] = half_row[q]
    padded[0] = above[...]
    padded[rows_n + 1] = below[...]

    def move(r, carry):
        padded[r + 1] = inner[r]
        return carry

    lax.fori_loop(0, rows_n, move, 0)
    for edge, column, sums in ((left, 0, left_sum), (right, 2, right_sum)):
        total = jnp.zeros((rows_n, 1, width), F32)
        for i in range(3):
            total = total + edge[i : i + rows_n] * conv_w[3 * i + column : 3 * i + column + 1, :][None]
        sums[...] = total
    first = lax.broadcasted_iota(jnp.int32, (cols_n, LANES), 0) == 0
    last = lax.broadcasted_iota(jnp.int32, (cols_n, LANES), 0) == cols_n - 1

    def row_step(r, carry):
        for part in range(width // LANES):
            lanes = slice(part * LANES, (part + 1) * LANES)
            rows = [padded[r + i, :, lanes].astype(F32) for i in range(3)]
            sums = []
            for j in range(3):
                total = rows[0] * conv_w[j : j + 1, lanes]
                total = total + rows[1] * conv_w[3 + j : 4 + j, lanes]
                sums.append(total + rows[2] * conv_w[6 + j : 7 + j, lanes])
            from_left = jnp.where(first, left_sum[r, :, lanes], pltpu.roll(sums[0], 1, 0))
            from_right = jnp.where(
                last, right_sum[r, :, lanes], pltpu.roll(sums[2], cols_n - 1, 0)
            )
            value = conv_bias[:, lanes] + from_left + sums[1] + from_right
            scanned = silu(value).astype(BF16)
            x_out[r, :, lanes] = scanned
            x_wide[r, :, lanes] = scanned.astype(F32)
        coef = dot(x_out[r], x_proj[...]).astype(BF16)
        coef_out[r] = coef
        coef_wide[r] = coef.astype(F32)
        flipped = coef.T
        into = spread(into_row[r], heads_map[...])
        for k in range(2):
            scaled = (x_wide[r] * into[k]).astype(BF16)
            b_part = flipped[2 * k * state_size : (2 * k + 1) * state_size, :]
            at = pl.multiple_of((r % each) * 2 * state_size + k * state_size, state_size)
            state_row[r // each, pl.ds(at, state_size), :] = dot(b_part, scaled).astype(BF16)
        return carry

    loop(rows_n, lambda r: row_step(r, 0), UNROLL)
    size = rows_n * SUB
    own = own_column((LANES, size), SUB, SUB)

    copies = [
        pltpu.make_async_copy(held, out, done.at[m])
        for m, (held, out) in enumerate(
            ((x_out, x_hbm), (coef_out, coef_hbm), (state_other, other_hbm), (state_own, own_hbm))
        )
    ]
    copies[0].start()
    copies[1].start()
    half = state_own.shape[0]
    deep = SUB * state_size

    def column_states(states, side):
        def col_step(j):
            g = side * half + j
            at = pl.ds(pl.multiple_of(g * SUB, SUB), SUB)
            x_group = x_wide[:, at, :].reshape(size, width)
            coef = coef_wide[:, at, :].reshape(size, LANES).astype(BF16)
            into = spread(into_col[g], heads_map[...])
            for k in range(2):
                scaled = (x_group * into[k]).astype(BF16)
                b_part = jnp.where(own, dot_nt(pick_b[k], coef), 0.0).astype(BF16)
                states[j, k * deep : (k + 1) * deep, :] = dot(b_part, scaled).astype(BF16)
            states[j, 2 * deep :, :] = half_col[g]

        loop(half, col_step, UNROLL)

    column_states(state_other, 1 - spot[0])
    copies[2].start()
    column_states(state_own, spot[0])
    copies[3].start()
    for copy in copies:
        copy.wait()


def conv_and_states(spot, inner, *rest):
    rows_n, cols_n, width = inner.shape
    half_row, half_col = rest[-2:]
    peers, tile_rows = half_row.shape[:2]
    groups, deep = half_col.shape[0] // 2, 2 * SUB * (LANES // 8) + half_col.shape[1]
    outs = (
        jax.ShapeDtypeStruct((rows_n, cols_n, width), BF16),
        jax.ShapeDtypeStruct((rows_n, cols_n, LANES), BF16),
        jax.ShapeDtypeStruct((peers, rows_n // peers * 2 * (LANES // 8) + tile_rows, width), BF16),
        jax.ShapeDtypeStruct((groups, deep, width), BF16),
        jax.ShapeDtypeStruct((groups, deep, width), BF16),
    )
    return call(
        conv_body,
        outs,
        [pl.BlockSpec(memory_space=pltpu.SMEM)] + [whole()] * 14,
        [
            pltpu.VMEM((rows_n + 2, cols_n, width), BF16),
            pltpu.VMEM((rows_n, cols_n, width), F32),
            pltpu.VMEM((rows_n, cols_n, LANES), F32),
            pltpu.VMEM((rows_n, 1, width), F32),
            pltpu.VMEM((rows_n, 1, width), F32),
            pltpu.VMEM((rows_n, cols_n, width), BF16),
            pltpu.VMEM((rows_n, cols_n, LANES), BF16),
            pltpu.VMEM((groups, deep, width), BF16),
            pltpu.VMEM((groups, deep, width), BF16),
            pltpu.SemaphoreType.DMA((4,)),
        ],
        name="conv_states",
        out_specs=(hbm(), hbm(), whole(), hbm(), hbm()),
    )(spot, inner, *rest)


def c_at_b(wide, k):
    state_size = LANES // 8
    lane = lax.broadcasted_iota(jnp.int32, (1, LANES), 1)
    rolled = pltpu.roll(wide, LANES - state_size, 1)
    return jnp.where((lane // state_size) == 2 * k, rolled, 0.0).astype(BF16)


def row_scan_body(x_in, coef_in, enter_row, into_row, out_row, heads_map, skip, total_out):
    rows_n, cols_n, width = x_in.shape
    t_row = lax.broadcasted_iota(jnp.int32, (cols_n, cols_n), 0)
    u_row = lax.broadcasted_iota(jnp.int32, (cols_n, cols_n), 1)
    masks = (t_row >= u_row, t_row <= u_row)

    state_size = LANES // 8

    def row_step(r):
        x_row = x_in[r].astype(F32)
        coef = coef_in[r]
        wide = coef.astype(F32)
        total = x_row * skip[...]
        into = spread(into_row[r], heads_map[...])
        out = spread(out_row[r], heads_map[...])
        for k in range(2):
            scores = dot_nt(c_at_b(wide, k), coef)
            mixing = jnp.where(masks[k], scores, 0.0).astype(BF16)
            c_part = coef[:, (2 * k + 1) * state_size : (2 * k + 2) * state_size]
            scaled = (x_row * into[k]).astype(BF16)
            both = dot(
                jnp.concatenate([mixing, c_part], axis=1),
                jnp.concatenate([scaled, enter_row[r, k]], axis=0),
            )
            total = total + both * out[k]
        total_out[r] = total.astype(BF16)

    loop(rows_n, row_step, UNROLL)


def row_scan(x_in, coef, enter_row, into_row, out_row, heads_map, skip):
    by_row = [block(array.shape, 0, UNROLL) for array in (x_in, coef, enter_row, into_row, out_row)]
    return call(
        row_scan_body,
        jax.ShapeDtypeStruct(x_in.shape, BF16),
        by_row + [same(heads_map.shape), same(skip.shape)],
        name="row_scan",
        out_specs=by_row[0],
        grid=(x_in.shape[0] // UNROLL,),
    )(x_in, coef, enter_row, into_row, out_row, heads_map, skip)


def inner_col_body(x_in, coef_in, into_col, out_col, heads_map, total_out, x_wide, coef_wide, acc):
    rows_n, cols_n, width = x_in.shape

    def widen(r):
        x_wide[r] = x_in[r].astype(F32)
        coef_wide[r] = coef_in[r].astype(F32)

    loop(rows_n, widen, UNROLL)
    size = rows_n * SUB
    t_col = lax.broadcasted_iota(jnp.int32, (size, size), 0)
    u_col = lax.broadcasted_iota(jnp.int32, (size, size), 1)
    same = (t_col & (SUB - 1)) == (u_col & (SUB - 1))
    masks = (same & (t_col >= u_col), same & (t_col <= u_col))

    def col_step(g):
        at = pl.ds(pl.multiple_of(g * SUB, SUB), SUB)
        x_group = x_wide[:, at, :].reshape(size, width)
        wide = coef_wide[:, at, :].reshape(size, LANES)
        coef = wide.astype(BF16)
        total = jnp.zeros((size, width), F32)
        into = spread(into_col[g], heads_map[...])
        out = spread(out_col[g], heads_map[...])
        for k in range(2):
            scores = dot_nt(c_at_b(wide, k + 2), coef)
            mixing = jnp.where(masks[k], scores, 0.0).astype(BF16)
            scaled = (x_group * into[k]).astype(BF16)
            total = total + dot(mixing, scaled) * out[k]
        acc[:, at, :] = total.reshape(rows_n, SUB, width)

    loop(cols_n // SUB, col_step, cols_n // SUB)

    def emit(r):
        total_out[r] = acc[r].astype(BF16)

    loop(rows_n, emit, UNROLL)


def inner_col(x_in, coef, into_col, out_col, heads_map):
    rows_n, cols_n, width = x_in.shape
    groups = 4
    wide = groups * SUB
    cols = block(x_in.shape, 1, wide)
    return call(
        inner_col_body,
        jax.ShapeDtypeStruct(x_in.shape, BF16),
        [
            cols,
            block(coef.shape, 1, wide),
            block(into_col.shape, 0, groups),
            block(out_col.shape, 0, groups),
            same(heads_map.shape),
        ],
        [
            pltpu.VMEM((rows_n, wide, width), F32),
            pltpu.VMEM((rows_n, wide, LANES), F32),
            pltpu.VMEM((rows_n, wide, width), F32),
        ],
        name="inner_col",
        out_specs=cols,
        grid=(cols_n // wide,),
    )(x_in, coef, into_col, out_col, heads_map)


def half_of(tile, k, heads_map):
    return dot(tile[:, 16 * k : 16 * k + 16], heads_map[:16, : heads_map.shape[1] // 2])


def chain_body(states, heads_map, entering):
    peers = states.shape[0]
    state_size = LANES // 8
    width = states.shape[2]
    lines = entering.shape[1] // (2 * state_size)
    top = 2 * lines * state_size
    for k in range(2):
        order = range(peers) if k == 0 else range(peers - 1, -1, -1)
        before = [jnp.zeros((state_size, width), F32)] * lines
        for at in order:
            scale = half_of(states[at, top:, :LANES], k, heads_map[...])
            for line in range(lines):
                rows = slice((2 * line + k) * state_size, (2 * line + k + 1) * state_size)
                own = scale[line : line + 1]
                entering[at, rows, :] = (own * before[line]).astype(BF16)
                before[line] = own * (own * before[line] + states[at, rows, :].astype(F32))


def chain(states, heads_map, lines):
    peers, _, width = states.shape
    return call(
        chain_body,
        jax.ShapeDtypeStruct((peers, lines * 2 * (LANES // 8), width), BF16),
        [whole()] * 2,
        name="chain",
    )(states, heads_map)


def pair_halves(upper, lower, j, top, heads_map):
    low_rows = pltpu.roll(lower[j, top:, :LANES].astype(F32), SUB, 0)
    first = lax.broadcasted_iota(jnp.int32, low_rows.shape, 0) < SUB
    tile = jnp.where(first, upper[j, top:, :LANES].astype(F32), low_rows).astype(BF16)
    halves = []
    for k in range(2):
        both = half_of(tile, k, heads_map)
        halves.append((both[:SUB], both[SUB:]))
    return tile, halves


def lines_of(states, j, k, lines_shape):
    deep = lines_shape[0] * lines_shape[1]
    return states[j, k * deep : (k + 1) * deep, :].astype(F32).reshape(lines_shape)


def by_core(spot, run, own, got):
    @pl.when(spot[0] == 0)
    def _():
        run(own, got)

    @pl.when(spot[0] != 0)
    def _():
        run(got, own)


def chip_total_body(spot, own, got, heads_map, *sends):
    groups, rows, width = own.shape
    state_size = LANES // 8
    deep = SUB * state_size
    shape = (state_size, SUB, width)
    chips = len(sends) + 1

    def run(upper, lower):
        def step(j):
            tile, halves = pair_halves(upper, lower, j, 2 * deep, heads_map[...])
            (up_2, low_2), (up_3, low_3) = halves
            down = (low_2 * low_2 * up_2) * lines_of(upper, j, 0, shape) + low_2 * lines_of(lower, j, 0, shape)
            rise = (up_3 * up_3 * low_3) * lines_of(lower, j, 1, shape) + up_3 * lines_of(upper, j, 1, shape)
            for shift, send in enumerate(sends, 1):
                past_end = spot[1] + shift >= chips
                send[j, :deep, :] = jnp.where(past_end, rise, down).reshape(deep, width).astype(BF16)
                send[j, deep:, :] = jnp.zeros((rows - 2 * deep, width), BF16)
                send[j, deep:, :LANES] = tile

        loop(groups, step, 4)

    by_core(spot, run, own, got)


def chip_total(spot, own, got, heads_map, chips):
    groups, rows, width = own.shape
    send = jax.ShapeDtypeStruct((groups, rows - SUB * (LANES // 8), width), BF16)
    return call(
        chip_total_body,
        (send,) * (chips - 1),
        [pl.BlockSpec(memory_space=pltpu.SMEM)] + [whole()] * 3,
        name="chip_total",
    )(spot, own, got, heads_map)


def entering_body(spot, own, got, heads_map, *rest):
    receipts, (enter_own, enter_other) = rest[:-2], rest[-2:]
    groups, rows, width = own.shape
    state_size = LANES // 8
    deep = SUB * state_size
    shape = (state_size, SUB, width)
    chips = len(receipts) + 1

    def run(upper, lower, enter_upper, enter_lower):
        def step(j):
            _, halves = pair_halves(upper, lower, j, 2 * deep, heads_map[...])
            (up_2, low_2), (up_3, low_3) = halves
            states = [lines_of(receipt, j, 0, shape) for receipt in receipts]
            keeps = []
            for k in range(2):
                keep = []
                for receipt in receipts:
                    both = half_of(receipt[j, deep:, :LANES], k, heads_map[...])
                    chip = both[:SUB] * both[SUB:]
                    keep.append(chip * chip)
                keeps.append(keep)
            down = jnp.zeros(shape, F32)
            rise = jnp.zeros(shape, F32)
            keep_2 = jnp.ones((SUB, width), F32)
            keep_3 = jnp.ones((SUB, width), F32)
            for away in range(1, chips):
                above, below = away - 1, chips - away - 1
                down = down + jnp.where(spot[1] >= away, keep_2, 0.0) * states[above]
                rise = rise + jnp.where(spot[1] + away < chips, keep_3, 0.0) * states[below]
                keep_2 = keep_2 * keeps[0][above]
                keep_3 = keep_3 * keeps[1][below]
            lower_2 = low_2 * up_2 * (up_2 * down + lines_of(upper, j, 0, shape))
            upper_3 = up_3 * low_3 * (low_3 * rise + lines_of(lower, j, 1, shape))
            enter_upper[j, 0] = (up_2 * down).reshape(deep, width).astype(BF16)
            enter_upper[j, 1] = upper_3.reshape(deep, width).astype(BF16)
            enter_lower[j, 0] = lower_2.reshape(deep, width).astype(BF16)
            enter_lower[j, 1] = (low_3 * rise).reshape(deep, width).astype(BF16)

        loop(groups, step, 4)

    @pl.when(spot[0] == 0)
    def _():
        run(own, got, enter_own, enter_other)

    @pl.when(spot[0] != 0)
    def _():
        run(got, own, enter_other, enter_own)


def entering_states(spot, own, got, heads_map, receipts):
    groups, rows, width = own.shape
    enter = jax.ShapeDtypeStruct((groups, 2, SUB * (LANES // 8), width), BF16)
    return call(
        entering_body,
        (enter, enter),
        [pl.BlockSpec(memory_space=pltpu.SMEM)] + [whole()] * (3 + len(receipts)),
        name="entering",
    )(spot, own, got, heads_map, *receipts)


def half_tiles(total, units):
    k, heads, lines = total.shape
    high, low = two_parts(jnp.exp(-0.5 * total))
    both = jnp.pad(jnp.concatenate([high, low], axis=1), ((0, 0), (0, 16 - 2 * heads), (0, 0)))
    both = jnp.transpose(both, (2, 0, 1)).reshape(units, lines // units, k * 16)
    rows = -(-both.shape[1] // 16) * 16
    return jnp.pad(both, ((0, 0), (0, rows - both.shape[1]), (0, 0)))


def finish_body(
    spot, total_row, total_col, coef_in, enter_own, enter_other, out_col, heads_map, pick_c, gate_in, grid,
    out_gain, out_w, mlp_gain, ff_in, ff_out, block_out, coef_wide, acc,
):
    rows_n, cols_n, width = total_row.shape
    half = enter_own.shape[0]

    def widen(r):
        coef_wide[r] = coef_in[r].astype(F32)
        acc[r] = total_row[r].astype(F32) + total_col[r].astype(F32)

    loop(rows_n, widen, UNROLL)
    size = rows_n * SUB
    own = own_column((size, LANES), SUB, SUB)

    def col_step(j):
        for enter, side in ((enter_own, spot[0]), (enter_other, 1 - spot[0])):
            g = side * half + j
            at = pl.ds(pl.multiple_of(g * SUB, SUB), SUB)
            coef = coef_wide[:, at, :].reshape(size, LANES).astype(BF16)
            value = acc[:, at, :].reshape(size, width)
            out = spread(out_col[g], heads_map[...])
            c_both = dot(coef, pick_c[...])
            for k in range(2):
                c_part = jnp.where(own, c_both[:, k * LANES : (k + 1) * LANES], 0.0).astype(BF16)
                value = value + dot(c_part, enter[j, k]) * out[k]
            acc[:, at, :] = value.reshape(rows_n, SUB, width)

    loop(half, col_step, UNROLL // 2)
    deep = TOGETHER * cols_n

    def last(i):
        at = pl.ds(pl.multiple_of(i * deep, deep), deep)
        value = acc[pl.ds(i * TOGETHER, TOGETHER)].reshape(deep, width)
        gated = (rms_scale(value, out_gain[...]) * gate_in[at, :].astype(F32)).astype(BF16)
        middle = (dot_nt(gated, out_w[...]) + grid[at, :].astype(F32)).astype(BF16)
        wide = middle.astype(F32)
        normed = rms_scale(wide, mlp_gain[...]).astype(BF16)
        hidden = dot(normed, ff_in[...])
        hidden = (hidden * (0.5 + 0.5 * lax.erf(hidden * (0.5**0.5)))).astype(BF16)
        result = dot_nt(hidden, ff_out[...]) + wide
        for j in range(TOGETHER):
            block_out[i * TOGETHER + j] = result[j * cols_n : (j + 1) * cols_n].T.astype(BF16)

    loop(rows_n // TOGETHER, last, LAST_UNROLL)


def finish(spot, total, total_col, coef, *rest, channels):
    rows_n, cols_n, width = total.shape
    return call(
        finish_body,
        jax.ShapeDtypeStruct((rows_n, channels, cols_n), BF16),
        [pl.BlockSpec(memory_space=pltpu.SMEM)] + [whole()] * 15,
        [pltpu.VMEM(coef.shape, F32), pltpu.VMEM(total.shape, F32)],
        name="finish",
    )(spot, total, total_col, coef, *rest)


def shifted(block, axis, up):
    count = lax.axis_size(axis)
    pairs = [(i, i + 1) if up else (i + 1, i) for i in range(count - 1)]
    return lax.ppermute(block, axis, pairs)


def local(
    tile_feats, tile_cell, tile_mask, tile_count, background, norm_gain, in_x, in_z, conv_w, conv_bias, x_proj,
    skip_gain, decay_rate, out_gain, out_w, mlp_gain, ff_in, ff_out,
):
    heads, rows_n, cols_n = decay_rate.shape[1:]
    owners, slots, channels = tile_feats.shape[1:]
    width = in_x.shape[1]
    state_size = x_proj.shape[1] // 8
    cells_n = rows_n * cols_n

    feats = jnp.transpose(tile_feats[0], (1, 2, 0))
    values = jnp.where(tile_mask[0].T[:, None, :] == 1, feats, background[None, :, None])
    live = jnp.arange(slots, dtype=jnp.int32)[:, None] < tile_count
    marked = jnp.where(live, tile_cell[0].T, cells_n)
    where = jnp.stack([marked // 64, marked % 64], axis=1).astype(BF16)
    filler = jnp.zeros((slots, 2 * LANES - channels - 2, owners), BF16)
    sent = jnp.concatenate([values, where, filler], axis=1)
    sent = with_layout_constraint(sent, Layout(major_to_minor=(0, 1, 2)))
    sent = lax.optimization_barrier(sent)
    sent = jnp.transpose(sent, (2, 0, 1))
    got = lax.all_to_all(sent, ("row", "col"), split_axis=0, concat_axis=0, tiled=True)
    into_row, out_row, into_col, out_col, total_row, total_col = decay_factors(decay_rate)
    half_row = half_tiles(total_row, lax.axis_size("col"))
    half_col = half_tiles(total_col, cols_n // SUB)
    half_row = jnp.pad(half_row, ((0, 0), (0, 0), (0, width - half_row.shape[2])))
    half_col = jnp.pad(half_col, ((0, 0), (0, 0), (0, width - half_col.shape[2])))
    line = lax.axis_index("row")
    spot = jnp.stack([line % 2, line // 2]).astype(jnp.int32)
    head_of = jnp.arange(2 * width, dtype=jnp.int32) // (width // heads)
    part_of = jnp.arange(32, dtype=jnp.int32)
    head_at = part_of // 16 * heads + part_of % 16 % heads
    heads_map = ((head_at[:, None] == head_of[None, :]) & (part_of % 16 < 2 * heads)[:, None]).astype(BF16)
    lane = jnp.arange(LANES, dtype=jnp.int32)
    picks = [
        (lane[:, None] == (m * state_size + lane // SUB)[None, :]).astype(BF16) for m in range(4, 8)
    ]
    pick_b = jnp.stack([picks[0].T, picks[2].T])
    pick_c = jnp.concatenate([picks[1], picks[3]], axis=1)

    got = got.reshape(owners * slots, sent.shape[2])
    ready = (into_row, out_row, into_col, out_col, half_row, half_col, heads_map, pick_b, pick_c, spot)
    got, ready = lax.optimization_barrier((got, ready))
    into_row, out_row, into_col, out_col, half_row, half_col, heads_map, pick_b, pick_c, spot = ready
    cells = got[:, channels].astype(jnp.int32) * 64 + got[:, channels + 1].astype(jnp.int32)

    grid, inner, left_edge, right_edge = place(
        cells, got, norm_gain[None], in_x, rows_n, cols_n, channels
    )
    from_left = shifted(right_edge, "col", True).astype(BF16)
    from_right = shifted(left_edge, "col", False).astype(BF16)
    top = jnp.concatenate([inner[:cols_n], from_left[:1], from_right[:1]])
    bottom = jnp.concatenate([inner[cells_n - cols_n :], from_left[rows_n - 1 :], from_right[rows_n - 1 :]])
    above = shifted(bottom, "row", True)
    below = shifted(top, "row", False)
    left = jnp.concatenate([above[cols_n : cols_n + 1], from_left, below[cols_n : cols_n + 1]])[:, None].astype(F32)
    right = jnp.concatenate([above[cols_n + 1 :], from_right, below[cols_n + 1 :]])[:, None].astype(F32)

    x_in, coef, state_row, state_own, state_other = conv_and_states(
        spot, inner.reshape(rows_n, cols_n, width), above[:cols_n], below[:cols_n], left, right,
        conv_w.reshape(9, width), conv_bias[None], x_proj, into_row, into_col, heads_map, pick_b, half_row, half_col,
    )
    order = lax.optimization_barrier
    lines, peers = lax.axis_size("row"), lax.axis_size("col")
    chips = lines // 2
    twin = [(i, i ^ 1) for i in range(lines)]
    state_got = lax.ppermute(state_other, "row", twin)
    split_row = lax.all_to_all(state_row, "col", split_axis=0, concat_axis=0, tiled=True)
    sends = chip_total(spot, state_own, state_got, heads_map, chips)
    receipts = [
        lax.ppermute(send, "row", [(i, (i + 2 * shift) % lines) for i in range(lines)])
        for shift, send in enumerate(sends, 1)
    ]
    grid_in, sends = order((grid, sends))
    gated = gate(grid_in, norm_gain[None], in_z)
    split_row, gated = order((split_row, gated))
    passed = chain(split_row, heads_map, rows_n // peers)
    enter_row = lax.all_to_all(passed, "col", split_axis=0, concat_axis=0, tiled=True)
    enter_row = enter_row.reshape(rows_n, 2, state_size, width)
    x_col, passed = order((x_in, passed))
    total_col = inner_col(x_col, coef, into_col, out_col, heads_map)
    x_row, total_col = order((x_in, total_col))
    total = row_scan(x_row, coef, enter_row, into_row, out_row, heads_map, skip_gain[None])
    receipts, total = order((receipts, total))
    enter_own, enter_other = entering_states(spot, state_own, state_got, heads_map, receipts)
    enter_other = lax.ppermute(enter_other, "row", twin)
    block = finish(
        spot, total, total_col, coef, enter_own, enter_other, out_col, heads_map, pick_c, gated, grid,
        out_gain[None], out_w.T, mlp_gain[None], ff_in, ff_out.T, channels=channels,
    )
    return jnp.swapaxes(block, 1, 2)


def solution(mesh):
    spread_all = (
        P(("row", "col"), None, None, None),
        P(("row", "col"), None, None),
        P(("row", "col"), None, None),
        P(("row", "col"), None),
    )
    placed = spread_all + (P(),) * 8 + (P(None, None, "row", "col"),) + (P(),) * 5
    return jax.shard_map(
        local, mesh=mesh, in_specs=placed, out_specs=P("row", "col", None), check_vma=False
    )
```

```python
import functools
import jax
import jax.numpy as jnp
from jax import lax
from jax.experimental import pallas as pl
from jax.experimental.layout import Layout, with_layout_constraint
from jax.experimental.pallas import tpu as pltpu
from jax.sharding import PartitionSpec as P

F32 = jnp.float32
BF16 = jnp.bfloat16
BLOCK = 1024
UNROLL = 8
TOGETHER = 4
LAST_UNROLL = 1
LANES = 128
SUB = 8
KERNEL_MIB = dict(
    place_norm_project=20, gate=10, conv_states=57, row_scan=57, inner_col=57, chain=8, chip_total=10, entering=13, finish=34
)


def whole():
    return pl.BlockSpec(memory_space=pltpu.VMEM)


KERNEL_US = dict(
    place_norm_project=12, gate=6, conv_states=31, row_scan=20, inner_col=16, chain=3, chip_total=5, entering=6, finish=25
)


def hbm():
    return pl.BlockSpec(memory_space=pltpu.HBM)


def block(shape, dim, size):
    where = tuple(size if at == dim else length for at, length in enumerate(shape))
    return pl.BlockSpec(where, lambda i: tuple(i if at == dim else 0 for at in range(len(shape))))


def same(shape):
    return pl.BlockSpec(shape, lambda i: (0,) * len(shape))


def call(body, outs, ins, scratch=(), name=None, out_specs=None, grid=()):
    work = KERNEL_US[name] * 10**7
    return pl.pallas_call(
        body,
        cost_estimate=pl.CostEstimate(flops=work, bytes_accessed=work // 400, transcendentals=0),
        out_shape=outs,
        grid=grid,
        in_specs=ins,
        out_specs=out_specs or jax.tree.map(lambda _: whole(), outs),
        scratch_shapes=list(scratch),
        compiler_params=pltpu.CompilerParams(vmem_limit_bytes=KERNEL_MIB[name] * 1024 * 1024),
        name=name,
    )


def loop(count, step, unroll=1):
    def body(i, carry):
        for j in range(unroll):
            step(i * unroll + j)
        return carry

    lax.fori_loop(0, count // unroll, body, 0)


def dot(a, b):
    return jnp.dot(a, b, preferred_element_type=F32)


def dot_nt(a, b):
    return lax.dot_general(a, b, (((1,), (1,)), ((), ())), preferred_element_type=F32)


def dot_tn(a, b):
    return lax.dot_general(a, b, (((0,), (0,)), ((), ())), preferred_element_type=F32)


def silu(values):
    half = 0.5 * values
    return half + half * jnp.tanh(half)


def rms_scale(values, gains):
    return values * lax.rsqrt(jnp.mean(values * values, axis=-1, keepdims=True) + 1e-06) * gains


def two_parts(values):
    high = lax.reduce_precision(values, 8, 7)
    return high.astype(BF16), (values - high).astype(BF16)


def factor_rows(values):
    high, low = two_parts(values)
    heads = values.shape[1]
    both = jnp.concatenate([high, low], axis=1)
    return jnp.pad(both, ((0, 0), (0, 16 - 2 * heads), (0, 0), (0, 0)))


def row_layout(parts):
    k, m, r, c = parts.shape
    return jnp.transpose(parts, (2, 0, 1, 3)).reshape(r, k * m, c)


def col_layout(parts):
    k, m, r, c = parts.shape
    parts = parts.reshape(k, m, r, c // SUB, SUB)
    parts = jnp.transpose(parts, (3, 0, 1, 2, 4)).reshape(c // SUB, k * m, r * SUB)
    return with_layout_constraint(parts, Layout(major_to_minor=(0, 1, 2)))


def decay_factors(decay):
    rows_n, cols_n = decay.shape[2:]
    upto_c = jnp.triu(jnp.ones((cols_n, cols_n), F32))
    upto_r = jnp.triu(jnp.ones((rows_n, rows_n), F32))
    exact = lax.Precision.HIGHEST
    cum = jnp.stack(
        [
            jnp.einsum("hru,ut->hrt", decay[0], upto_c, precision=exact),
            jnp.einsum("hru,ut->hrt", decay[1], upto_c.T, precision=exact),
            jnp.einsum("huc,ut->htc", decay[2], upto_r, precision=exact),
            jnp.einsum("huc,ut->htc", decay[3], upto_r.T, precision=exact),
        ]
    )
    total_row = jnp.sum(decay[:2], axis=3)
    total_col = jnp.sum(decay[2:], axis=2)
    mid = 0.5 * jnp.concatenate(
        [
            jnp.broadcast_to(total_row[..., None], decay[:2].shape),
            jnp.broadcast_to(total_col[:, :, None, :], decay[2:].shape),
        ]
    )
    weight = jnp.sqrt(-jnp.expm1(-2.0 * decay))
    into = factor_rows(weight * jnp.exp(cum - mid))
    out = factor_rows(jnp.exp(mid - cum))
    return (
        row_layout(into[:2]),
        row_layout(out[:2]),
        col_layout(into[2:]),
        col_layout(out[2:]),
        total_row,
        total_col,
    )


def place_body(cells, got, gain, in_x, grid_out, inner_out, left_out, right_out, *scratch):
    src, dst = scratch[:2], scratch[2:]
    slots = got.shape[0]
    channels = grid_out.shape[1]
    cells_n = grid_out.shape[0]
    cols_n = cells_n // left_out.shape[0]

    def fill(i, carry):
        at = pl.ds(pl.multiple_of(i * 256, 256), 256)
        for part in dst:
            part[at, :] = jnp.zeros((256, LANES), F32)
        return carry

    lax.fori_loop(0, cells_n // 256, fill, 0)

    def widen(i, carry):
        at = pl.ds(pl.multiple_of(i * 256, 256), 256)
        for m, part in enumerate(src):
            part[at, :] = got[at, m * LANES : (m + 1) * LANES].astype(F32)
        return carry

    lax.fori_loop(0, slots // 256, widen, 0)

    def place(i, carry):
        base = i * 16
        for j in range(16):
            cell = cells[base + j]
            for from_part, to_part in zip(src, dst):
                to_part[pl.ds(cell, 1), :] = from_part[pl.ds(base + j, 1), :]
        return carry

    lax.fori_loop(0, slots // 16, place, 0)

    def project(r, carry):
        at = pl.ds(pl.multiple_of(r * cols_n, cols_n), cols_n)
        tiles = jnp.concatenate([dst[0][at, :], dst[1][at, : channels - LANES]], axis=1)
        grid_out[at, :] = tiles.astype(BF16)
        normed = rms_scale(tiles, gain[...]).astype(BF16)
        inner = dot(normed, in_x[...]).astype(BF16)
        inner_out[at, :] = inner
        wide = inner.astype(F32)
        left_out[pl.ds(r, 1), :] = wide[:1]
        right_out[pl.ds(r, 1), :] = wide[cols_n - 1 :]
        return carry

    loop(cells_n // cols_n, lambda r: project(r, 0), UNROLL)


def place(cells, got, gain, in_x, rows_n, cols_n, channels):
    cells_n = rows_n * cols_n
    width = in_x.shape[1]
    outs = (
        jax.ShapeDtypeStruct((cells_n, channels), BF16),
        jax.ShapeDtypeStruct((cells_n, width), BF16),
        jax.ShapeDtypeStruct((rows_n, width), F32),
        jax.ShapeDtypeStruct((rows_n, width), F32),
    )
    return call(
        place_body,
        outs,
        [pl.BlockSpec(memory_space=pltpu.SMEM), whole(), whole(), whole()],
        [
            pltpu.VMEM((got.shape[0], LANES), F32),
            pltpu.VMEM((got.shape[0], LANES), F32),
            pltpu.VMEM((cells_n + SUB, LANES), F32),
            pltpu.VMEM((cells_n + SUB, LANES), F32),
        ],
        name="place_norm_project",
    )(cells, got, gain, in_x)


def gate_body(grid, gain, in_z, gate_out, *, block):
    def step(i, carry):
        at = pl.ds(pl.multiple_of(i * block, block), block)
        normed = rms_scale(grid[at, :].astype(F32), gain[...]).astype(BF16)
        gate = dot(normed, in_z[...]).astype(BF16).astype(F32)
        gate_out[at, :] = silu(gate).astype(BF16)
        return carry

    lax.fori_loop(0, grid.shape[0] // block, step, 0)


def gate(grid, gain, in_z):
    return call(
        functools.partial(gate_body, block=BLOCK),
        jax.ShapeDtypeStruct((grid.shape[0], in_z.shape[1]), BF16),
        [whole()] * 3,
        name="gate",
    )(grid, gain, in_z)


def spread(parts, heads_map):
    both = dot_tn(parts, heads_map)
    width = both.shape[1] // 2
    return both[:, :width], both[:, width:]


def own_column(shape, row_mod, col_mod):
    rows = lax.broadcasted_iota(jnp.int32, shape, 0)
    cols = lax.broadcasted_iota(jnp.int32, shape, 1)
    return (rows & (row_mod - 1)) == (cols & (col_mod - 1))


def conv_body(
    spot, inner, above, below, left, right, conv_w, conv_bias, x_proj, into_row, into_col, heads_map, pick_b,
    half_row, half_col, x_hbm, coef_hbm, state_row, own_hbm, other_hbm,
    padded, x_wide, coef_wide, left_sum, right_sum, x_out, coef_out, state_own, state_other, done,
):
    rows_n, cols_n, width = inner.shape
    state_size = LANES // 8
    peers, tile_rows = half_row.shape[:2]
    each = rows_n // peers
    for q in range(peers):
        state_row[q, 2 * each * state_size :] = half_row[q]
    padded[0] = above[...]
    padded[rows_n + 1] = below[...]

    def move(r, carry):
        padded[r + 1] = inner[r]
        return carry

    lax.fori_loop(0, rows_n, move, 0)
    for edge, column, sums in ((left, 0, left_sum), (right, 2, right_sum)):
        total = jnp.zeros((rows_n, 1, width), F32)
        for i in range(3):
            total = total + edge[i : i + rows_n] * conv_w[3 * i + column : 3 * i + column + 1, :][None]
        sums[...] = total
    first = lax.broadcasted_iota(jnp.int32, (cols_n, LANES), 0) == 0
    last = lax.broadcasted_iota(jnp.int32, (cols_n, LANES), 0) == cols_n - 1

    def row_step(r, carry):
        for part in range(width // LANES):
            lanes = slice(part * LANES, (part + 1) * LANES)
            rows = [padded[r + i, :, lanes].astype(F32) for i in range(3)]
            sums = []
            for j in range(3):
                total = rows[0] * conv_w[j : j + 1, lanes]
                total = total + rows[1] * conv_w[3 + j : 4 + j, lanes]
                sums.append(total + rows[2] * conv_w[6 + j : 7 + j, lanes])
            from_left = jnp.where(first, left_sum[r, :, lanes], pltpu.roll(sums[0], 1, 0))
            from_right = jnp.where(
                last, right_sum[r, :, lanes], pltpu.roll(sums[2], cols_n - 1, 0)
            )
            value = conv_bias[:, lanes] + from_left + sums[1] + from_right
            scanned = silu(value).astype(BF16)
            x_out[r, :, lanes] = scanned
            x_wide[r, :, lanes] = scanned.astype(F32)
        coef = dot(x_out[r], x_proj[...]).astype(BF16)
        coef_out[r] = coef
        coef_wide[r] = coef.astype(F32)
        flipped = coef.T
        into = spread(into_row[r], heads_map[...])
        for k in range(2):
            scaled = (x_wide[r] * into[k]).astype(BF16)
            b_part = flipped[2 * k * state_size : (2 * k + 1) * state_size, :]
            at = pl.multiple_of((r % each) * 2 * state_size + k * state_size, state_size)
            state_row[r // each, pl.ds(at, state_size), :] = dot(b_part, scaled).astype(BF16)
        return carry

    loop(rows_n, lambda r: row_step(r, 0), UNROLL)
    size = rows_n * SUB
    own = own_column((LANES, size), SUB, SUB)

    copies = [
        pltpu.make_async_copy(held, out, done.at[m])
        for m, (held, out) in enumerate(
            ((x_out, x_hbm), (coef_out, coef_hbm), (state_other, other_hbm), (state_own, own_hbm))
        )
    ]
    copies[0].start()
    copies[1].start()
    half = state_own.shape[0]
    deep = SUB * state_size

    def column_states(states, side):
        def col_step(j):
            g = side * half + j
            at = pl.ds(pl.multiple_of(g * SUB, SUB), SUB)
            x_group = x_wide[:, at, :].reshape(size, width)
            coef = coef_wide[:, at, :].reshape(size, LANES).astype(BF16)
            into = spread(into_col[g], heads_map[...])
            for k in range(2):
                scaled = (x_group * into[k]).astype(BF16)
                b_part = jnp.where(own, dot_nt(pick_b[k], coef), 0.0).astype(BF16)
                states[j, k * deep : (k + 1) * deep, :] = dot(b_part, scaled).astype(BF16)
            states[j, 2 * deep :, :] = half_col[g]

        loop(half, col_step, UNROLL)

    column_states(state_other, 1 - spot[0])
    copies[2].start()
    column_states(state_own, spot[0])
    copies[3].start()
    for copy in copies:
        copy.wait()


def conv_and_states(spot, inner, *rest):
    rows_n, cols_n, width = inner.shape
    half_row, half_col = rest[-2:]
    peers, tile_rows = half_row.shape[:2]
    groups, deep = half_col.shape[0] // 2, 2 * SUB * (LANES // 8) + half_col.shape[1]
    outs = (
        jax.ShapeDtypeStruct((rows_n, cols_n, width), BF16),
        jax.ShapeDtypeStruct((rows_n, cols_n, LANES), BF16),
        jax.ShapeDtypeStruct((peers, rows_n // peers * 2 * (LANES // 8) + tile_rows, width), BF16),
        jax.ShapeDtypeStruct((groups, deep, width), BF16),
        jax.ShapeDtypeStruct((groups, deep, width), BF16),
    )
    return call(
        conv_body,
        outs,
        [pl.BlockSpec(memory_space=pltpu.SMEM)] + [whole()] * 14,
        [
            pltpu.VMEM((rows_n + 2, cols_n, width), BF16),
            pltpu.VMEM((rows_n, cols_n, width), F32),
            pltpu.VMEM((rows_n, cols_n, LANES), F32),
            pltpu.VMEM((rows_n, 1, width), F32),
            pltpu.VMEM((rows_n, 1, width), F32),
            pltpu.VMEM((rows_n, cols_n, width), BF16),
            pltpu.VMEM((rows_n, cols_n, LANES), BF16),
            pltpu.VMEM((groups, deep, width), BF16),
            pltpu.VMEM((groups, deep, width), BF16),
            pltpu.SemaphoreType.DMA((4,)),
        ],
        name="conv_states",
        out_specs=(hbm(), hbm(), whole(), hbm(), hbm()),
    )(spot, inner, *rest)


def c_at_b(wide, k):
    state_size = LANES // 8
    lane = lax.broadcasted_iota(jnp.int32, (1, LANES), 1)
    rolled = pltpu.roll(wide, LANES - state_size, 1)
    return jnp.where((lane // state_size) == 2 * k, rolled, 0.0).astype(BF16)


def row_scan_body(x_in, coef_in, enter_row, into_row, out_row, heads_map, skip, total_out):
    rows_n, cols_n, width = x_in.shape
    t_row = lax.broadcasted_iota(jnp.int32, (cols_n, cols_n), 0)
    u_row = lax.broadcasted_iota(jnp.int32, (cols_n, cols_n), 1)
    masks = (t_row >= u_row, t_row <= u_row)

    state_size = LANES // 8

    def row_step(r):
        x_row = x_in[r].astype(F32)
        coef = coef_in[r]
        wide = coef.astype(F32)
        total = x_row * skip[...]
        into = spread(into_row[r], heads_map[...])
        out = spread(out_row[r], heads_map[...])
        for k in range(2):
            scores = dot_nt(c_at_b(wide, k), coef)
            mixing = jnp.where(masks[k], scores, 0.0).astype(BF16)
            c_part = coef[:, (2 * k + 1) * state_size : (2 * k + 2) * state_size]
            scaled = (x_row * into[k]).astype(BF16)
            both = dot(
                jnp.concatenate([mixing, c_part], axis=1),
                jnp.concatenate([scaled, enter_row[r, k]], axis=0),
            )
            total = total + both * out[k]
        total_out[r] = total.astype(BF16)

    loop(rows_n, row_step, UNROLL)


def row_scan(x_in, coef, enter_row, into_row, out_row, heads_map, skip):
    by_row = [block(array.shape, 0, UNROLL) for array in (x_in, coef, enter_row, into_row, out_row)]
    return call(
        row_scan_body,
        jax.ShapeDtypeStruct(x_in.shape, BF16),
        by_row + [same(heads_map.shape), same(skip.shape)],
        name="row_scan",
        out_specs=by_row[0],
        grid=(x_in.shape[0] // UNROLL,),
    )(x_in, coef, enter_row, into_row, out_row, heads_map, skip)


def inner_col_body(x_in, coef_in, into_col, out_col, heads_map, total_out, x_wide, coef_wide, acc):
    rows_n, cols_n, width = x_in.shape

    def widen(r):
        x_wide[r] = x_in[r].astype(F32)
        coef_wide[r] = coef_in[r].astype(F32)

    loop(rows_n, widen, UNROLL)
    size = rows_n * SUB
    t_col = lax.broadcasted_iota(jnp.int32, (size, size), 0)
    u_col = lax.broadcasted_iota(jnp.int32, (size, size), 1)
    same = (t_col & (SUB - 1)) == (u_col & (SUB - 1))
    masks = (same & (t_col >= u_col), same & (t_col <= u_col))

    def col_step(g):
        at = pl.ds(pl.multiple_of(g * SUB, SUB), SUB)
        x_group = x_wide[:, at, :].reshape(size, width)
        wide = coef_wide[:, at, :].reshape(size, LANES)
        coef = wide.astype(BF16)
        total = jnp.zeros((size, width), F32)
        into = spread(into_col[g], heads_map[...])
        out = spread(out_col[g], heads_map[...])
        for k in range(2):
            scores = dot_nt(c_at_b(wide, k + 2), coef)
            mixing = jnp.where(masks[k], scores, 0.0).astype(BF16)
            scaled = (x_group * into[k]).astype(BF16)
            total = total + dot(mixing, scaled) * out[k]
        acc[:, at, :] = total.reshape(rows_n, SUB, width)

    loop(cols_n // SUB, col_step, cols_n // SUB)

    def emit(r):
        total_out[r] = acc[r].astype(BF16)

    loop(rows_n, emit, UNROLL)


def inner_col(x_in, coef, into_col, out_col, heads_map):
    rows_n, cols_n, width = x_in.shape
    groups = 4
    wide = groups * SUB
    cols = block(x_in.shape, 1, wide)
    return call(
        inner_col_body,
        jax.ShapeDtypeStruct(x_in.shape, BF16),
        [
            cols,
            block(coef.shape, 1, wide),
            block(into_col.shape, 0, groups),
            block(out_col.shape, 0, groups),
            same(heads_map.shape),
        ],
        [
            pltpu.VMEM((rows_n, wide, width), F32),
            pltpu.VMEM((rows_n, wide, LANES), F32),
            pltpu.VMEM((rows_n, wide, width), F32),
        ],
        name="inner_col",
        out_specs=cols,
        grid=(cols_n // wide,),
    )(x_in, coef, into_col, out_col, heads_map)


def half_of(tile, k, heads_map):
    return dot(tile[:, 16 * k : 16 * k + 16], heads_map[:16, : heads_map.shape[1] // 2])


def chain_body(states, heads_map, entering):
    peers = states.shape[0]
    state_size = LANES // 8
    width = states.shape[2]
    lines = entering.shape[1] // (2 * state_size)
    top = 2 * lines * state_size
    for k in range(2):
        order = range(peers) if k == 0 else range(peers - 1, -1, -1)
        before = [jnp.zeros((state_size, width), F32)] * lines
        for at in order:
            scale = half_of(states[at, top:, :LANES], k, heads_map[...])
            for line in range(lines):
                rows = slice((2 * line + k) * state_size, (2 * line + k + 1) * state_size)
                own = scale[line : line + 1]
                entering[at, rows, :] = (own * before[line]).astype(BF16)
                before[line] = own * (own * before[line] + states[at, rows, :].astype(F32))


def chain(states, heads_map, lines):
    peers, _, width = states.shape
    return call(
        chain_body,
        jax.ShapeDtypeStruct((peers, lines * 2 * (LANES // 8), width), BF16),
        [whole()] * 2,
        name="chain",
    )(states, heads_map)


def pair_halves(upper, lower, j, top, heads_map):
    low_rows = pltpu.roll(lower[j, top:, :LANES].astype(F32), SUB, 0)
    first = lax.broadcasted_iota(jnp.int32, low_rows.shape, 0) < SUB
    tile = jnp.where(first, upper[j, top:, :LANES].astype(F32), low_rows).astype(BF16)
    halves = []
    for k in range(2):
        both = half_of(tile, k, heads_map)
        halves.append((both[:SUB], both[SUB:]))
    return tile, halves


def lines_of(states, j, k, lines_shape):
    deep = lines_shape[0] * lines_shape[1]
    return states[j, k * deep : (k + 1) * deep, :].astype(F32).reshape(lines_shape)


def by_core(spot, run, own, got):
    @pl.when(spot[0] == 0)
    def _():
        run(own, got)

    @pl.when(spot[0] != 0)
    def _():
        run(got, own)


def chip_total_body(spot, own, got, heads_map, *sends):
    groups, rows, width = own.shape
    state_size = LANES // 8
    deep = SUB * state_size
    shape = (state_size, SUB, width)
    chips = len(sends) + 1

    def run(upper, lower):
        def step(j):
            tile, halves = pair_halves(upper, lower, j, 2 * deep, heads_map[...])
            (up_2, low_2), (up_3, low_3) = halves
            down = (low_2 * low_2 * up_2) * lines_of(upper, j, 0, shape) + low_2 * lines_of(lower, j, 0, shape)
            rise = (up_3 * up_3 * low_3) * lines_of(lower, j, 1, shape) + up_3 * lines_of(upper, j, 1, shape)
            for shift, send in enumerate(sends, 1):
                past_end = spot[1] + shift >= chips
                send[j, :deep, :] = jnp.where(past_end, rise, down).reshape(deep, width).astype(BF16)
                send[j, deep:, :] = jnp.zeros((rows - 2 * deep, width), BF16)
                send[j, deep:, :LANES] = tile

        loop(groups, step, 4)

    by_core(spot, run, own, got)


def chip_total(spot, own, got, heads_map, chips):
    groups, rows, width = own.shape
    send = jax.ShapeDtypeStruct((groups, rows - SUB * (LANES // 8), width), BF16)
    return call(
        chip_total_body,
        (send,) * (chips - 1),
        [pl.BlockSpec(memory_space=pltpu.SMEM)] + [whole()] * 3,
        name="chip_total",
    )(spot, own, got, heads_map)


def entering_body(spot, own, got, heads_map, *rest):
    receipts, (enter_own, enter_other) = rest[:-2], rest[-2:]
    groups, rows, width = own.shape
    state_size = LANES // 8
    deep = SUB * state_size
    shape = (state_size, SUB, width)
    chips = len(receipts) + 1

    def run(upper, lower, enter_upper, enter_lower):
        def step(j):
            _, halves = pair_halves(upper, lower, j, 2 * deep, heads_map[...])
            (up_2, low_2), (up_3, low_3) = halves
            states = [lines_of(receipt, j, 0, shape) for receipt in receipts]
            keeps = []
            for k in range(2):
                keep = []
                for receipt in receipts:
                    both = half_of(receipt[j, deep:, :LANES], k, heads_map[...])
                    chip = both[:SUB] * both[SUB:]
                    keep.append(chip * chip)
                keeps.append(keep)
            down = jnp.zeros(shape, F32)
            rise = jnp.zeros(shape, F32)
            keep_2 = jnp.ones((SUB, width), F32)
            keep_3 = jnp.ones((SUB, width), F32)
            for away in range(1, chips):
                above, below = away - 1, chips - away - 1
                down = down + jnp.where(spot[1] >= away, keep_2, 0.0) * states[above]
                rise = rise + jnp.where(spot[1] + away < chips, keep_3, 0.0) * states[below]
                keep_2 = keep_2 * keeps[0][above]
                keep_3 = keep_3 * keeps[1][below]
            lower_2 = low_2 * up_2 * (up_2 * down + lines_of(upper, j, 0, shape))
            upper_3 = up_3 * low_3 * (low_3 * rise + lines_of(lower, j, 1, shape))
            enter_upper[j, 0] = (up_2 * down).reshape(deep, width).astype(BF16)
            enter_upper[j, 1] = upper_3.reshape(deep, width).astype(BF16)
            enter_lower[j, 0] = lower_2.reshape(deep, width).astype(BF16)
            enter_lower[j, 1] = (low_3 * rise).reshape(deep, width).astype(BF16)

        loop(groups, step, 4)

    @pl.when(spot[0] == 0)
    def _():
        run(own, got, enter_own, enter_other)

    @pl.when(spot[0] != 0)
    def _():
        run(got, own, enter_other, enter_own)


def entering_states(spot, own, got, heads_map, receipts):
    groups, rows, width = own.shape
    enter = jax.ShapeDtypeStruct((groups, 2, SUB * (LANES // 8), width), BF16)
    return call(
        entering_body,
        (enter, enter),
        [pl.BlockSpec(memory_space=pltpu.SMEM)] + [whole()] * (3 + len(receipts)),
        name="entering",
    )(spot, own, got, heads_map, *receipts)


def half_tiles(total, units):
    k, heads, lines = total.shape
    high, low = two_parts(jnp.exp(-0.5 * total))
    both = jnp.pad(jnp.concatenate([high, low], axis=1), ((0, 0), (0, 16 - 2 * heads), (0, 0)))
    both = jnp.transpose(both, (2, 0, 1)).reshape(units, lines // units, k * 16)
    rows = -(-both.shape[1] // 16) * 16
    return jnp.pad(both, ((0, 0), (0, rows - both.shape[1]), (0, 0)))


def finish_body(
    spot, total_row, total_col, coef_in, enter_own, enter_other, out_col, heads_map, pick_c, gate_in, grid,
    out_gain, out_w, mlp_gain, ff_in, ff_out, block_out, coef_wide, acc,
):
    rows_n, cols_n, width = total_row.shape
    half = enter_own.shape[0]

    def widen(r):
        coef_wide[r] = coef_in[r].astype(F32)
        acc[r] = total_row[r].astype(F32) + total_col[r].astype(F32)

    loop(rows_n, widen, UNROLL)
    size = rows_n * SUB
    own = own_column((size, LANES), SUB, SUB)

    def col_step(j):
        for enter, side in ((enter_own, spot[0]), (enter_other, 1 - spot[0])):
            g = side * half + j
            at = pl.ds(pl.multiple_of(g * SUB, SUB), SUB)
            coef = coef_wide[:, at, :].reshape(size, LANES).astype(BF16)
            value = acc[:, at, :].reshape(size, width)
            out = spread(out_col[g], heads_map[...])
            c_both = dot(coef, pick_c[...])
            for k in range(2):
                c_part = jnp.where(own, c_both[:, k * LANES : (k + 1) * LANES], 0.0).astype(BF16)
                value = value + dot(c_part, enter[j, k]) * out[k]
            acc[:, at, :] = value.reshape(rows_n, SUB, width)

    loop(half, col_step, UNROLL // 2)
    deep = TOGETHER * cols_n

    def last(i):
        at = pl.ds(pl.multiple_of(i * deep, deep), deep)
        value = acc[pl.ds(i * TOGETHER, TOGETHER)].reshape(deep, width)
        gated = (rms_scale(value, out_gain[...]) * gate_in[at, :].astype(F32)).astype(BF16)
        middle = (dot_nt(gated, out_w[...]) + grid[at, :].astype(F32)).astype(BF16)
        wide = middle.astype(F32)
        normed = rms_scale(wide, mlp_gain[...]).astype(BF16)
        hidden = dot(normed, ff_in[...])
        hidden = (hidden * (0.5 + 0.5 * lax.erf(hidden * (0.5**0.5)))).astype(BF16)
        result = dot_nt(hidden, ff_out[...]) + wide
        for j in range(TOGETHER):
            block_out[i * TOGETHER + j] = result[j * cols_n : (j + 1) * cols_n].T.astype(BF16)

    loop(rows_n // TOGETHER, last, LAST_UNROLL)


def finish(spot, total, total_col, coef, *rest, channels):
    rows_n, cols_n, width = total.shape
    return call(
        finish_body,
        jax.ShapeDtypeStruct((rows_n, channels, cols_n), BF16),
        [pl.BlockSpec(memory_space=pltpu.SMEM)] + [whole()] * 15,
        [pltpu.VMEM(coef.shape, F32), pltpu.VMEM(total.shape, F32)],
        name="finish",
    )(spot, total, total_col, coef, *rest)


def shifted(block, axis, up):
    count = lax.axis_size(axis)
    pairs = [(i, i + 1) if up else (i + 1, i) for i in range(count - 1)]
    return lax.ppermute(block, axis, pairs)


def local(
    tile_feats, tile_cell, tile_mask, tile_count, background, norm_gain, in_x, in_z, conv_w, conv_bias, x_proj,
    skip_gain, decay_rate, out_gain, out_w, mlp_gain, ff_in, ff_out,
):
    heads, rows_n, cols_n = decay_rate.shape[1:]
    owners, slots, channels = tile_feats.shape[1:]
    width = in_x.shape[1]
    state_size = x_proj.shape[1] // 8
    cells_n = rows_n * cols_n

    feats = jnp.transpose(tile_feats[0], (1, 2, 0))
    values = jnp.where(tile_mask[0].T[:, None, :] == 1, feats, background[None, :, None])
    live = jnp.arange(slots, dtype=jnp.int32)[:, None] < tile_count
    marked = jnp.where(live, tile_cell[0].T, cells_n)
    where = jnp.stack([marked // 64, marked % 64], axis=1).astype(BF16)
    filler = jnp.zeros((slots, 2 * LANES - channels - 2, owners), BF16)
    sent = jnp.concatenate([values, where, filler], axis=1)
    sent = with_layout_constraint(sent, Layout(major_to_minor=(0, 1, 2)))
    sent = lax.optimization_barrier(sent)
    sent = jnp.transpose(sent, (2, 0, 1))
    got = lax.all_to_all(sent, ("row", "col"), split_axis=0, concat_axis=0, tiled=True)
    into_row, out_row, into_col, out_col, total_row, total_col = decay_factors(decay_rate)
    half_row = half_tiles(total_row, lax.axis_size("col"))
    half_col = half_tiles(total_col, cols_n // SUB)
    half_row = jnp.pad(half_row, ((0, 0), (0, 0), (0, width - half_row.shape[2])))
    half_col = jnp.pad(half_col, ((0, 0), (0, 0), (0, width - half_col.shape[2])))
    line = lax.axis_index("row")
    spot = jnp.stack([line % 2, line // 2]).astype(jnp.int32)
    head_of = jnp.arange(2 * width, dtype=jnp.int32) // (width // heads)
    part_of = jnp.arange(32, dtype=jnp.int32)
    head_at = part_of // 16 * heads + part_of % 16 % heads
    heads_map = ((head_at[:, None] == head_of[None, :]) & (part_of % 16 < 2 * heads)[:, None]).astype(BF16)
    lane = jnp.arange(LANES, dtype=jnp.int32)
    picks = [
        (lane[:, None] == (m * state_size + lane // SUB)[None, :]).astype(BF16) for m in range(4, 8)
    ]
    pick_b = jnp.stack([picks[0].T, picks[2].T])
    pick_c = jnp.concatenate([picks[1], picks[3]], axis=1)

    got = got.reshape(owners * slots, sent.shape[2])
    ready = (into_row, out_row, into_col, out_col, half_row, half_col, heads_map, pick_b, pick_c, spot)
    got, ready = lax.optimization_barrier((got, ready))
    into_row, out_row, into_col, out_col, half_row, half_col, heads_map, pick_b, pick_c, spot = ready
    cells = got[:, channels].astype(jnp.int32) * 64 + got[:, channels + 1].astype(jnp.int32)

    grid, inner, left_edge, right_edge = place(
        cells, got, norm_gain[None], in_x, rows_n, cols_n, channels
    )
    from_left = shifted(right_edge, "col", True).astype(BF16)
    from_right = shifted(left_edge, "col", False).astype(BF16)
    top = jnp.concatenate([inner[:cols_n], from_left[:1], from_right[:1]])
    bottom = jnp.concatenate([inner[cells_n - cols_n :], from_left[rows_n - 1 :], from_right[rows_n - 1 :]])
    above = shifted(bottom, "row", True)
    below = shifted(top, "row", False)
    left = jnp.concatenate([above[cols_n : cols_n + 1], from_left, below[cols_n : cols_n + 1]])[:, None].astype(F32)
    right = jnp.concatenate([above[cols_n + 1 :], from_right, below[cols_n + 1 :]])[:, None].astype(F32)

    x_in, coef, state_row, state_own, state_other = conv_and_states(
        spot, inner.reshape(rows_n, cols_n, width), above[:cols_n], below[:cols_n], left, right,
        conv_w.reshape(9, width), conv_bias[None], x_proj, into_row, into_col, heads_map, pick_b, half_row, half_col,
    )
    order = lax.optimization_barrier
    lines, peers = lax.axis_size("row"), lax.axis_size("col")
    chips = lines // 2
    twin = [(i, i ^ 1) for i in range(lines)]
    state_got = lax.ppermute(state_other, "row", twin)
    split_row = lax.all_to_all(state_row, "col", split_axis=0, concat_axis=0, tiled=True)
    sends = chip_total(spot, state_own, state_got, heads_map, chips)
    receipts = [
        lax.ppermute(send, "row", [(i, (i + 2 * shift) % lines) for i in range(lines)])
        for shift, send in enumerate(sends, 1)
    ]
    grid_in, sends = order((grid, sends))
    gated = gate(grid_in, norm_gain[None], in_z)
    split_row, gated = order((split_row, gated))
    passed = chain(split_row, heads_map, rows_n // peers)
    enter_row = lax.all_to_all(passed, "col", split_axis=0, concat_axis=0, tiled=True)
    enter_row = enter_row.reshape(rows_n, 2, state_size, width)
    x_col, passed = order((x_in, passed))
    total_col = inner_col(x_col, coef, into_col, out_col, heads_map)
    x_row, total_col = order((x_in, total_col))
    total = row_scan(x_row, coef, enter_row, into_row, out_row, heads_map, skip_gain[None])
    receipts, total = order((receipts, total))
    enter_own, enter_other = entering_states(spot, state_own, state_got, heads_map, receipts)
    enter_other = lax.ppermute(enter_other, "row", twin)
    block = finish(
        spot, total, total_col, coef, enter_own, enter_other, out_col, heads_map, pick_c, gated, grid,
        out_gain[None], out_w.T, mlp_gain[None], ff_in, ff_out.T, channels=channels,
    )
    return jnp.swapaxes(block, 1, 2)


def solution(mesh):
    spread_all = (
        P(("row", "col"), None, None, None),
        P(("row", "col"), None, None),
        P(("row", "col"), None, None),
        P(("row", "col"), None),
    )
    placed = spread_all + (P(),) * 8 + (P(None, None, "row", "col"),) + (P(),) * 5
    return jax.shard_map(
        local, mesh=mesh, in_specs=placed, out_specs=P("row", "col", None), check_vma=False
    )
```
